128 devices in a mesh: ctx: 16 (over z, y_lo, core), fsdp: 8 (over x, y_hi).
Axes of the slice: x: 4, y: 4 (y_hi: 2, y_lo: 2; y = y_hi * 2 + y_lo), z: 4, core: 2. Of those that a mesh axis runs over, the one named last changes fastest.
Arguments:
- hidden: bfloat16 [8, 4096, 5376], P('fsdp', 'ctx'), may hold values from -6 to 6
- queries: bfloat16 [8, 4096, 2048], P('fsdp', 'ctx'), may hold values from -23 to 23
- key_heads: bfloat16 [8, 4096, 1024], P('fsdp', 'ctx'), may hold values from -6 to 6
- w_value: bfloat16 [5376, 1024], P('fsdp'), may hold values from -0.078125 to 0.078125
- d_out: bfloat16 [8, 4096, 2048], P('fsdp', 'ctx'), may hold values from -6 to 6
- segments: int32 [8, 4096], P('fsdp', 'ctx'), may hold values from 0 to 3, never falling along the last dimension, each value on 1 to 2048 neighbouring positions
Outputs:
- attn_out: bfloat16 [8, 4096, 2048], P('fsdp', 'ctx')
- d_queries: bfloat16 [8, 4096, 2048], P('fsdp', 'ctx')
- d_keys: bfloat16 [8, 4096, 1024], P('fsdp', 'ctx')
- d_hidden: bfloat16 [8, 4096, 5376], P('fsdp', 'ctx')
- d_w_value: float32 [5376, 1024], P(('ctx', 'fsdp'))
The draws below stay inside these ranges and needn't reach their ends.
Inputs may be any that keep to these rules, and one draw needn't show every extreme that they name: `segments`: document ids never fall along a sequence; a document holds at most half of the 4096 tokens.
All inputs are finite; a program needn't handle non-finite values.
Results may differ from the reference program's by a relative error of at most 0.024.
Values may be sent and summed in bfloat16 or wider, within the bound.
A program may use at most 256 MiB of HBM per device.

```python
import math
import jax
import jax.numpy as jnp
import numpy as np
from jax import lax

D = 5376
HQ = 16
HK = 8
HD = 128
WINDOW = 1024
TOK_DEV = 256
GROUP = 2
SPAN = 4096
BATCH = 8


def drawn_pair(key):
    query_key = jax.random.fold_in(key, 101)
    keys_key = jax.random.fold_in(key, 102)
    query_draw = jnp.clip(jax.random.normal(query_key, (BATCH, SPAN, HK, GROUP, HD), jnp.float32), -6.0, 6.0)
    key_draw = jnp.clip(jax.random.normal(keys_key, (BATCH, SPAN, HK, HD), jnp.float32), -6.0, 6.0)
    return (query_draw.reshape(BATCH, SPAN, HQ * HD), key_draw.reshape(BATCH, SPAN, HK * HD))


def draw_queries(key, part):
    return drawn_pair(key)[0].astype(jnp.bfloat16)


def draw_key_heads(key, part):
    return drawn_pair(key)[1].astype(jnp.bfloat16)


def spiked(entries, rng, source, target, blocks, factor):
    owner, partner = [(jnp.arange(entries.shape[axis_at]) // (entries.shape[axis_at] // blocks)).reshape([-1 if axis == axis_at else 1 for axis in range(entries.ndim)]) for axis_at in (source, target)]
    chosen = jax.random.permutation(rng, blocks)[partner]
    strong = (owner == chosen) | (owner == (partner + blocks // 2) % blocks)
    return jnp.where(strong, factor * entries, entries)


def block_scale(rng, extent, pieces, smallest, high):
    def one(axis_at, shards_of):
        heights = jax.random.uniform(jax.random.fold_in(jax.random.fold_in(rng, 6), axis_at), (shards_of,), jnp.float32, smallest / len(pieces), high / len(pieces))
        return jnp.repeat(jnp.exp(heights), extent[axis_at] // shards_of).reshape((-1,) + (1,) * (len(extent) - axis_at - 1))

    gain = one(*pieces[0])
    for cut in pieces[1:]:
        gain = gain * one(*cut)
    return gain


def length_profile(count, total, limit, skew):
    portions = [(1 << 20) // math.isqrt(standing ** skew) + 1 for standing in range(2, count + 1)]
    rest, counts = total - limit - (count - 1), [1] * (count - 1)
    while rest > 0:
        movable = [i for i in range(count - 1) if counts[i] < limit]
        mass, left = sum([portions[i] for i in movable]), rest
        for i in movable:
            addition = min(limit - counts[i], max(1, left * portions[i] // mass), rest)
            counts[i] = counts[i] + addition
            rest = rest - addition
    return np.array([limit] + counts)


def ragged_sizes(rng, count, total, reach, skew):
    if count == 2:
        one = jax.random.randint(rng, (), max(1, total - reach), min(reach, total - 1) + 1)
        return jnp.stack([one, total - one])
    sizes = jnp.asarray(length_profile(count, total, reach, skew), jnp.int32)
    couples = (count - 1) // 2
    source_of, taker = sizes[1:1 + 2 * couples:2], sizes[2:2 + 2 * couples:2]
    room = jnp.minimum(source_of - 1, reach - taker)
    moved = jax.random.randint(jax.random.fold_in(rng, 1), (couples,), 0, 1 << 20) % (room + 1)
    sizes = sizes.at[1:1 + 2 * couples:2].set(source_of - moved).at[2:2 + 2 * couples:2].set(taker + moved)
    return sizes[jax.random.permutation(jax.random.fold_in(rng, 2), count)]


def centred(rng, dims, width, most, split=(), kind=jnp.bfloat16):
    entries = width * jax.random.normal(rng, dims, jnp.float32)
    if split:
        entries = entries * block_scale(rng, dims, split, -0.22, 0.18)
    return jnp.clip(entries, -most, most).astype(kind)


def heavy_noise(own_key, dims, scale, reach, cuts, heavy, kind=jnp.bfloat16):
    drawn = scale * jax.random.normal(own_key, dims, jnp.float32)
    if cuts:
        drawn = drawn * block_scale(own_key, dims, cuts, -0.22, 0.18)
    return jnp.clip(spiked(drawn, jax.random.fold_in(own_key, 3), *heavy), -reach, reach).astype(kind)


def setup_inputs(seed: int = 0) -> dict:
    streams_of = jax.random.split(jax.random.key(seed), 7)
    hidden = heavy_noise(streams_of[0], (BATCH, SPAN, D), 1.0, 6.0, ((0, 8), (1, 16)), (1, 2, 16, 2.0))
    queries = draw_queries(jax.random.fold_in(streams_of[6], 71), 0)
    key_heads = draw_key_heads(jax.random.fold_in(streams_of[6], 71), 0)
    w_value = centred(streams_of[3], (D, HK * HD), D ** -0.5, 0.078125, ((0, 8),))
    d_out = centred(streams_of[4], (BATCH, SPAN, HQ * HD), 1.0, 6.0, ((0, 8), (1, 16)))
    segments = jax.vmap(lambda own: jnp.searchsorted(jnp.cumsum(ragged_sizes(own, 4, SPAN, SPAN // 2, 1)), jnp.arange(SPAN), side="right"))(jax.random.split(streams_of[5], BATCH)).reshape((BATCH, SPAN)).astype(jnp.int32)
    return dict(hidden=hidden, queries=queries, key_heads=key_heads, w_value=w_value, d_out=d_out, segments=segments)


score_scale = 1.0 / math.sqrt(168.0)

def one_sequence(tokens_in, query_all, key_all, w_value, grad_all, segment_ids):
    values = jnp.dot(tokens_in, w_value, preferred_element_type=jnp.float32).astype(jnp.bfloat16)
    kv_width = HK * HD
    span_rows = WINDOW + TOK_DEV
    pad_keys = jnp.concatenate([jnp.zeros((WINDOW, kv_width), key_all.dtype), key_all], 0)
    pad_values = jnp.concatenate([jnp.zeros((WINDOW, kv_width), values.dtype), values], 0)
    pad_segments = jnp.concatenate([jnp.full((WINDOW,), -1, jnp.int32), segment_ids.astype(jnp.int32)], 0)

    def block_step(carry, block_index):
        key_acc, value_acc = carry
        first_row = (block_index * TOK_DEV).astype(jnp.int32)
        query_rows = lax.dynamic_slice_in_dim(query_all, first_row, TOK_DEV, 0).reshape(TOK_DEV, HK, GROUP, HD).astype(jnp.float32)
        grad_heads = lax.dynamic_slice_in_dim(grad_all, first_row, TOK_DEV, 0).reshape(TOK_DEV, HK, GROUP, HD).astype(jnp.float32)
        window_keys = lax.dynamic_slice_in_dim(pad_keys, first_row, span_rows, 0).reshape(span_rows, HK, HD).astype(jnp.float32)
        window_values = lax.dynamic_slice_in_dim(pad_values, first_row, span_rows, 0).reshape(span_rows, HK, HD).astype(jnp.float32)
        window_tags = lax.dynamic_slice_in_dim(pad_segments, first_row, span_rows, 0)
        query_tags = lax.dynamic_slice_in_dim(segment_ids.astype(jnp.int32), first_row, TOK_DEV, 0)
        query_pos = first_row + jnp.arange(TOK_DEV, dtype=jnp.int32)
        key_pos = first_row - WINDOW + jnp.arange(span_rows, dtype=jnp.int32)
        distance = query_pos[:, None] - key_pos[None, :]
        allowed = (query_tags[:, None] == window_tags[None, :]) & (distance >= 0) & (distance < WINDOW) & (key_pos[None, :] >= 0)
        scores = jnp.einsum('tgrd,lgd->grtl', query_rows, window_keys) * score_scale
        scores = jnp.where(allowed, scores, -jnp.inf)
        highest = lax.optimization_barrier(jnp.max(scores, axis=-1, keepdims=True))
        raw_weights = jnp.exp(scores - highest)
        probs = raw_weights / lax.optimization_barrier(jnp.sum(raw_weights, axis=-1, keepdims=True))
        probs_low = probs.astype(jnp.bfloat16).astype(jnp.float32)
        out_heads = jnp.einsum('grtl,lgd->tgrd', probs_low, window_values).astype(jnp.bfloat16)
        grad_probs = jnp.einsum('tgrd,lgd->grtl', grad_heads, window_values)
        delta_sum = lax.optimization_barrier(jnp.sum(grad_heads * out_heads.astype(jnp.float32), axis=-1))
        delta_sum = jnp.transpose(delta_sum, (1, 2, 0))[..., None]
        grad_scores = (probs * (grad_probs - delta_sum)).astype(jnp.bfloat16).astype(jnp.float32)
        d_query_heads = (score_scale * jnp.einsum('grtl,lgd->tgrd', grad_scores, window_keys)).astype(jnp.bfloat16)
        key_terms = (score_scale * jnp.einsum('grtl,tgrd->lgd', grad_scores, query_rows)).astype(jnp.bfloat16)
        value_terms = jnp.einsum('grtl,tgrd->lgd', probs_low, grad_heads).astype(jnp.bfloat16)
        key_slice = lax.dynamic_slice_in_dim(key_acc, first_row, span_rows, 0) + key_terms.reshape(span_rows, kv_width).astype(jnp.float32)
        value_slice = lax.dynamic_slice_in_dim(value_acc, first_row, span_rows, 0) + value_terms.reshape(span_rows, kv_width).astype(jnp.float32)
        key_acc = lax.dynamic_update_slice_in_dim(key_acc, key_slice, first_row, 0)
        value_acc = lax.dynamic_update_slice_in_dim(value_acc, value_slice, first_row, 0)
        return ((key_acc, value_acc), (out_heads.reshape(TOK_DEV, HQ * HD), d_query_heads.reshape(TOK_DEV, HQ * HD)))
    start_acc = jnp.zeros((SPAN + WINDOW, kv_width), jnp.float32)
    (key_acc, value_acc), (out_blocks, query_blocks) = lax.scan(block_step, (start_acc, start_acc), jnp.arange(SPAN // TOK_DEV, dtype=jnp.int32))
    d_key_rows = key_acc[WINDOW:].astype(jnp.bfloat16)
    d_values = value_acc[WINDOW:]
    d_values_low = d_values.astype(jnp.bfloat16)
    d_tokens = lax.dot_general(d_values_low, w_value, (((1,), (1,)), ((), ())), preferred_element_type=jnp.float32).astype(jnp.bfloat16)
    weight_term = lax.dot_general(tokens_in, d_values_low, (((0,), (0,)), ((), ())), preferred_element_type=jnp.float32)
    return (out_blocks.reshape(SPAN, HQ * HD), query_blocks.reshape(SPAN, HQ * HD), d_key_rows, d_tokens, weight_term)

def reference(hidden, queries, key_heads, w_value, d_out, segments):

    def batch_step(weight_acc, members):
        tokens_in, query_all, key_all, grad_all, segment_ids = members
        out_rows, query_grads, key_grads, token_grads, weight_term = one_sequence(tokens_in, query_all, key_all, w_value, grad_all, segment_ids)
        return (weight_acc + weight_term, (out_rows, query_grads, key_grads, token_grads))
    weight_start = jnp.zeros((D, HK * HD), jnp.float32)
    d_w_value, (attn_out, d_queries, d_keys, d_hidden) = lax.scan(batch_step, weight_start, (hidden, queries, key_heads, d_out, segments))
    return (attn_out, d_queries, d_keys, d_hidden, d_w_value)
```

```python
import math

import jax
import jax.numpy as jnp
from jax import lax
from jax.sharding import PartitionSpec as P

HQ = 16
HK = 8
HD = 128
WINDOW = 1024
GROUP = 2


score_scale = 1.0 / math.sqrt(168.0)


def shifted(x, axis, by):
    length = lax.axis_size(axis)
    pairs = [(i, i + by) for i in range(length) if 0 <= i + by < length]
    return lax.ppermute(x, axis, pairs)


def shards(hidden, queries, key_heads, w_value, d_out, segments):
    shard_rows = hidden.shape[1]
    kv_width = w_value.shape[1]
    n_hops = WINDOW // shard_rows
    span_rows = (n_hops + 1) * shard_rows
    tokens_in = hidden[0]
    query_rows = queries[0].reshape(shard_rows, HK, GROUP, HD)
    own_keys = key_heads[0]
    own_segments = segments[0]
    grad_heads = d_out[0].reshape(shard_rows, HK, GROUP, HD)
    n_fsdp = lax.axis_size("fsdp")
    n_ctx = lax.axis_size("ctx")
    model_width = tokens_in.shape[1]
    half_rows = w_value.shape[0] // 2
    core = lax.axis_index("ctx") % 2
    w_mine = lax.all_gather(
        lax.dynamic_slice_in_dim(w_value, core * half_rows, half_rows, 0), "fsdp", axis=0, tiled=False
    )
    w_other = lax.ppermute(w_mine, "ctx", [(i, i ^ 1) for i in range(n_ctx)])
    token_halves = tokens_in.reshape(shard_rows, n_fsdp, 2, half_rows)
    tokens_mine = lax.dynamic_index_in_dim(token_halves, core, axis=2, keepdims=False)
    tokens_other = lax.dynamic_index_in_dim(token_halves, 1 - core, axis=2, keepdims=False)
    values = (
        jnp.einsum("tfr,frn->tn", tokens_mine, w_mine, preferred_element_type=jnp.float32)
        + jnp.einsum("tfr,frn->tn", tokens_other, w_other, preferred_element_type=jnp.float32)
    ).astype(jnp.bfloat16)
    out_rows = model_width // (n_ctx * n_fsdp)
    token_cols = (
        tokens_in.reshape(shard_rows, n_ctx, n_fsdp, out_rows).transpose(2, 0, 1, 3)
    )
    token_cols = lax.all_to_all(token_cols, "fsdp", 0, 0, tiled=True)
    segment_tags = own_segments.astype(jnp.bfloat16)
    arrived = []
    for hop_index in range(1, n_hops + 1):
        arrived.append(shifted((own_keys, values, segment_tags), "ctx", hop_index))
    ordered = arrived[::-1] + [(own_keys, values, segment_tags)]
    window_keys = jnp.concatenate([parcel[0] for parcel in ordered], 0).reshape(span_rows, HK, HD)
    window_values = jnp.concatenate([parcel[1] for parcel in ordered], 0).reshape(span_rows, HK, HD)
    window_tags = jnp.concatenate([parcel[2] for parcel in ordered], 0).astype(jnp.float32)
    first_query = lax.axis_index("ctx") * shard_rows
    query_pos = first_query + jnp.arange(shard_rows, dtype=jnp.int32)
    key_pos = first_query - WINDOW + jnp.arange(span_rows, dtype=jnp.int32)
    distance = query_pos[:, None] - key_pos[None, :]
    allowed = (
        (own_segments.astype(jnp.float32)[:, None] == window_tags[None, :])
        & (distance >= 0)
        & (distance < WINDOW)
        & (key_pos[None, :] >= 0)
    )
    scores = (
        jnp.einsum("tgrd,lgd->grtl", query_rows, window_keys, preferred_element_type=jnp.float32)
        * score_scale
    )
    scores = jnp.where(allowed, scores, -jnp.inf)
    highest = jnp.max(scores, axis=-1, keepdims=True)
    raw_weights = jnp.exp(scores - highest)
    probs = raw_weights / jnp.sum(raw_weights, axis=-1, keepdims=True)
    probs_low = probs.astype(jnp.bfloat16)
    out_heads = jnp.einsum(
        "grtl,lgd->tgrd", probs_low, window_values, preferred_element_type=jnp.float32
    ).astype(jnp.bfloat16)
    grad_probs = jnp.einsum(
        "tgrd,lgd->grtl", grad_heads, window_values, preferred_element_type=jnp.float32
    )
    delta_sum = jnp.sum(grad_heads.astype(jnp.float32) * out_heads.astype(jnp.float32), axis=-1)
    delta_sum = jnp.transpose(delta_sum, (1, 2, 0))[..., None]
    grad_scores = (probs * (grad_probs - delta_sum)).astype(jnp.bfloat16)
    d_query_heads = (
        score_scale
        * jnp.einsum("grtl,lgd->tgrd", grad_scores, window_keys, preferred_element_type=jnp.float32)
    ).astype(jnp.bfloat16)
    key_terms = (
        (
            score_scale
            * jnp.einsum(
                "grtl,tgrd->lgd", grad_scores, query_rows, preferred_element_type=jnp.float32
            )
        )
        .astype(jnp.bfloat16)
        .reshape(span_rows, kv_width)
    )
    value_terms = (
        jnp.einsum("grtl,tgrd->lgd", probs_low, grad_heads, preferred_element_type=jnp.float32)
        .astype(jnp.bfloat16)
        .reshape(span_rows, kv_width)
    )
    own_start = n_hops * shard_rows
    key_total = key_terms[own_start:].astype(jnp.float32)
    value_total = value_terms[own_start:].astype(jnp.float32)
    for hop_index in range(1, n_hops + 1):
        low_edge = (n_hops - hop_index) * shard_rows
        back_keys, back_values = shifted(
            (
                key_terms[low_edge : low_edge + shard_rows],
                value_terms[low_edge : low_edge + shard_rows],
            ),
            "ctx",
            -hop_index,
        )
        key_total = key_total + back_keys.astype(jnp.float32)
        value_total = value_total + back_values.astype(jnp.float32)
    d_key_rows = key_total.astype(jnp.bfloat16)
    d_values_low = value_total.astype(jnp.bfloat16)
    d_mine = jnp.einsum("tn,frn->tfr", d_values_low, w_mine, preferred_element_type=jnp.float32).astype(jnp.bfloat16)
    d_other = jnp.einsum("tn,frn->tfr", d_values_low, w_other, preferred_element_type=jnp.float32).astype(jnp.bfloat16)
    d_tokens = jnp.where(
        core == 0, jnp.stack([d_mine, d_other], 2), jnp.stack([d_other, d_mine], 2)
    ).reshape(shard_rows, model_width)
    grads_all = lax.all_gather(d_values_low, "fsdp", axis=0, tiled=False)
    weight_part = jnp.einsum(
        "ftcr,ftn->crn", token_cols, grads_all, preferred_element_type=jnp.float32
    ).reshape(n_ctx * out_rows, kv_width)
    d_weight = lax.psum_scatter(weight_part, "ctx", scatter_dimension=0, tiled=True)
    return (
        out_heads.reshape(shard_rows, HQ * HD)[None],
        d_query_heads.reshape(shard_rows, HQ * HD)[None],
        d_key_rows[None],
        d_tokens[None],
        d_weight,
    )


def solution(mesh):
    in_specs = (
        P("fsdp", "ctx", None),
        P("fsdp", "ctx", None),
        P("fsdp", "ctx", None),
        P("fsdp", None),
        P("fsdp", "ctx", None),
        P("fsdp", "ctx"),
    )
    out_specs = (
        P("fsdp", "ctx", None),
        P("fsdp", "ctx", None),
        P("fsdp", "ctx", None),
        P("fsdp", "ctx", None),
        P(("ctx", "fsdp"), None),
    )
    return jax.shard_map(shards, mesh=mesh, in_specs=in_specs, out_specs=out_specs, check_vma=False)
```

```python
import math

import jax
import jax.numpy as jnp
from jax import lax
from jax.sharding import PartitionSpec as P

HQ = 16
HK = 8
HD = 128
WINDOW = 1024
GROUP = 2


score_scale = 1.0 / math.sqrt(168.0)


def shifted(x, axis, by):
    length = lax.axis_size(axis)
    pairs = [(i, i + by) for i in range(length) if 0 <= i + by < length]
    return lax.ppermute(x, axis, pairs)


def shards(hidden, queries, key_heads, w_value, d_out, segments):
    shard_rows = hidden.shape[1]
    kv_width = w_value.shape[1]
    n_hops = WINDOW // shard_rows
    span_rows = (n_hops + 1) * shard_rows
    tokens_in = hidden[0]
    query_rows = queries[0].reshape(shard_rows, HK, GROUP, HD)
    own_keys = key_heads[0]
    own_segments = segments[0]
    grad_heads = d_out[0].reshape(shard_rows, HK, GROUP, HD)
    n_fsdp = lax.axis_size("fsdp")
    n_ctx = lax.axis_size("ctx")
    model_width = tokens_in.shape[1]
    half_rows = w_value.shape[0] // 2
    core = lax.axis_index("ctx") % 2
    w_mine = lax.all_gather(
        lax.dynamic_slice_in_dim(w_value, core * half_rows, half_rows, 0), "fsdp", axis=0, tiled=False
    )
    w_other = lax.ppermute(w_mine, "ctx", [(i, i ^ 1) for i in range(n_ctx)])
    token_halves = tokens_in.reshape(shard_rows, n_fsdp, 2, half_rows)
    tokens_mine = lax.dynamic_index_in_dim(token_halves, core, axis=2, keepdims=False)
    tokens_other = lax.dynamic_index_in_dim(token_halves, 1 - core, axis=2, keepdims=False)
    values = (
        jnp.einsum("tfr,frn->tn", tokens_mine, w_mine, preferred_element_type=jnp.float32)
        + jnp.einsum("tfr,frn->tn", tokens_other, w_other, preferred_element_type=jnp.float32)
    ).astype(jnp.bfloat16)
    out_rows = model_width // (n_ctx * n_fsdp)
    token_cols = (
        tokens_in.reshape(shard_rows, n_ctx, n_fsdp, out_rows).transpose(2, 0, 1, 3)
    )
    token_cols = lax.all_to_all(token_cols, "fsdp", 0, 0, tiled=True)
    segment_tags = own_segments.astype(jnp.bfloat16)
    arrived = []
    for hop_index in range(1, n_hops + 1):
        arrived.append(shifted((own_keys, values, segment_tags), "ctx", hop_index))
    ordered = arrived[::-1] + [(own_keys, values, segment_tags)]
    window_keys = jnp.concatenate([parcel[0] for parcel in ordered], 0).reshape(span_rows, HK, HD)
    window_values = jnp.concatenate([parcel[1] for parcel in ordered], 0).reshape(span_rows, HK, HD)
    window_tags = jnp.concatenate([parcel[2] for parcel in ordered], 0).astype(jnp.float32)
    first_query = lax.axis_index("ctx") * shard_rows
    query_pos = first_query + jnp.arange(shard_rows, dtype=jnp.int32)
    key_pos = first_query - WINDOW + jnp.arange(span_rows, dtype=jnp.int32)
    distance = query_pos[:, None] - key_pos[None, :]
    allowed = (
        (own_segments.astype(jnp.float32)[:, None] == window_tags[None, :])
        & (distance >= 0)
        & (distance < WINDOW)
        & (key_pos[None, :] >= 0)
    )
    scores = (
        jnp.einsum("tgrd,lgd->grtl", query_rows, window_keys, preferred_element_type=jnp.float32)
        * score_scale
    )
    scores = jnp.where(allowed, scores, -jnp.inf)
    highest = jnp.max(scores, axis=-1, keepdims=True)
    raw_weights = jnp.exp(scores - highest)
    probs = raw_weights / jnp.sum(raw_weights, axis=-1, keepdims=True)
    probs_low = probs.astype(jnp.bfloat16)
    out_heads = jnp.einsum(
        "grtl,lgd->tgrd", probs_low, window_values, preferred_element_type=jnp.float32
    ).astype(jnp.bfloat16)
    grad_probs = jnp.einsum(
        "tgrd,lgd->grtl", grad_heads, window_values, preferred_element_type=jnp.float32
    )
    delta_sum = jnp.sum(grad_heads.astype(jnp.float32) * out_heads.astype(jnp.float32), axis=-1)
    delta_sum = jnp.transpose(delta_sum, (1, 2, 0))[..., None]
    grad_scores = (probs * (grad_probs - delta_sum)).astype(jnp.bfloat16)
    d_query_heads = (
        score_scale
        * jnp.einsum("grtl,lgd->tgrd", grad_scores, window_keys, preferred_element_type=jnp.float32)
    ).astype(jnp.bfloat16)
    key_terms = (
        (
            score_scale
            * jnp.einsum(
                "grtl,tgrd->lgd", grad_scores, query_rows, preferred_element_type=jnp.float32
            )
        )
        .astype(jnp.bfloat16)
        .reshape(span_rows, kv_width)
    )
    value_terms = (
        jnp.einsum("grtl,tgrd->lgd", probs_low, grad_heads, preferred_element_type=jnp.float32)
        .astype(jnp.bfloat16)
        .reshape(span_rows, kv_width)
    )
    own_start = n_hops * shard_rows
    key_total = key_terms[own_start:].astype(jnp.float32)
    value_total = value_terms[own_start:].astype(jnp.float32)
    for hop_index in range(1, n_hops + 1):
        low_edge = (n_hops - hop_index) * shard_rows
        back_keys, back_values = shifted(
            (
                key_terms[low_edge : low_edge + shard_rows],
                value_terms[low_edge : low_edge + shard_rows],
            ),
            "ctx",
            -hop_index,
        )
        key_total = key_total + back_keys.astype(jnp.float32)
        value_total = value_total + back_values.astype(jnp.float32)
    d_key_rows = key_total.astype(jnp.bfloat16)
    d_values_low = value_total.astype(jnp.bfloat16)
    d_mine = jnp.einsum("tn,frn->tfr", d_values_low, w_mine, preferred_element_type=jnp.float32).astype(jnp.bfloat16)
    d_other = jnp.einsum("tn,frn->tfr", d_values_low, w_other, preferred_element_type=jnp.float32).astype(jnp.bfloat16)
    d_tokens = jnp.where(
        core == 0, jnp.stack([d_mine, d_other], 2), jnp.stack([d_other, d_mine], 2)
    ).reshape(shard_rows, model_width)
    grads_all = lax.all_gather(d_values_low, "fsdp", axis=0, tiled=False)
    token_cols, grads_all, d_query_heads, d_tokens = lax.optimization_barrier(
        (token_cols, grads_all, d_query_heads, d_tokens)
    )
    weight_part = jnp.einsum(
        "ftcr,ftn->crn", token_cols, grads_all, preferred_element_type=jnp.float32
    ).reshape(n_ctx * out_rows, kv_width)
    d_weight = lax.psum_scatter(weight_part, "ctx", scatter_dimension=0, tiled=True)
    return (
        out_heads.reshape(shard_rows, HQ * HD)[None],
        d_query_heads.reshape(shard_rows, HQ * HD)[None],
        d_key_rows[None],
        d_tokens[None],
        d_weight,
    )


def solution(mesh):
    in_specs = (
        P("fsdp", "ctx", None),
        P("fsdp", "ctx", None),
        P("fsdp", "ctx", None),
        P("fsdp", None),
        P("fsdp", "ctx", None),
        P("fsdp", "ctx"),
    )
    out_specs = (
        P("fsdp", "ctx", None),
        P("fsdp", "ctx", None),
        P("fsdp", "ctx", None),
        P("fsdp", "ctx", None),
        P(("ctx", "fsdp"), None),
    )
    return jax.shard_map(shards, mesh=mesh, in_specs=in_specs, out_specs=out_specs, check_vma=False)
```

```python
import math

import jax
import jax.numpy as jnp
from jax import lax
from jax.experimental import pallas as pl
from jax.experimental.pallas import tpu as pltpu
from jax.sharding import PartitionSpec as P

HQ = 16
HK = 8
HD = 128
WINDOW = 1024
GROUP = 2


score_scale = 1.0 / math.sqrt(168.0)


def attention_kernel(q_ref, k_ref, v_ref, do_ref, qtag_ref, ktag_ref, out_ref, dq_ref, dk_ref, dv_ref):
    rows = q_ref.shape[0]
    span = k_ref.shape[0]
    reach = span - rows
    q = jnp.concatenate([q_ref[:, r * HD:(r + 1) * HD] for r in range(GROUP)], axis=0)
    grad = jnp.concatenate([do_ref[:, r * HD:(r + 1) * HD] for r in range(GROUP)], axis=0)
    keys = k_ref[...]
    vals = v_ref[...]
    t_idx = lax.broadcasted_iota(jnp.int32, (rows, span), 0)
    l_idx = lax.broadcasted_iota(jnp.int32, (rows, span), 1)
    allowed = (qtag_ref[...] == ktag_ref[...]) & (l_idx > t_idx) & (l_idx <= t_idx + reach)
    allowed = jnp.concatenate([allowed] * GROUP, axis=0)
    scores = lax.dot_general(q, keys, (((1,), (1,)), ((), ())), preferred_element_type=jnp.float32) * score_scale
    scores = jnp.where(allowed, scores, -jnp.inf)
    highest = jnp.max(scores, axis=-1, keepdims=True)
    raw = jnp.exp(scores - highest)
    probs = raw / jnp.sum(raw, axis=-1, keepdims=True)
    probs_low = probs.astype(jnp.bfloat16)
    out = jnp.dot(probs_low, vals, preferred_element_type=jnp.float32).astype(jnp.bfloat16)
    grad_probs = lax.dot_general(grad, vals, (((1,), (1,)), ((), ())), preferred_element_type=jnp.float32)
    delta = jnp.sum(grad.astype(jnp.float32) * out.astype(jnp.float32), axis=-1, keepdims=True)
    grad_scores = (probs * (grad_probs - delta)).astype(jnp.bfloat16)
    dq = (score_scale * jnp.dot(grad_scores, keys, preferred_element_type=jnp.float32)).astype(jnp.bfloat16)
    dk = score_scale * lax.dot_general(grad_scores, q, (((0,), (0,)), ((), ())), preferred_element_type=jnp.float32)
    dv = lax.dot_general(probs_low, grad, (((0,), (0,)), ((), ())), preferred_element_type=jnp.float32)
    for r in range(GROUP):
        out_ref[:, r * HD:(r + 1) * HD] = out[r * rows:(r + 1) * rows]
        dq_ref[:, r * HD:(r + 1) * HD] = dq[r * rows:(r + 1) * rows]
    dk_ref[...] = dk.astype(jnp.bfloat16)
    dv_ref[...] = dv.astype(jnp.bfloat16)


def fused_attention(queries, keys, values, grads, query_tags, key_tags):
    rows, q_width = queries.shape
    span, kv_width = keys.shape
    heads = kv_width // HD
    group_width = GROUP * HD
    q_spec = pl.BlockSpec((rows, group_width), lambda g: (0, g))
    kv_spec = pl.BlockSpec((span, HD), lambda g: (0, g))
    flops = 12 * rows * GROUP * span * HD * heads
    return pl.pallas_call(
        attention_kernel,
        grid=(heads,),
        in_specs=[
            q_spec,
            kv_spec,
            kv_spec,
            q_spec,
            pl.BlockSpec((rows, 1), lambda g: (0, 0)),
            pl.BlockSpec((1, span), lambda g: (0, 0)),
        ],
        out_specs=[q_spec, q_spec, kv_spec, kv_spec],
        out_shape=[
            jax.ShapeDtypeStruct((rows, q_width), jnp.bfloat16),
            jax.ShapeDtypeStruct((rows, q_width), jnp.bfloat16),
            jax.ShapeDtypeStruct((span, kv_width), jnp.bfloat16),
            jax.ShapeDtypeStruct((span, kv_width), jnp.bfloat16),
        ],
        cost_estimate=pl.CostEstimate(
            flops=flops,
            transcendentals=rows * GROUP * span * heads,
            bytes_accessed=2 * (4 * rows * q_width + 4 * span * kv_width),
        ),
    )(queries, keys, values, grads, query_tags, key_tags)


def shifted(x, axis, by):
    length = lax.axis_size(axis)
    pairs = [(i, i + by) for i in range(length) if 0 <= i + by < length]
    return lax.ppermute(x, axis, pairs)


def shards(hidden, queries, key_heads, w_value, d_out, segments):
    shard_rows = hidden.shape[1]
    kv_width = w_value.shape[1]
    n_hops = WINDOW // shard_rows
    span_rows = (n_hops + 1) * shard_rows
    tokens_in = hidden[0]
    own_keys = key_heads[0]
    own_segments = segments[0]
    n_fsdp = lax.axis_size("fsdp")
    n_ctx = lax.axis_size("ctx")
    model_width = tokens_in.shape[1]
    half_rows = w_value.shape[0] // 2
    core = lax.axis_index("ctx") % 2
    w_mine = lax.all_gather(
        lax.dynamic_slice_in_dim(w_value, core * half_rows, half_rows, 0), "fsdp", axis=0, tiled=False
    )
    w_other = lax.ppermute(w_mine, "ctx", [(i, i ^ 1) for i in range(n_ctx)])
    token_halves = tokens_in.reshape(shard_rows, n_fsdp, 2, half_rows)
    tokens_mine = lax.dynamic_index_in_dim(token_halves, core, axis=2, keepdims=False)
    tokens_other = lax.dynamic_index_in_dim(token_halves, 1 - core, axis=2, keepdims=False)
    values = (
        jnp.einsum("tfr,frn->tn", tokens_mine, w_mine, preferred_element_type=jnp.float32)
        + jnp.einsum("tfr,frn->tn", tokens_other, w_other, preferred_element_type=jnp.float32)
    ).astype(jnp.bfloat16)
    out_rows = model_width // (n_ctx * n_fsdp)
    token_cols = (
        tokens_in.reshape(shard_rows, n_ctx, n_fsdp, out_rows).transpose(2, 0, 1, 3)
    )
    token_cols = lax.all_to_all(token_cols, "fsdp", 0, 0, tiled=True)
    segment_tags = own_segments.astype(jnp.bfloat16)
    arrived = []
    for hop_index in range(1, n_hops + 1):
        arrived.append(shifted((own_keys, values, segment_tags), "ctx", hop_index))
    ordered = arrived[::-1] + [(own_keys, values, segment_tags)]
    window_keys = jnp.concatenate([parcel[0] for parcel in ordered], 0)
    window_values = jnp.concatenate([parcel[1] for parcel in ordered], 0)
    window_tags = jnp.concatenate([parcel[2] for parcel in ordered], 0).astype(jnp.int32)
    first_query = lax.axis_index("ctx") * shard_rows
    key_pos = first_query - WINDOW + jnp.arange(span_rows, dtype=jnp.int32)
    key_tags = jnp.where(key_pos >= 0, window_tags, -1)
    out_rows_attn, d_query_heads, key_terms, value_terms = fused_attention(
        queries[0],
        window_keys,
        window_values,
        d_out[0],
        own_segments.astype(jnp.int32)[:, None],
        key_tags[None, :],
    )
    own_start = n_hops * shard_rows
    key_total = key_terms[own_start:].astype(jnp.float32)
    value_total = value_terms[own_start:].astype(jnp.float32)
    for hop_index in range(1, n_hops + 1):
        low_edge = (n_hops - hop_index) * shard_rows
        back_keys, back_values = shifted(
            (
                key_terms[low_edge : low_edge + shard_rows],
                value_terms[low_edge : low_edge + shard_rows],
            ),
            "ctx",
            -hop_index,
        )
        key_total = key_total + back_keys.astype(jnp.float32)
        value_total = value_total + back_values.astype(jnp.float32)
    d_key_rows = key_total.astype(jnp.bfloat16)
    d_values_low = value_total.astype(jnp.bfloat16)
    d_mine = jnp.einsum("tn,frn->tfr", d_values_low, w_mine, preferred_element_type=jnp.float32).astype(jnp.bfloat16)
    d_other = jnp.einsum("tn,frn->tfr", d_values_low, w_other, preferred_element_type=jnp.float32).astype(jnp.bfloat16)
    d_tokens = jnp.where(
        core == 0, jnp.stack([d_mine, d_other], 2), jnp.stack([d_other, d_mine], 2)
    ).reshape(shard_rows, model_width)
    grads_all = lax.all_gather(d_values_low, "fsdp", axis=0, tiled=False)
    token_cols, grads_all, d_query_heads, d_tokens = lax.optimization_barrier(
        (token_cols, grads_all, d_query_heads, d_tokens)
    )
    weight_part = jnp.einsum(
        "ftcr,ftn->crn", token_cols, grads_all, preferred_element_type=jnp.float32
    ).reshape(n_ctx * out_rows, kv_width)
    d_weight = lax.psum_scatter(weight_part, "ctx", scatter_dimension=0, tiled=True)
    return (
        out_rows_attn[None],
        d_query_heads[None],
        d_key_rows[None],
        d_tokens[None],
        d_weight,
    )


def solution(mesh):
    in_specs = (
        P("fsdp", "ctx", None),
        P("fsdp", "ctx", None),
        P("fsdp", "ctx", None),
        P("fsdp", None),
        P("fsdp", "ctx", None),
        P("fsdp", "ctx"),
    )
    out_specs = (
        P("fsdp", "ctx", None),
        P("fsdp", "ctx", None),
        P("fsdp", "ctx", None),
        P("fsdp", "ctx", None),
        P(("ctx", "fsdp"), None),
    )
    return jax.shard_map(shards, mesh=mesh, in_specs=in_specs, out_specs=out_specs, check_vma=False)
```

```python
import functools
import math

import jax
import jax.numpy as jnp
from jax import lax
from jax.experimental import pallas as pl
from jax.experimental.pallas import tpu as pltpu
from jax.sharding import PartitionSpec as P

HQ = 16
HK = 8
HD = 128
WINDOW = 1024
GROUP = 2


score_scale = 1.0 / math.sqrt(168.0)


def attention_kernel(q_ref, k_ref, v_ref, do_ref, qtag_ref, ktag_ref, out_ref, dq_ref, dk_ref, dv_ref):
    rows = q_ref.shape[0]
    span = k_ref.shape[0]
    reach = span - rows
    q = jnp.concatenate([q_ref[:, r * HD:(r + 1) * HD] for r in range(GROUP)], axis=0)
    grad = jnp.concatenate([do_ref[:, r * HD:(r + 1) * HD] for r in range(GROUP)], axis=0)
    keys = k_ref[...]
    vals = v_ref[...]
    t_idx = lax.broadcasted_iota(jnp.int32, (rows, span), 0)
    l_idx = lax.broadcasted_iota(jnp.int32, (rows, span), 1)
    allowed = (qtag_ref[...] == ktag_ref[...]) & (l_idx > t_idx) & (l_idx <= t_idx + reach)
    allowed = jnp.concatenate([allowed] * GROUP, axis=0)
    scores = lax.dot_general(q, keys, (((1,), (1,)), ((), ())), preferred_element_type=jnp.float32) * score_scale
    scores = jnp.where(allowed, scores, -jnp.inf)
    highest = jnp.max(scores, axis=-1, keepdims=True)
    raw = jnp.exp(scores - highest)
    probs = raw / jnp.sum(raw, axis=-1, keepdims=True)
    probs_low = probs.astype(jnp.bfloat16)
    out = jnp.dot(probs_low, vals, preferred_element_type=jnp.float32).astype(jnp.bfloat16)
    grad_probs = lax.dot_general(grad, vals, (((1,), (1,)), ((), ())), preferred_element_type=jnp.float32)
    delta = jnp.sum(grad.astype(jnp.float32) * out.astype(jnp.float32), axis=-1, keepdims=True)
    grad_scores = (probs * (grad_probs - delta)).astype(jnp.bfloat16)
    dq = (score_scale * jnp.dot(grad_scores, keys, preferred_element_type=jnp.float32)).astype(jnp.bfloat16)
    dk = score_scale * lax.dot_general(grad_scores, q, (((0,), (0,)), ((), ())), preferred_element_type=jnp.float32)
    dv = lax.dot_general(probs_low, grad, (((0,), (0,)), ((), ())), preferred_element_type=jnp.float32)
    for r in range(GROUP):
        out_ref[:, r * HD:(r + 1) * HD] = out[r * rows:(r + 1) * rows]
        dq_ref[:, r * HD:(r + 1) * HD] = dq[r * rows:(r + 1) * rows]
    dk_ref[...] = dk.astype(jnp.bfloat16)
    dv_ref[...] = dv.astype(jnp.bfloat16)


def fused_attention(queries, keys, values, grads, query_tags, key_tags):
    rows, q_width = queries.shape
    span, kv_width = keys.shape
    heads = kv_width // HD
    group_width = GROUP * HD
    q_spec = pl.BlockSpec((rows, group_width), lambda g: (0, g))
    kv_spec = pl.BlockSpec((span, HD), lambda g: (0, g))
    flops = 12 * rows * GROUP * span * HD * heads
    return pl.pallas_call(
        attention_kernel,
        grid=(heads,),
        in_specs=[
            q_spec,
            kv_spec,
            kv_spec,
            q_spec,
            pl.BlockSpec((rows, 1), lambda g: (0, 0)),
            pl.BlockSpec((1, span), lambda g: (0, 0)),
        ],
        out_specs=[q_spec, q_spec, kv_spec, kv_spec],
        out_shape=[
            jax.ShapeDtypeStruct((rows, q_width), jnp.bfloat16),
            jax.ShapeDtypeStruct((rows, q_width), jnp.bfloat16),
            jax.ShapeDtypeStruct((span, kv_width), jnp.bfloat16),
            jax.ShapeDtypeStruct((span, kv_width), jnp.bfloat16),
        ],
        cost_estimate=pl.CostEstimate(
            flops=flops,
            transcendentals=rows * GROUP * span * heads,
            bytes_accessed=2 * (4 * rows * q_width + 4 * span * kv_width),
        ),
    )(queries, keys, values, grads, query_tags, key_tags)


def peer_gather_kernel(axis, n, x_ref, o_ref, send_sem, recv_sem, local_sem):
    me = lax.axis_index(axis)
    barrier = pltpu.get_barrier_semaphore()
    for k in range(1, n):
        pl.semaphore_signal(
            barrier, inc=1, device_id={axis: lax.rem(me + k, n)}, device_id_type=pl.DeviceIdType.MESH
        )
    pl.semaphore_wait(barrier, n - 1)
    local = pltpu.make_async_copy(x_ref, o_ref.at[me], local_sem)
    local.start()
    copies = []
    for k in range(1, n):
        copy = pltpu.make_async_remote_copy(
            src_ref=x_ref,
            dst_ref=o_ref.at[me],
            send_sem=send_sem.at[k],
            recv_sem=recv_sem.at[k],
            device_id={axis: lax.rem(me + k, n)},
            device_id_type=pl.DeviceIdType.MESH,
        )
        copy.start()
        copies.append(copy)
    for copy in copies:
        copy.wait()
    local.wait()


def peer_gather(x, axis, collective_id):
    n = lax.axis_size(axis)
    return pl.pallas_call(
        functools.partial(peer_gather_kernel, axis, n),
        out_shape=jax.ShapeDtypeStruct((n,) + x.shape, x.dtype),
        in_specs=[pl.BlockSpec(memory_space=pl.ANY)],
        out_specs=pl.BlockSpec(memory_space=pl.ANY),
        scratch_shapes=[
            pltpu.SemaphoreType.DMA((n,)),
            pltpu.SemaphoreType.DMA((n,)),
            pltpu.SemaphoreType.DMA,
        ],
        compiler_params=pltpu.CompilerParams(collective_id=collective_id, has_side_effects=True),
    )(x)


def shifted(x, axis, by):
    length = lax.axis_size(axis)
    pairs = [(i, i + by) for i in range(length) if 0 <= i + by < length]
    return lax.ppermute(x, axis, pairs)


def shards(hidden, queries, key_heads, w_value, d_out, segments):
    shard_rows = hidden.shape[1]
    kv_width = w_value.shape[1]
    n_hops = WINDOW // shard_rows
    span_rows = (n_hops + 1) * shard_rows
    tokens_in = hidden[0]
    own_keys = key_heads[0]
    own_segments = segments[0]
    n_fsdp = lax.axis_size("fsdp")
    n_ctx = lax.axis_size("ctx")
    model_width = tokens_in.shape[1]
    half_rows = w_value.shape[0] // 2
    core = lax.axis_index("ctx") % 2
    w_mine = peer_gather(lax.dynamic_slice_in_dim(w_value, core * half_rows, half_rows, 0), "fsdp", 1)
    w_other = lax.ppermute(w_mine, "ctx", [(i, i ^ 1) for i in range(n_ctx)])
    token_halves = tokens_in.reshape(shard_rows, n_fsdp, 2, half_rows)
    tokens_mine = lax.dynamic_index_in_dim(token_halves, core, axis=2, keepdims=False)
    tokens_other = lax.dynamic_index_in_dim(token_halves, 1 - core, axis=2, keepdims=False)
    values = (
        jnp.einsum("tfr,frn->tn", tokens_mine, w_mine, preferred_element_type=jnp.float32)
        + jnp.einsum("tfr,frn->tn", tokens_other, w_other, preferred_element_type=jnp.float32)
    ).astype(jnp.bfloat16)
    out_rows = model_width // (n_ctx * n_fsdp)
    token_cols = (
        tokens_in.reshape(shard_rows, n_ctx, n_fsdp, out_rows).transpose(2, 0, 1, 3)
    )
    token_cols = lax.all_to_all(token_cols, "fsdp", 0, 0, tiled=True)
    segment_tags = own_segments.astype(jnp.bfloat16)
    arrived = []
    for hop_index in range(1, n_hops + 1):
        arrived.append(shifted((own_keys, values, segment_tags), "ctx", hop_index))
    ordered = arrived[::-1] + [(own_keys, values, segment_tags)]
    window_keys = jnp.concatenate([parcel[0] for parcel in ordered], 0)
    window_values = jnp.concatenate([parcel[1] for parcel in ordered], 0)
    window_tags = jnp.concatenate([parcel[2] for parcel in ordered], 0).astype(jnp.int32)
    first_query = lax.axis_index("ctx") * shard_rows
    key_pos = first_query - WINDOW + jnp.arange(span_rows, dtype=jnp.int32)
    key_tags = jnp.where(key_pos >= 0, window_tags, -1)
    out_rows_attn, d_query_heads, key_terms, value_terms = fused_attention(
        queries[0],
        window_keys,
        window_values,
        d_out[0],
        own_segments.astype(jnp.int32)[:, None],
        key_tags[None, :],
    )
    own_start = n_hops * shard_rows
    key_total = key_terms[own_start:].astype(jnp.float32)
    value_total = value_terms[own_start:].astype(jnp.float32)
    for hop_index in range(1, n_hops + 1):
        low_edge = (n_hops - hop_index) * shard_rows
        back_keys, back_values = shifted(
            (
                key_terms[low_edge : low_edge + shard_rows],
                value_terms[low_edge : low_edge + shard_rows],
            ),
            "ctx",
            -hop_index,
        )
        key_total = key_total + back_keys.astype(jnp.float32)
        value_total = value_total + back_values.astype(jnp.float32)
    d_key_rows = key_total.astype(jnp.bfloat16)
    d_values_low = value_total.astype(jnp.bfloat16)
    d_mine = jnp.einsum("tn,frn->tfr", d_values_low, w_mine, preferred_element_type=jnp.float32).astype(jnp.bfloat16)
    d_other = jnp.einsum("tn,frn->tfr", d_values_low, w_other, preferred_element_type=jnp.float32).astype(jnp.bfloat16)
    d_tokens = jnp.where(
        core == 0, jnp.stack([d_mine, d_other], 2), jnp.stack([d_other, d_mine], 2)
    ).reshape(shard_rows, model_width)
    grads_all = peer_gather(d_values_low, "fsdp", 2)
    token_cols, grads_all, d_query_heads, d_tokens = lax.optimization_barrier(
        (token_cols, grads_all, d_query_heads, d_tokens)
    )
    weight_part = jnp.einsum(
        "ftcr,ftn->crn", token_cols, grads_all, preferred_element_type=jnp.float32
    ).reshape(n_ctx * out_rows, kv_width)
    d_weight = lax.psum_scatter(weight_part, "ctx", scatter_dimension=0, tiled=True)
    return (
        out_rows_attn[None],
        d_query_heads[None],
        d_key_rows[None],
        d_tokens[None],
        d_weight,
    )


def solution(mesh):
    in_specs = (
        P("fsdp", "ctx", None),
        P("fsdp", "ctx", None),
        P("fsdp", "ctx", None),
        P("fsdp", None),
        P("fsdp", "ctx", None),
        P("fsdp", "ctx"),
    )
    out_specs = (
        P("fsdp", "ctx", None),
        P("fsdp", "ctx", None),
        P("fsdp", "ctx", None),
        P("fsdp", "ctx", None),
        P(("ctx", "fsdp"), None),
    )
    return jax.shard_map(shards, mesh=mesh, in_specs=in_specs, out_specs=out_specs, check_vma=False)
```

```python
import functools
import math

import jax
import jax.numpy as jnp
from jax import lax
from jax.experimental import pallas as pl
from jax.experimental.pallas import tpu as pltpu
from jax.sharding import PartitionSpec as P

HQ = 16
HK = 8
HD = 128
WINDOW = 1024
GROUP = 2


score_scale = 1.0 / math.sqrt(168.0)


def attention_kernel(q_ref, k_ref, v_ref, do_ref, qtag_ref, ktag_ref, out_ref, dq_ref, dk_ref, dv_ref):
    rows = q_ref.shape[0]
    span = k_ref.shape[0]
    reach = span - rows
    q = jnp.concatenate([q_ref[:, r * HD:(r + 1) * HD] for r in range(GROUP)], axis=0)
    grad = jnp.concatenate([do_ref[:, r * HD:(r + 1) * HD] for r in range(GROUP)], axis=0)
    keys = k_ref[...]
    vals = v_ref[...]
    t_idx = lax.broadcasted_iota(jnp.int32, (rows, span), 0)
    l_idx = lax.broadcasted_iota(jnp.int32, (rows, span), 1)
    allowed = (qtag_ref[...] == ktag_ref[...]) & (l_idx > t_idx) & (l_idx <= t_idx + reach)
    allowed = jnp.concatenate([allowed] * GROUP, axis=0)
    scores = lax.dot_general(q, keys, (((1,), (1,)), ((), ())), preferred_element_type=jnp.float32) * score_scale
    scores = jnp.where(allowed, scores, -jnp.inf)
    highest = jnp.max(scores, axis=-1, keepdims=True)
    raw = jnp.exp(scores - highest)
    probs = raw / jnp.sum(raw, axis=-1, keepdims=True)
    probs_low = probs.astype(jnp.bfloat16)
    out = jnp.dot(probs_low, vals, preferred_element_type=jnp.float32).astype(jnp.bfloat16)
    grad_probs = lax.dot_general(grad, vals, (((1,), (1,)), ((), ())), preferred_element_type=jnp.float32)
    delta = jnp.sum(grad.astype(jnp.float32) * out.astype(jnp.float32), axis=-1, keepdims=True)
    grad_scores = (probs * (grad_probs - delta)).astype(jnp.bfloat16)
    dq = (score_scale * jnp.dot(grad_scores, keys, preferred_element_type=jnp.float32)).astype(jnp.bfloat16)
    dk = score_scale * lax.dot_general(grad_scores, q, (((0,), (0,)), ((), ())), preferred_element_type=jnp.float32)
    dv = lax.dot_general(probs_low, grad, (((0,), (0,)), ((), ())), preferred_element_type=jnp.float32)
    for r in range(GROUP):
        out_ref[:, r * HD:(r + 1) * HD] = out[r * rows:(r + 1) * rows]
        dq_ref[:, r * HD:(r + 1) * HD] = dq[r * rows:(r + 1) * rows]
    dk_ref[...] = dk.astype(jnp.bfloat16)
    dv_ref[...] = dv.astype(jnp.bfloat16)


def fused_attention(queries, keys, values, grads, query_tags, key_tags):
    rows, q_width = queries.shape
    span, kv_width = keys.shape
    heads = kv_width // HD
    group_width = GROUP * HD
    q_spec = pl.BlockSpec((rows, group_width), lambda g: (0, g))
    kv_spec = pl.BlockSpec((span, HD), lambda g: (0, g))
    flops = 12 * rows * GROUP * span * HD * heads
    return pl.pallas_call(
        attention_kernel,
        grid=(heads,),
        in_specs=[
            q_spec,
            kv_spec,
            kv_spec,
            q_spec,
            pl.BlockSpec((rows, 1), lambda g: (0, 0)),
            pl.BlockSpec((1, span), lambda g: (0, 0)),
        ],
        out_specs=[q_spec, q_spec, kv_spec, kv_spec],
        out_shape=[
            jax.ShapeDtypeStruct((rows, q_width), jnp.bfloat16),
            jax.ShapeDtypeStruct((rows, q_width), jnp.bfloat16),
            jax.ShapeDtypeStruct((span, kv_width), jnp.bfloat16),
            jax.ShapeDtypeStruct((span, kv_width), jnp.bfloat16),
        ],
        cost_estimate=pl.CostEstimate(
            flops=flops,
            transcendentals=rows * GROUP * span * heads,
            bytes_accessed=2 * (4 * rows * q_width + 4 * span * kv_width),
        ),
    )(queries, keys, values, grads, query_tags, key_tags)


def peer_gather_kernel(axis, n, x_ref, o_ref, send_sem, recv_sem, local_sem):
    me = lax.axis_index(axis)
    barrier = pltpu.get_barrier_semaphore()
    for k in range(1, n):
        pl.semaphore_signal(
            barrier, inc=1, device_id={axis: lax.rem(me + k, n)}, device_id_type=pl.DeviceIdType.MESH
        )
    pl.semaphore_wait(barrier, n - 1)
    local = pltpu.make_async_copy(x_ref, o_ref.at[me], local_sem)
    local.start()
    copies = []
    for k in range(1, n):
        copy = pltpu.make_async_remote_copy(
            src_ref=x_ref,
            dst_ref=o_ref.at[me],
            send_sem=send_sem.at[k],
            recv_sem=recv_sem.at[k],
            device_id={axis: lax.rem(me + k, n)},
            device_id_type=pl.DeviceIdType.MESH,
        )
        copy.start()
        copies.append(copy)
    for copy in copies:
        copy.wait()
    local.wait()


def peer_gather(x, axis, collective_id):
    n = lax.axis_size(axis)
    return pl.pallas_call(
        functools.partial(peer_gather_kernel, axis, n),
        out_shape=jax.ShapeDtypeStruct((n,) + x.shape, x.dtype),
        in_specs=[pl.BlockSpec(memory_space=pl.ANY)],
        out_specs=pl.BlockSpec(memory_space=pl.ANY),
        scratch_shapes=[
            pltpu.SemaphoreType.DMA((n,)),
            pltpu.SemaphoreType.DMA((n,)),
            pltpu.SemaphoreType.DMA,
        ],
        compiler_params=pltpu.CompilerParams(collective_id=collective_id, has_side_effects=True),
    )(x)


def peer_sum_kernel(axis, n, x_ref, o_ref, landed, send_sem, recv_sem, local_sem):
    me = lax.axis_index(axis)
    barrier = pltpu.get_barrier_semaphore()
    for k in range(1, n):
        pl.semaphore_signal(
            barrier, inc=1, device_id={axis: lax.rem(me + k, n)}, device_id_type=pl.DeviceIdType.MESH
        )
    pl.semaphore_wait(barrier, n - 1)
    local = pltpu.make_async_copy(x_ref.at[me], landed.at[0], local_sem)
    local.start()
    copies = []
    for k in range(1, n):
        peer = lax.rem(me + k, n)
        copy = pltpu.make_async_remote_copy(
            src_ref=x_ref.at[peer],
            dst_ref=landed.at[k],
            send_sem=send_sem.at[k],
            recv_sem=recv_sem.at[k],
            device_id={axis: peer},
            device_id_type=pl.DeviceIdType.MESH,
        )
        copy.start()
        copies.append(copy)
    local.wait()
    total = landed[0]
    for k in range(1, n):
        copies[k - 1].wait()
        total = total + landed[k]
    o_ref[...] = total


def peer_sum_scatter(x, axis, collective_id):
    n = lax.axis_size(axis)
    return pl.pallas_call(
        functools.partial(peer_sum_kernel, axis, n),
        out_shape=jax.ShapeDtypeStruct(x.shape[1:], x.dtype),
        in_specs=[pl.BlockSpec(memory_space=pl.ANY)],
        out_specs=pl.BlockSpec(memory_space=pltpu.VMEM),
        scratch_shapes=[
            pltpu.VMEM(x.shape, x.dtype),
            pltpu.SemaphoreType.DMA((n,)),
            pltpu.SemaphoreType.DMA((n,)),
            pltpu.SemaphoreType.DMA,
        ],
        compiler_params=pltpu.CompilerParams(collective_id=collective_id, has_side_effects=True),
    )(x)


def shifted(x, axis, by):
    length = lax.axis_size(axis)
    pairs = [(i, i + by) for i in range(length) if 0 <= i + by < length]
    return lax.ppermute(x, axis, pairs)


def shards(hidden, queries, key_heads, w_value, d_out, segments):
    shard_rows = hidden.shape[1]
    kv_width = w_value.shape[1]
    n_hops = WINDOW // shard_rows
    span_rows = (n_hops + 1) * shard_rows
    tokens_in = hidden[0]
    own_keys = key_heads[0]
    own_segments = segments[0]
    n_fsdp = lax.axis_size("fsdp")
    n_ctx = lax.axis_size("ctx")
    model_width = tokens_in.shape[1]
    half_rows = w_value.shape[0] // 2
    core = lax.axis_index("ctx") % 2
    w_mine = peer_gather(lax.dynamic_slice_in_dim(w_value, core * half_rows, half_rows, 0), "fsdp", 1)
    w_other = lax.ppermute(w_mine, "ctx", [(i, i ^ 1) for i in range(n_ctx)])
    token_halves = tokens_in.reshape(shard_rows, n_fsdp, 2, half_rows)
    tokens_mine = lax.dynamic_index_in_dim(token_halves, core, axis=2, keepdims=False)
    tokens_other = lax.dynamic_index_in_dim(token_halves, 1 - core, axis=2, keepdims=False)
    values = (
        jnp.einsum("tfr,frn->tn", tokens_mine, w_mine, preferred_element_type=jnp.float32)
        + jnp.einsum("tfr,frn->tn", tokens_other, w_other, preferred_element_type=jnp.float32)
    ).astype(jnp.bfloat16)
    out_rows = model_width // (n_ctx * n_fsdp)
    token_cols = (
        tokens_in.reshape(shard_rows, n_ctx, n_fsdp, out_rows).transpose(2, 0, 1, 3)
    )
    token_cols = lax.all_to_all(token_cols, "fsdp", 0, 0, tiled=True)
    segment_tags = own_segments.astype(jnp.bfloat16)
    arrived = []
    for hop_index in range(1, n_hops + 1):
        arrived.append(shifted((own_keys, values, segment_tags), "ctx", hop_index))
    ordered = arrived[::-1] + [(own_keys, values, segment_tags)]
    window_keys = jnp.concatenate([parcel[0] for parcel in ordered], 0)
    window_values = jnp.concatenate([parcel[1] for parcel in ordered], 0)
    window_tags = jnp.concatenate([parcel[2] for parcel in ordered], 0).astype(jnp.int32)
    first_query = lax.axis_index("ctx") * shard_rows
    key_pos = first_query - WINDOW + jnp.arange(span_rows, dtype=jnp.int32)
    key_tags = jnp.where(key_pos >= 0, window_tags, -1)
    out_rows_attn, d_query_heads, key_terms, value_terms = fused_attention(
        queries[0],
        window_keys,
        window_values,
        d_out[0],
        own_segments.astype(jnp.int32)[:, None],
        key_tags[None, :],
    )
    own_start = n_hops * shard_rows
    key_total = key_terms[own_start:].astype(jnp.float32)
    value_total = value_terms[own_start:].astype(jnp.float32)
    for hop_index in range(1, n_hops + 1):
        low_edge = (n_hops - hop_index) * shard_rows
        back_keys, back_values = shifted(
            (
                key_terms[low_edge : low_edge + shard_rows],
                value_terms[low_edge : low_edge + shard_rows],
            ),
            "ctx",
            -hop_index,
        )
        key_total = key_total + back_keys.astype(jnp.float32)
        value_total = value_total + back_values.astype(jnp.float32)
    d_key_rows = key_total.astype(jnp.bfloat16)
    d_values_low = value_total.astype(jnp.bfloat16)
    d_mine = jnp.einsum("tn,frn->tfr", d_values_low, w_mine, preferred_element_type=jnp.float32).astype(jnp.bfloat16)
    d_other = jnp.einsum("tn,frn->tfr", d_values_low, w_other, preferred_element_type=jnp.float32).astype(jnp.bfloat16)
    d_tokens = jnp.where(
        core == 0, jnp.stack([d_mine, d_other], 2), jnp.stack([d_other, d_mine], 2)
    ).reshape(shard_rows, model_width)
    grads_all = peer_gather(d_values_low, "fsdp", 2)
    token_cols, grads_all, d_query_heads, d_tokens = lax.optimization_barrier(
        (token_cols, grads_all, d_query_heads, d_tokens)
    )
    weight_part = jnp.einsum(
        "ftcr,ftn->crn", token_cols, grads_all, preferred_element_type=jnp.float32
    )
    d_weight = peer_sum_scatter(weight_part, "ctx", 3)
    return (
        out_rows_attn[None],
        d_query_heads[None],
        d_key_rows[None],
        d_tokens[None],
        d_weight,
    )


def solution(mesh):
    in_specs = (
        P("fsdp", "ctx", None),
        P("fsdp", "ctx", None),
        P("fsdp", "ctx", None),
        P("fsdp", None),
        P("fsdp", "ctx", None),
        P("fsdp", "ctx"),
    )
    out_specs = (
        P("fsdp", "ctx", None),
        P("fsdp", "ctx", None),
        P("fsdp", "ctx", None),
        P("fsdp", "ctx", None),
        P(("ctx", "fsdp"), None),
    )
    return jax.shard_map(shards, mesh=mesh, in_specs=in_specs, out_specs=out_specs, check_vma=False)
```

```python
import functools
import math

import jax
import jax.numpy as jnp
from jax import lax
from jax.experimental import pallas as pl
from jax.experimental.pallas import tpu as pltpu
from jax.sharding import PartitionSpec as P

HQ = 16
HK = 8
HD = 128
WINDOW = 1024
GROUP = 2


score_scale = 1.0 / math.sqrt(168.0)


def window_probs(q, keys, qtag_ref, ktag_ref):
    rows = qtag_ref.shape[0]
    span = keys.shape[0]
    reach = span - rows
    t_idx = lax.broadcasted_iota(jnp.int32, (rows, span), 0)
    l_idx = lax.broadcasted_iota(jnp.int32, (rows, span), 1)
    allowed = (qtag_ref[...] == ktag_ref[...]) & (l_idx > t_idx) & (l_idx <= t_idx + reach)
    allowed = jnp.concatenate([allowed] * GROUP, axis=0)
    scores = lax.dot_general(q, keys, (((1,), (1,)), ((), ())), preferred_element_type=jnp.float32) * score_scale
    scores = jnp.where(allowed, scores, -jnp.inf)
    highest = jnp.max(scores, axis=-1, keepdims=True)
    raw = jnp.exp(scores - highest)
    return raw / jnp.sum(raw, axis=-1, keepdims=True)


def stacked_heads(ref):
    return jnp.concatenate([ref[:, r * HD:(r + 1) * HD] for r in range(GROUP)], axis=0)


def value_grad_kernel(q_ref, k_ref, do_ref, qtag_ref, ktag_ref, dv_ref):
    probs_low = window_probs(stacked_heads(q_ref), k_ref[...], qtag_ref, ktag_ref).astype(jnp.bfloat16)
    grad = stacked_heads(do_ref)
    dv = lax.dot_general(probs_low, grad, (((0,), (0,)), ((), ())), preferred_element_type=jnp.float32)
    dv_ref[...] = dv.astype(jnp.bfloat16)


def attention_kernel(q_ref, k_ref, v_ref, do_ref, qtag_ref, ktag_ref, out_ref, dq_ref, dk_ref):
    rows = q_ref.shape[0]
    q = stacked_heads(q_ref)
    grad = stacked_heads(do_ref)
    keys = k_ref[...]
    vals = v_ref[...]
    probs = window_probs(q, keys, qtag_ref, ktag_ref)
    probs_low = probs.astype(jnp.bfloat16)
    out = jnp.dot(probs_low, vals, preferred_element_type=jnp.float32).astype(jnp.bfloat16)
    grad_probs = lax.dot_general(grad, vals, (((1,), (1,)), ((), ())), preferred_element_type=jnp.float32)
    delta = jnp.sum(grad.astype(jnp.float32) * out.astype(jnp.float32), axis=-1, keepdims=True)
    grad_scores = (probs * (grad_probs - delta)).astype(jnp.bfloat16)
    dq = (score_scale * jnp.dot(grad_scores, keys, preferred_element_type=jnp.float32)).astype(jnp.bfloat16)
    dk = score_scale * lax.dot_general(grad_scores, q, (((0,), (0,)), ((), ())), preferred_element_type=jnp.float32)
    for r in range(GROUP):
        out_ref[:, r * HD:(r + 1) * HD] = out[r * rows:(r + 1) * rows]
        dq_ref[:, r * HD:(r + 1) * HD] = dq[r * rows:(r + 1) * rows]
    dk_ref[...] = dk.astype(jnp.bfloat16)


def head_specs(rows, span):
    q_spec = pl.BlockSpec((rows, GROUP * HD), lambda g: (0, g))
    kv_spec = pl.BlockSpec((span, HD), lambda g: (0, g))
    tag_specs = [pl.BlockSpec((rows, 1), lambda g: (0, 0)), pl.BlockSpec((1, span), lambda g: (0, 0))]
    return q_spec, kv_spec, tag_specs


def value_grads(queries, keys, grads, query_tags, key_tags):
    rows, q_width = queries.shape
    span, kv_width = keys.shape
    heads = kv_width // HD
    q_spec, kv_spec, tag_specs = head_specs(rows, span)
    return pl.pallas_call(
        value_grad_kernel,
        grid=(heads,),
        in_specs=[q_spec, kv_spec, q_spec] + tag_specs,
        out_specs=kv_spec,
        out_shape=jax.ShapeDtypeStruct((span, kv_width), jnp.bfloat16),
        cost_estimate=pl.CostEstimate(
            flops=4 * rows * GROUP * span * HD * heads,
            transcendentals=rows * GROUP * span * heads,
            bytes_accessed=2 * (2 * rows * q_width + 2 * span * kv_width),
        ),
    )(queries, keys, grads, query_tags, key_tags)


def fused_attention(queries, keys, values, grads, query_tags, key_tags):
    rows, q_width = queries.shape
    span, kv_width = keys.shape
    heads = kv_width // HD
    q_spec, kv_spec, tag_specs = head_specs(rows, span)
    return pl.pallas_call(
        attention_kernel,
        grid=(heads,),
        in_specs=[q_spec, kv_spec, kv_spec, q_spec] + tag_specs,
        out_specs=[q_spec, q_spec, kv_spec],
        out_shape=[
            jax.ShapeDtypeStruct((rows, q_width), jnp.bfloat16),
            jax.ShapeDtypeStruct((rows, q_width), jnp.bfloat16),
            jax.ShapeDtypeStruct((span, kv_width), jnp.bfloat16),
        ],
        cost_estimate=pl.CostEstimate(
            flops=10 * rows * GROUP * span * HD * heads,
            transcendentals=rows * GROUP * span * heads,
            bytes_accessed=2 * (4 * rows * q_width + 3 * span * kv_width),
        ),
    )(queries, keys, values, grads, query_tags, key_tags)


def peer_gather_kernel(axis, n, x_ref, o_ref, send_sem, recv_sem, local_sem):
    me = lax.axis_index(axis)
    barrier = pltpu.get_barrier_semaphore()
    for k in range(1, n):
        pl.semaphore_signal(
            barrier, inc=1, device_id={axis: lax.rem(me + k, n)}, device_id_type=pl.DeviceIdType.MESH
        )
    pl.semaphore_wait(barrier, n - 1)
    local = pltpu.make_async_copy(x_ref, o_ref.at[me], local_sem)
    local.start()
    copies = []
    for k in range(1, n):
        copy = pltpu.make_async_remote_copy(
            src_ref=x_ref,
            dst_ref=o_ref.at[me],
            send_sem=send_sem.at[k],
            recv_sem=recv_sem.at[k],
            device_id={axis: lax.rem(me + k, n)},
            device_id_type=pl.DeviceIdType.MESH,
        )
        copy.start()
        copies.append(copy)
    for copy in copies:
        copy.wait()
    local.wait()


def peer_gather(x, axis, collective_id):
    n = lax.axis_size(axis)
    return pl.pallas_call(
        functools.partial(peer_gather_kernel, axis, n),
        out_shape=jax.ShapeDtypeStruct((n,) + x.shape, x.dtype),
        in_specs=[pl.BlockSpec(memory_space=pl.ANY)],
        out_specs=pl.BlockSpec(memory_space=pl.ANY),
        scratch_shapes=[
            pltpu.SemaphoreType.DMA((n,)),
            pltpu.SemaphoreType.DMA((n,)),
            pltpu.SemaphoreType.DMA,
        ],
        compiler_params=pltpu.CompilerParams(collective_id=collective_id, has_side_effects=True),
    )(x)


def peer_sum_kernel(axis, n, x_ref, o_ref, landed, send_sem, recv_sem, local_sem):
    me = lax.axis_index(axis)
    barrier = pltpu.get_barrier_semaphore()
    for k in range(1, n):
        pl.semaphore_signal(
            barrier, inc=1, device_id={axis: lax.rem(me + k, n)}, device_id_type=pl.DeviceIdType.MESH
        )
    pl.semaphore_wait(barrier, n - 1)
    local = pltpu.make_async_copy(x_ref.at[me], landed.at[0], local_sem)
    local.start()
    copies = []
    for k in range(1, n):
        peer = lax.rem(me + k, n)
        copy = pltpu.make_async_remote_copy(
            src_ref=x_ref.at[peer],
            dst_ref=landed.at[k],
            send_sem=send_sem.at[k],
            recv_sem=recv_sem.at[k],
            device_id={axis: peer},
            device_id_type=pl.DeviceIdType.MESH,
        )
        copy.start()
        copies.append(copy)
    local.wait()
    total = landed[0]
    for k in range(1, n):
        copies[k - 1].wait()
        total = total + landed[k]
    o_ref[...] = total


def peer_sum_scatter(x, axis, collective_id):
    n = lax.axis_size(axis)
    return pl.pallas_call(
        functools.partial(peer_sum_kernel, axis, n),
        out_shape=jax.ShapeDtypeStruct(x.shape[1:], x.dtype),
        in_specs=[pl.BlockSpec(memory_space=pl.ANY)],
        out_specs=pl.BlockSpec(memory_space=pltpu.VMEM),
        scratch_shapes=[
            pltpu.VMEM(x.shape, x.dtype),
            pltpu.SemaphoreType.DMA((n,)),
            pltpu.SemaphoreType.DMA((n,)),
            pltpu.SemaphoreType.DMA,
        ],
        compiler_params=pltpu.CompilerParams(collective_id=collective_id, has_side_effects=True),
    )(x)


def shifted(x, axis, by):
    length = lax.axis_size(axis)
    pairs = [(i, i + by) for i in range(length) if 0 <= i + by < length]
    return lax.ppermute(x, axis, pairs)


def shards(hidden, queries, key_heads, w_value, d_out, segments):
    shard_rows = hidden.shape[1]
    kv_width = w_value.shape[1]
    n_hops = WINDOW // shard_rows
    span_rows = (n_hops + 1) * shard_rows
    tokens_in = hidden[0]
    own_keys = key_heads[0]
    own_segments = segments[0]
    n_fsdp = lax.axis_size("fsdp")
    n_ctx = lax.axis_size("ctx")
    model_width = tokens_in.shape[1]
    half_rows = w_value.shape[0] // 2
    core = lax.axis_index("ctx") % 2
    w_mine = lax.all_gather(
        lax.dynamic_slice_in_dim(w_value, core * half_rows, half_rows, 0), "fsdp", axis=0, tiled=False
    )
    token_halves = tokens_in.reshape(shard_rows, n_fsdp, 2, half_rows)
    tokens_mine = lax.dynamic_index_in_dim(token_halves, core, axis=2, keepdims=False)
    tokens_other = lax.dynamic_index_in_dim(token_halves, 1 - core, axis=2, keepdims=False)
    out_rows = model_width // (n_ctx * n_fsdp)
    token_cols = (
        tokens_in.reshape(shard_rows, n_ctx, n_fsdp, out_rows).transpose(2, 0, 1, 3)
    )
    token_cols = lax.all_to_all(token_cols, "fsdp", 0, 0, tiled=True)
    segment_tags = own_segments.astype(jnp.bfloat16)
    arrived = [shifted((own_keys, segment_tags), "ctx", hop) for hop in range(1, n_hops + 1)]
    ordered = arrived[::-1] + [(own_keys, segment_tags)]
    window_keys = jnp.concatenate([parcel[0] for parcel in ordered], 0)
    window_tags = jnp.concatenate([parcel[1] for parcel in ordered], 0).astype(jnp.int32)
    first_query = lax.axis_index("ctx") * shard_rows
    key_pos = first_query - WINDOW + jnp.arange(span_rows, dtype=jnp.int32)
    key_tags = jnp.where(key_pos >= 0, window_tags, -1)
    query_tags = own_segments.astype(jnp.int32)[:, None]
    own_start = n_hops * shard_rows

    def returned_sum(terms):
        total = terms[own_start:].astype(jnp.float32)
        for hop in range(1, n_hops + 1):
            low_edge = (n_hops - hop) * shard_rows
            total = total + shifted(terms[low_edge : low_edge + shard_rows], "ctx", -hop).astype(jnp.float32)
        return total.astype(jnp.bfloat16)

    value_terms = value_grads(queries[0], window_keys, d_out[0], query_tags, key_tags[None, :])
    w_mine, value_terms = lax.optimization_barrier((w_mine, value_terms))
    w_other = lax.ppermute(w_mine, "ctx", [(i, i ^ 1) for i in range(n_ctx)])
    d_values_low = returned_sum(value_terms)
    grads_all = peer_gather(d_values_low, "fsdp", 2)
    weight_part = jnp.einsum(
        "ftcr,ftn->crn", token_cols, grads_all, preferred_element_type=jnp.float32
    )
    d_weight = peer_sum_scatter(weight_part, "ctx", 3)

    values = (
        jnp.einsum("tfr,frn->tn", tokens_mine, w_mine, preferred_element_type=jnp.float32)
        + jnp.einsum("tfr,frn->tn", tokens_other, w_other, preferred_element_type=jnp.float32)
    ).astype(jnp.bfloat16)
    arrived_values = [shifted(values, "ctx", hop) for hop in range(1, n_hops + 1)]
    window_values = jnp.concatenate(arrived_values[::-1] + [values], 0)
    out_rows_attn, d_query_heads, key_terms = fused_attention(
        queries[0], window_keys, window_values, d_out[0], query_tags, key_tags[None, :]
    )
    d_key_rows = returned_sum(key_terms)
    d_mine = jnp.einsum("tn,frn->tfr", d_values_low, w_mine, preferred_element_type=jnp.float32).astype(jnp.bfloat16)
    d_other = jnp.einsum("tn,frn->tfr", d_values_low, w_other, preferred_element_type=jnp.float32).astype(jnp.bfloat16)
    d_tokens = jnp.where(
        core == 0, jnp.stack([d_mine, d_other], 2), jnp.stack([d_other, d_mine], 2)
    ).reshape(shard_rows, model_width)
    return (
        out_rows_attn[None],
        d_query_heads[None],
        d_key_rows[None],
        d_tokens[None],
        d_weight,
    )


def solution(mesh):
    in_specs = (
        P("fsdp", "ctx", None),
        P("fsdp", "ctx", None),
        P("fsdp", "ctx", None),
        P("fsdp", None),
        P("fsdp", "ctx", None),
        P("fsdp", "ctx"),
    )
    out_specs = (
        P("fsdp", "ctx", None),
        P("fsdp", "ctx", None),
        P("fsdp", "ctx", None),
        P("fsdp", "ctx", None),
        P(("ctx", "fsdp"), None),
    )
    return jax.shard_map(shards, mesh=mesh, in_specs=in_specs, out_specs=out_specs, check_vma=False)
```

```python
import functools
import math

import jax
import jax.numpy as jnp
from jax import lax
from jax.experimental import pallas as pl
from jax.experimental.pallas import tpu as pltpu
from jax.sharding import PartitionSpec as P

HQ = 16
HK = 8
HD = 128
WINDOW = 1024
GROUP = 2


score_scale = 1.0 / math.sqrt(168.0)


def window_probs(q, keys, qtag_ref, ktag_ref):
    rows = qtag_ref.shape[0]
    span = keys.shape[0]
    reach = span - rows
    t_idx = lax.broadcasted_iota(jnp.int32, (rows, span), 0)
    l_idx = lax.broadcasted_iota(jnp.int32, (rows, span), 1)
    allowed = (qtag_ref[...] == ktag_ref[...]) & (l_idx > t_idx) & (l_idx <= t_idx + reach)
    allowed = jnp.concatenate([allowed] * GROUP, axis=0)
    scores = lax.dot_general(q, keys, (((1,), (1,)), ((), ())), preferred_element_type=jnp.float32) * score_scale
    scores = jnp.where(allowed, scores, -jnp.inf)
    highest = jnp.max(scores, axis=-1, keepdims=True)
    raw = jnp.exp(scores - highest)
    return raw / jnp.sum(raw, axis=-1, keepdims=True)


def stacked_heads(ref):
    return jnp.concatenate([ref[:, r * HD:(r + 1) * HD] for r in range(GROUP)], axis=0)


def value_grad_kernel(q_ref, k_ref, do_ref, qtag_ref, ktag_ref, dv_ref):
    probs_low = window_probs(stacked_heads(q_ref), k_ref[...], qtag_ref, ktag_ref).astype(jnp.bfloat16)
    grad = stacked_heads(do_ref)
    dv = lax.dot_general(probs_low, grad, (((0,), (0,)), ((), ())), preferred_element_type=jnp.float32)
    dv_ref[...] = dv.astype(jnp.bfloat16)


def attention_kernel(q_ref, k_ref, v_ref, do_ref, qtag_ref, ktag_ref, out_ref, dq_ref, dk_ref):
    rows = q_ref.shape[0]
    q = stacked_heads(q_ref)
    grad = stacked_heads(do_ref)
    keys = k_ref[...]
    vals = v_ref[...]
    probs = window_probs(q, keys, qtag_ref, ktag_ref)
    probs_low = probs.astype(jnp.bfloat16)
    out = jnp.dot(probs_low, vals, preferred_element_type=jnp.float32).astype(jnp.bfloat16)
    grad_probs = lax.dot_general(grad, vals, (((1,), (1,)), ((), ())), preferred_element_type=jnp.float32)
    delta = jnp.sum(grad.astype(jnp.float32) * out.astype(jnp.float32), axis=-1, keepdims=True)
    grad_scores = (probs * (grad_probs - delta)).astype(jnp.bfloat16)
    dq = (score_scale * jnp.dot(grad_scores, keys, preferred_element_type=jnp.float32)).astype(jnp.bfloat16)
    dk = score_scale * lax.dot_general(grad_scores, q, (((0,), (0,)), ((), ())), preferred_element_type=jnp.float32)
    for r in range(GROUP):
        out_ref[:, r * HD:(r + 1) * HD] = out[r * rows:(r + 1) * rows]
        dq_ref[:, r * HD:(r + 1) * HD] = dq[r * rows:(r + 1) * rows]
    dk_ref[...] = dk.astype(jnp.bfloat16)


def head_specs(rows, span):
    q_spec = pl.BlockSpec((rows, GROUP * HD), lambda g: (0, g))
    kv_spec = pl.BlockSpec((span, HD), lambda g: (0, g))
    tag_specs = [pl.BlockSpec((rows, 1), lambda g: (0, 0)), pl.BlockSpec((1, span), lambda g: (0, 0))]
    return q_spec, kv_spec, tag_specs


def value_grads(queries, keys, grads, query_tags, key_tags):
    rows, q_width = queries.shape
    span, kv_width = keys.shape
    heads = kv_width // HD
    q_spec, kv_spec, tag_specs = head_specs(rows, span)
    return pl.pallas_call(
        value_grad_kernel,
        grid=(heads,),
        in_specs=[q_spec, kv_spec, q_spec] + tag_specs,
        out_specs=kv_spec,
        out_shape=jax.ShapeDtypeStruct((span, kv_width), jnp.bfloat16),
        cost_estimate=pl.CostEstimate(
            flops=4 * rows * GROUP * span * HD * heads,
            transcendentals=rows * GROUP * span * heads,
            bytes_accessed=2 * (2 * rows * q_width + 2 * span * kv_width),
        ),
    )(queries, keys, grads, query_tags, key_tags)


def fused_attention(queries, keys, values, grads, query_tags, key_tags):
    rows, q_width = queries.shape
    span, kv_width = keys.shape
    heads = kv_width // HD
    q_spec, kv_spec, tag_specs = head_specs(rows, span)
    return pl.pallas_call(
        attention_kernel,
        grid=(heads,),
        in_specs=[q_spec, kv_spec, kv_spec, q_spec] + tag_specs,
        out_specs=[q_spec, q_spec, kv_spec],
        out_shape=[
            jax.ShapeDtypeStruct((rows, q_width), jnp.bfloat16),
            jax.ShapeDtypeStruct((rows, q_width), jnp.bfloat16),
            jax.ShapeDtypeStruct((span, kv_width), jnp.bfloat16),
        ],
        cost_estimate=pl.CostEstimate(
            flops=10 * rows * GROUP * span * HD * heads,
            transcendentals=rows * GROUP * span * heads,
            bytes_accessed=2 * (4 * rows * q_width + 3 * span * kv_width),
        ),
    )(queries, keys, values, grads, query_tags, key_tags)


def peer_gather_kernel(axis, n, x_ref, o_ref, send_sem, recv_sem, local_sem):
    me = lax.axis_index(axis)
    barrier = pltpu.get_barrier_semaphore()
    for k in range(1, n):
        pl.semaphore_signal(
            barrier, inc=1, device_id={axis: lax.rem(me + k, n)}, device_id_type=pl.DeviceIdType.MESH
        )
    pl.semaphore_wait(barrier, n - 1)
    local = pltpu.make_async_copy(x_ref, o_ref.at[me], local_sem)
    local.start()
    copies = []
    for k in range(1, n):
        copy = pltpu.make_async_remote_copy(
            src_ref=x_ref,
            dst_ref=o_ref.at[me],
            send_sem=send_sem.at[k],
            recv_sem=recv_sem.at[k],
            device_id={axis: lax.rem(me + k, n)},
            device_id_type=pl.DeviceIdType.MESH,
        )
        copy.start()
        copies.append(copy)
    for copy in copies:
        copy.wait()
    local.wait()


def peer_gather(x, axis, collective_id):
    n = lax.axis_size(axis)
    return pl.pallas_call(
        functools.partial(peer_gather_kernel, axis, n),
        out_shape=jax.ShapeDtypeStruct((n,) + x.shape, x.dtype),
        in_specs=[pl.BlockSpec(memory_space=pl.ANY)],
        out_specs=pl.BlockSpec(memory_space=pl.ANY),
        scratch_shapes=[
            pltpu.SemaphoreType.DMA((n,)),
            pltpu.SemaphoreType.DMA((n,)),
            pltpu.SemaphoreType.DMA,
        ],
        compiler_params=pltpu.CompilerParams(collective_id=collective_id, has_side_effects=True),
    )(x)


def peer_sum_kernel(axis, n, x_ref, o_ref, landed, send_sem, recv_sem, local_sem):
    me = lax.axis_index(axis)
    barrier = pltpu.get_barrier_semaphore()
    for k in range(1, n):
        pl.semaphore_signal(
            barrier, inc=1, device_id={axis: lax.rem(me + k, n)}, device_id_type=pl.DeviceIdType.MESH
        )
    pl.semaphore_wait(barrier, n - 1)
    local = pltpu.make_async_copy(x_ref.at[me], landed.at[0], local_sem)
    local.start()
    copies = []
    for k in range(1, n):
        peer = lax.rem(me + k, n)
        copy = pltpu.make_async_remote_copy(
            src_ref=x_ref.at[peer],
            dst_ref=landed.at[k],
            send_sem=send_sem.at[k],
            recv_sem=recv_sem.at[k],
            device_id={axis: peer},
            device_id_type=pl.DeviceIdType.MESH,
        )
        copy.start()
        copies.append(copy)
    local.wait()
    total = landed[0].astype(jnp.float32)
    for k in range(1, n):
        copies[k - 1].wait()
        total = total + landed[k].astype(jnp.float32)
    o_ref[...] = total


def peer_sum_scatter(x, axis, collective_id):
    n = lax.axis_size(axis)
    return pl.pallas_call(
        functools.partial(peer_sum_kernel, axis, n),
        out_shape=jax.ShapeDtypeStruct(x.shape[1:], jnp.float32),
        in_specs=[pl.BlockSpec(memory_space=pl.ANY)],
        out_specs=pl.BlockSpec(memory_space=pltpu.VMEM),
        scratch_shapes=[
            pltpu.VMEM(x.shape, x.dtype),
            pltpu.SemaphoreType.DMA((n,)),
            pltpu.SemaphoreType.DMA((n,)),
            pltpu.SemaphoreType.DMA,
        ],
        compiler_params=pltpu.CompilerParams(collective_id=collective_id, has_side_effects=True),
    )(x)


def shifted(x, axis, by):
    length = lax.axis_size(axis)
    pairs = [(i, i + by) for i in range(length) if 0 <= i + by < length]
    return lax.ppermute(x, axis, pairs)


def shards(hidden, queries, key_heads, w_value, d_out, segments):
    shard_rows = hidden.shape[1]
    kv_width = w_value.shape[1]
    n_hops = WINDOW // shard_rows
    span_rows = (n_hops + 1) * shard_rows
    tokens_in = hidden[0]
    own_keys = key_heads[0]
    own_segments = segments[0]
    n_fsdp = lax.axis_size("fsdp")
    n_ctx = lax.axis_size("ctx")
    model_width = tokens_in.shape[1]
    half_rows = w_value.shape[0] // 2
    core = lax.axis_index("ctx") % 2
    w_mine = lax.all_gather(
        lax.dynamic_slice_in_dim(w_value, core * half_rows, half_rows, 0), "fsdp", axis=0, tiled=False
    )
    token_halves = tokens_in.reshape(shard_rows, n_fsdp, 2, half_rows)
    tokens_mine = lax.dynamic_index_in_dim(token_halves, core, axis=2, keepdims=False)
    tokens_other = lax.dynamic_index_in_dim(token_halves, 1 - core, axis=2, keepdims=False)
    out_rows = model_width // (n_ctx * n_fsdp)
    token_cols = (
        tokens_in.reshape(shard_rows, n_ctx, n_fsdp, out_rows).transpose(2, 0, 1, 3)
    )
    token_cols = lax.all_to_all(token_cols, "fsdp", 0, 0, tiled=True)
    tag_columns = jnp.broadcast_to(own_segments.astype(jnp.bfloat16)[:, None], (shard_rows, HD))
    parcel = jnp.concatenate([own_keys, tag_columns], 1)
    arrived = [shifted(parcel, "ctx", hop) for hop in range(1, n_hops + 1)]
    window_parcel = jnp.concatenate(arrived[::-1] + [parcel], 0)
    window_keys = window_parcel[:, :kv_width]
    window_tags = window_parcel[:, kv_width].astype(jnp.int32)
    first_query = lax.axis_index("ctx") * shard_rows
    key_pos = first_query - WINDOW + jnp.arange(span_rows, dtype=jnp.int32)
    key_tags = jnp.where(key_pos >= 0, window_tags, -1)
    query_tags = own_segments.astype(jnp.int32)[:, None]
    own_start = n_hops * shard_rows

    def returned_sum(terms):
        total = terms[own_start:].astype(jnp.float32)
        for hop in range(1, n_hops + 1):
            low_edge = (n_hops - hop) * shard_rows
            total = total + shifted(terms[low_edge : low_edge + shard_rows], "ctx", -hop).astype(jnp.float32)
        return total.astype(jnp.bfloat16)

    value_terms = value_grads(queries[0], window_keys, d_out[0], query_tags, key_tags[None, :])
    w_mine, value_terms = lax.optimization_barrier((w_mine, value_terms))
    w_other = lax.ppermute(w_mine, "ctx", [(i, i ^ 1) for i in range(n_ctx)])
    d_values_low = returned_sum(value_terms)
    grads_all = peer_gather(d_values_low, "fsdp", 2)
    weight_part = jnp.einsum(
        "ftcr,ftn->crn", token_cols, grads_all, preferred_element_type=jnp.float32
    )
    d_weight = peer_sum_scatter(weight_part.astype(jnp.bfloat16), "ctx", 3)

    values = (
        jnp.einsum("tfr,frn->tn", tokens_mine, w_mine, preferred_element_type=jnp.float32)
        + jnp.einsum("tfr,frn->tn", tokens_other, w_other, preferred_element_type=jnp.float32)
    ).astype(jnp.bfloat16)
    arrived_values = [shifted(values, "ctx", hop) for hop in range(1, n_hops + 1)]
    window_values = jnp.concatenate(arrived_values[::-1] + [values], 0)
    out_rows_attn, d_query_heads, key_terms = fused_attention(
        queries[0], window_keys, window_values, d_out[0], query_tags, key_tags[None, :]
    )
    d_key_rows = returned_sum(key_terms)
    d_mine = jnp.einsum("tn,frn->tfr", d_values_low, w_mine, preferred_element_type=jnp.float32).astype(jnp.bfloat16)
    d_other = jnp.einsum("tn,frn->tfr", d_values_low, w_other, preferred_element_type=jnp.float32).astype(jnp.bfloat16)
    d_tokens = jnp.where(
        core == 0, jnp.stack([d_mine, d_other], 2), jnp.stack([d_other, d_mine], 2)
    ).reshape(shard_rows, model_width)
    return (
        out_rows_attn[None],
        d_query_heads[None],
        d_key_rows[None],
        d_tokens[None],
        d_weight,
    )


def solution(mesh):
    in_specs = (
        P("fsdp", "ctx", None),
        P("fsdp", "ctx", None),
        P("fsdp", "ctx", None),
        P("fsdp", None),
        P("fsdp", "ctx", None),
        P("fsdp", "ctx"),
    )
    out_specs = (
        P("fsdp", "ctx", None),
        P("fsdp", "ctx", None),
        P("fsdp", "ctx", None),
        P("fsdp", "ctx", None),
        P(("ctx", "fsdp"), None),
    )
    return jax.shard_map(shards, mesh=mesh, in_specs=in_specs, out_specs=out_specs, check_vma=False)
```

```python
import functools
import math

import jax
import jax.numpy as jnp
from jax import lax
from jax.experimental import pallas as pl
from jax.experimental.pallas import tpu as pltpu
from jax.sharding import PartitionSpec as P

HQ = 16
HK = 8
HD = 128
WINDOW = 1024
GROUP = 2


score_scale = 1.0 / math.sqrt(168.0)


def window_probs(q, keys, qtag_ref, ktag_ref):
    rows = qtag_ref.shape[0]
    span = keys.shape[0]
    reach = span - rows
    t_idx = lax.broadcasted_iota(jnp.int32, (rows, span), 0)
    l_idx = lax.broadcasted_iota(jnp.int32, (rows, span), 1)
    allowed = (qtag_ref[...] == ktag_ref[...]) & (l_idx > t_idx) & (l_idx <= t_idx + reach)
    allowed = jnp.concatenate([allowed] * GROUP, axis=0)
    scores = lax.dot_general(q, keys, (((1,), (1,)), ((), ())), preferred_element_type=jnp.float32) * score_scale
    scores = jnp.where(allowed, scores, -jnp.inf)
    highest = jnp.max(scores, axis=-1, keepdims=True)
    raw = jnp.exp(scores - highest)
    return raw / jnp.sum(raw, axis=-1, keepdims=True)


def stacked_heads(ref):
    return jnp.concatenate([ref[:, r * HD:(r + 1) * HD] for r in range(GROUP)], axis=0)


def value_grad_kernel(q_ref, k_ref, do_ref, qtag_ref, ktag_ref, dv_ref):
    probs_low = window_probs(stacked_heads(q_ref), k_ref[...], qtag_ref, ktag_ref).astype(jnp.bfloat16)
    grad = stacked_heads(do_ref)
    dv = lax.dot_general(probs_low, grad, (((0,), (0,)), ((), ())), preferred_element_type=jnp.float32)
    dv_ref[...] = dv.astype(jnp.bfloat16)


def attention_kernel(q_ref, k_ref, v_ref, do_ref, qtag_ref, ktag_ref, out_ref, dq_ref, dk_ref):
    rows = q_ref.shape[0]
    q = stacked_heads(q_ref)
    grad = stacked_heads(do_ref)
    keys = k_ref[...]
    vals = v_ref[...]
    probs = window_probs(q, keys, qtag_ref, ktag_ref)
    probs_low = probs.astype(jnp.bfloat16)
    out = jnp.dot(probs_low, vals, preferred_element_type=jnp.float32).astype(jnp.bfloat16)
    grad_probs = lax.dot_general(grad, vals, (((1,), (1,)), ((), ())), preferred_element_type=jnp.float32)
    delta = jnp.sum(grad.astype(jnp.float32) * out.astype(jnp.float32), axis=-1, keepdims=True)
    grad_scores = (probs * (grad_probs - delta)).astype(jnp.bfloat16)
    dq = (score_scale * jnp.dot(grad_scores, keys, preferred_element_type=jnp.float32)).astype(jnp.bfloat16)
    dk = score_scale * lax.dot_general(grad_scores, q, (((0,), (0,)), ((), ())), preferred_element_type=jnp.float32)
    for r in range(GROUP):
        out_ref[:, r * HD:(r + 1) * HD] = out[r * rows:(r + 1) * rows]
        dq_ref[:, r * HD:(r + 1) * HD] = dq[r * rows:(r + 1) * rows]
    dk_ref[...] = dk.astype(jnp.bfloat16)


def head_specs(rows, span):
    q_spec = pl.BlockSpec((rows, GROUP * HD), lambda g: (0, g))
    kv_spec = pl.BlockSpec((span, HD), lambda g: (0, g))
    tag_specs = [pl.BlockSpec((rows, 1), lambda g: (0, 0)), pl.BlockSpec((1, span), lambda g: (0, 0))]
    return q_spec, kv_spec, tag_specs


def value_grads(queries, keys, grads, query_tags, key_tags):
    rows, q_width = queries.shape
    span, kv_width = keys.shape
    heads = kv_width // HD
    q_spec, kv_spec, tag_specs = head_specs(rows, span)
    return pl.pallas_call(
        value_grad_kernel,
        grid=(heads,),
        in_specs=[q_spec, kv_spec, q_spec] + tag_specs,
        out_specs=kv_spec,
        out_shape=jax.ShapeDtypeStruct((span, kv_width), jnp.bfloat16),
        cost_estimate=pl.CostEstimate(
            flops=4 * rows * GROUP * span * HD * heads,
            transcendentals=rows * GROUP * span * heads,
            bytes_accessed=2 * (2 * rows * q_width + 2 * span * kv_width),
        ),
    )(queries, keys, grads, query_tags, key_tags)


def fused_attention(queries, keys, values, grads, query_tags, key_tags):
    rows, q_width = queries.shape
    span, kv_width = keys.shape
    heads = kv_width // HD
    q_spec, kv_spec, tag_specs = head_specs(rows, span)
    return pl.pallas_call(
        attention_kernel,
        grid=(heads,),
        in_specs=[q_spec, kv_spec, kv_spec, q_spec] + tag_specs,
        out_specs=[q_spec, q_spec, kv_spec],
        out_shape=[
            jax.ShapeDtypeStruct((rows, q_width), jnp.bfloat16),
            jax.ShapeDtypeStruct((rows, q_width), jnp.bfloat16),
            jax.ShapeDtypeStruct((span, kv_width), jnp.bfloat16),
        ],
        cost_estimate=pl.CostEstimate(
            flops=10 * rows * GROUP * span * HD * heads,
            transcendentals=rows * GROUP * span * heads,
            bytes_accessed=2 * (4 * rows * q_width + 3 * span * kv_width),
        ),
    )(queries, keys, values, grads, query_tags, key_tags)


def peer_gather_kernel(axis, n, x_ref, o_ref, send_sem, recv_sem, local_sem):
    me = lax.axis_index(axis)
    barrier = pltpu.get_barrier_semaphore()
    for k in range(1, n):
        pl.semaphore_signal(
            barrier, inc=1, device_id={axis: lax.rem(me + k, n)}, device_id_type=pl.DeviceIdType.MESH
        )
    pl.semaphore_wait(barrier, n - 1)
    local = pltpu.make_async_copy(x_ref, o_ref.at[me], local_sem)
    local.start()
    copies = []
    for k in range(1, n):
        copy = pltpu.make_async_remote_copy(
            src_ref=x_ref,
            dst_ref=o_ref.at[me],
            send_sem=send_sem.at[k],
            recv_sem=recv_sem.at[k],
            device_id={axis: lax.rem(me + k, n)},
            device_id_type=pl.DeviceIdType.MESH,
        )
        copy.start()
        copies.append(copy)
    for copy in copies:
        copy.wait()
    local.wait()


def peer_gather(x, axis, collective_id):
    n = lax.axis_size(axis)
    return pl.pallas_call(
        functools.partial(peer_gather_kernel, axis, n),
        out_shape=jax.ShapeDtypeStruct((n,) + x.shape, x.dtype),
        in_specs=[pl.BlockSpec(memory_space=pl.ANY)],
        out_specs=pl.BlockSpec(memory_space=pl.ANY),
        scratch_shapes=[
            pltpu.SemaphoreType.DMA((n,)),
            pltpu.SemaphoreType.DMA((n,)),
            pltpu.SemaphoreType.DMA,
        ],
        compiler_params=pltpu.CompilerParams(collective_id=collective_id, has_side_effects=True),
    )(x)


def peer_sum_kernel(axis, n, x_ref, o_ref, landed, send_sem, recv_sem, local_sem):
    me = lax.axis_index(axis)
    barrier = pltpu.get_barrier_semaphore()
    for k in range(1, n):
        pl.semaphore_signal(
            barrier, inc=1, device_id={axis: lax.rem(me + k, n)}, device_id_type=pl.DeviceIdType.MESH
        )
    pl.semaphore_wait(barrier, n - 1)
    local = pltpu.make_async_copy(x_ref.at[me], landed.at[0], local_sem)
    local.start()
    copies = []
    for k in range(1, n):
        peer = lax.rem(me + k, n)
        copy = pltpu.make_async_remote_copy(
            src_ref=x_ref.at[peer],
            dst_ref=landed.at[k],
            send_sem=send_sem.at[k],
            recv_sem=recv_sem.at[k],
            device_id={axis: peer},
            device_id_type=pl.DeviceIdType.MESH,
        )
        copy.start()
        copies.append(copy)
    local.wait()
    total = landed[0].astype(jnp.float32)
    for k in range(1, n):
        copies[k - 1].wait()
        total = total + landed[k].astype(jnp.float32)
    o_ref[...] = total


def peer_sum_scatter(x, axis, collective_id):
    n = lax.axis_size(axis)
    return pl.pallas_call(
        functools.partial(peer_sum_kernel, axis, n),
        out_shape=jax.ShapeDtypeStruct(x.shape[1:], jnp.float32),
        in_specs=[pl.BlockSpec(memory_space=pl.ANY)],
        out_specs=pl.BlockSpec(memory_space=pltpu.VMEM),
        scratch_shapes=[
            pltpu.VMEM(x.shape, x.dtype),
            pltpu.SemaphoreType.DMA((n,)),
            pltpu.SemaphoreType.DMA((n,)),
            pltpu.SemaphoreType.DMA,
        ],
        compiler_params=pltpu.CompilerParams(collective_id=collective_id, has_side_effects=True),
    )(x)


def shifted(x, axis, by):
    length = lax.axis_size(axis)
    pairs = [(i, i + by) for i in range(length) if 0 <= i + by < length]
    return lax.ppermute(x, axis, pairs)


def shards(hidden, queries, key_heads, w_value, d_out, segments):
    shard_rows = hidden.shape[1]
    kv_width = w_value.shape[1]
    n_hops = WINDOW // shard_rows
    span_rows = (n_hops + 1) * shard_rows
    tokens_in = hidden[0]
    own_keys = key_heads[0]
    own_segments = segments[0]
    n_fsdp = lax.axis_size("fsdp")
    n_ctx = lax.axis_size("ctx")
    model_width = tokens_in.shape[1]
    half_rows = w_value.shape[0] // 2
    core = lax.axis_index("ctx") % 2
    w_mine = lax.all_gather(
        lax.dynamic_slice_in_dim(w_value, core * half_rows, half_rows, 0), "fsdp", axis=0, tiled=False
    )
    token_halves = tokens_in.reshape(shard_rows, n_fsdp, 2, half_rows)
    tokens_mine = lax.dynamic_index_in_dim(token_halves, core, axis=2, keepdims=False)
    tokens_other = lax.dynamic_index_in_dim(token_halves, 1 - core, axis=2, keepdims=False)
    out_rows = model_width // (n_ctx * n_fsdp)
    token_cols = (
        tokens_in.reshape(shard_rows, n_ctx, n_fsdp, out_rows).transpose(2, 0, 1, 3)
    )
    token_cols = lax.all_to_all(token_cols, "fsdp", 0, 0, tiled=True)
    tag_columns = jnp.broadcast_to(own_segments.astype(jnp.bfloat16)[:, None], (shard_rows, HD))
    parcel = jnp.concatenate([own_keys, tag_columns], 1)
    arrived = [shifted(parcel, "ctx", hop) for hop in range(1, n_hops + 1)]
    window_parcel = jnp.concatenate(arrived[::-1] + [parcel], 0)
    window_keys = window_parcel[:, :kv_width]
    window_tags = window_parcel[:, kv_width].astype(jnp.int32)
    first_query = lax.axis_index("ctx") * shard_rows
    key_pos = first_query - WINDOW + jnp.arange(span_rows, dtype=jnp.int32)
    key_tags = jnp.where(key_pos >= 0, window_tags, -1)
    query_tags = own_segments.astype(jnp.int32)[:, None]
    own_start = n_hops * shard_rows

    def returned_sum(terms):
        total = terms[own_start:].astype(jnp.float32)
        for hop in range(1, n_hops + 1):
            low_edge = (n_hops - hop) * shard_rows
            total = total + shifted(terms[low_edge : low_edge + shard_rows], "ctx", -hop).astype(jnp.float32)
        return total.astype(jnp.bfloat16)

    value_terms = value_grads(queries[0], window_keys, d_out[0], query_tags, key_tags[None, :])
    d_values_low = returned_sum(value_terms)
    w_mine, _ = lax.optimization_barrier((w_mine, d_values_low))
    w_other = lax.ppermute(w_mine, "ctx", [(i, i ^ 1) for i in range(n_ctx)])
    grads_all = peer_gather(d_values_low, "fsdp", 2)
    weight_part = jnp.einsum(
        "ftcr,ftn->crn", token_cols, grads_all, preferred_element_type=jnp.float32
    )
    d_weight = peer_sum_scatter(weight_part.astype(jnp.bfloat16), "ctx", 3)

    values = (
        jnp.einsum("tfr,frn->tn", tokens_mine, w_mine, preferred_element_type=jnp.float32)
        + jnp.einsum("tfr,frn->tn", tokens_other, w_other, preferred_element_type=jnp.float32)
    ).astype(jnp.bfloat16)
    arrived_values = [shifted(values, "ctx", hop) for hop in range(1, n_hops + 1)]
    window_values = jnp.concatenate(arrived_values[::-1] + [values], 0)
    out_rows_attn, d_query_heads, key_terms = fused_attention(
        queries[0], window_keys, window_values, d_out[0], query_tags, key_tags[None, :]
    )
    d_key_rows = returned_sum(key_terms)
    d_mine = jnp.einsum("tn,frn->tfr", d_values_low, w_mine, preferred_element_type=jnp.float32).astype(jnp.bfloat16)
    d_other = jnp.einsum("tn,frn->tfr", d_values_low, w_other, preferred_element_type=jnp.float32).astype(jnp.bfloat16)
    d_tokens = jnp.where(
        core == 0, jnp.stack([d_mine, d_other], 2), jnp.stack([d_other, d_mine], 2)
    ).reshape(shard_rows, model_width)
    return (
        out_rows_attn[None],
        d_query_heads[None],
        d_key_rows[None],
        d_tokens[None],
        d_weight,
    )


def solution(mesh):
    in_specs = (
        P("fsdp", "ctx", None),
        P("fsdp", "ctx", None),
        P("fsdp", "ctx", None),
        P("fsdp", None),
        P("fsdp", "ctx", None),
        P("fsdp", "ctx"),
    )
    out_specs = (
        P("fsdp", "ctx", None),
        P("fsdp", "ctx", None),
        P("fsdp", "ctx", None),
        P("fsdp", "ctx", None),
        P(("ctx", "fsdp"), None),
    )
    return jax.shard_map(shards, mesh=mesh, in_specs=in_specs, out_specs=out_specs, check_vma=False)
```

```python
import functools
import math

import jax
import jax.numpy as jnp
from jax import lax
from jax.experimental import pallas as pl
from jax.experimental.pallas import tpu as pltpu
from jax.sharding import PartitionSpec as P

HQ = 16
HK = 8
HD = 128
WINDOW = 1024
GROUP = 2


score_scale = 1.0 / math.sqrt(168.0)


def window_probs(q, keys, qtag_ref, ktag_ref):
    rows = qtag_ref.shape[0]
    span = keys.shape[0]
    reach = span - rows
    t_idx = lax.broadcasted_iota(jnp.int32, (rows, span), 0)
    l_idx = lax.broadcasted_iota(jnp.int32, (rows, span), 1)
    allowed = (qtag_ref[...] == ktag_ref[...]) & (l_idx > t_idx) & (l_idx <= t_idx + reach)
    allowed = jnp.concatenate([allowed] * GROUP, axis=0)
    scores = lax.dot_general(q, keys, (((1,), (1,)), ((), ())), preferred_element_type=jnp.float32) * score_scale
    scores = jnp.where(allowed, scores, -jnp.inf)
    highest = jnp.max(scores, axis=-1, keepdims=True)
    raw = jnp.exp(scores - highest)
    return raw / jnp.sum(raw, axis=-1, keepdims=True)


def stacked_heads(ref):
    return jnp.concatenate([ref[:, r * HD:(r + 1) * HD] for r in range(GROUP)], axis=0)


def value_grad_kernel(q_ref, k_ref, do_ref, qtag_ref, ktag_ref, dv_ref):
    probs_low = window_probs(stacked_heads(q_ref), k_ref[...], qtag_ref, ktag_ref).astype(jnp.bfloat16)
    grad = stacked_heads(do_ref)
    dv = lax.dot_general(probs_low, grad, (((0,), (0,)), ((), ())), preferred_element_type=jnp.float32)
    dv_ref[...] = dv.astype(jnp.bfloat16)


def attention_kernel(q_ref, k_ref, v_ref, do_ref, qtag_ref, ktag_ref, out_ref, dq_ref, dk_ref):
    rows = q_ref.shape[0]
    q = stacked_heads(q_ref)
    grad = stacked_heads(do_ref)
    keys = k_ref[...]
    vals = v_ref[...]
    probs = window_probs(q, keys, qtag_ref, ktag_ref)
    probs_low = probs.astype(jnp.bfloat16)
    out = jnp.dot(probs_low, vals, preferred_element_type=jnp.float32).astype(jnp.bfloat16)
    grad_probs = lax.dot_general(grad, vals, (((1,), (1,)), ((), ())), preferred_element_type=jnp.float32)
    delta = jnp.sum(grad.astype(jnp.float32) * out.astype(jnp.float32), axis=-1, keepdims=True)
    grad_scores = (probs * (grad_probs - delta)).astype(jnp.bfloat16)
    dq = (score_scale * jnp.dot(grad_scores, keys, preferred_element_type=jnp.float32)).astype(jnp.bfloat16)
    dk = score_scale * lax.dot_general(grad_scores, q, (((0,), (0,)), ((), ())), preferred_element_type=jnp.float32)
    for r in range(GROUP):
        out_ref[:, r * HD:(r + 1) * HD] = out[r * rows:(r + 1) * rows]
        dq_ref[:, r * HD:(r + 1) * HD] = dq[r * rows:(r + 1) * rows]
    dk_ref[...] = dk.astype(jnp.bfloat16)


def head_specs(rows, span):
    q_spec = pl.BlockSpec((rows, GROUP * HD), lambda g: (0, g))
    kv_spec = pl.BlockSpec((span, HD), lambda g: (0, g))
    tag_specs = [pl.BlockSpec((rows, 1), lambda g: (0, 0)), pl.BlockSpec((1, span), lambda g: (0, 0))]
    return q_spec, kv_spec, tag_specs


def value_grads(queries, keys, grads, query_tags, key_tags):
    rows, q_width = queries.shape
    span, kv_width = keys.shape
    heads = kv_width // HD
    q_spec, kv_spec, tag_specs = head_specs(rows, span)
    return pl.pallas_call(
        value_grad_kernel,
        grid=(heads,),
        in_specs=[q_spec, kv_spec, q_spec] + tag_specs,
        out_specs=kv_spec,
        out_shape=jax.ShapeDtypeStruct((span, kv_width), jnp.bfloat16),
        cost_estimate=pl.CostEstimate(
            flops=4 * rows * GROUP * span * HD * heads,
            transcendentals=rows * GROUP * span * heads,
            bytes_accessed=2 * (2 * rows * q_width + 2 * span * kv_width),
        ),
    )(queries, keys, grads, query_tags, key_tags)


def fused_attention(queries, keys, values, grads, query_tags, key_tags):
    rows, q_width = queries.shape
    span, kv_width = keys.shape
    heads = kv_width // HD
    q_spec, kv_spec, tag_specs = head_specs(rows, span)
    return pl.pallas_call(
        attention_kernel,
        grid=(heads,),
        in_specs=[q_spec, kv_spec, kv_spec, q_spec] + tag_specs,
        out_specs=[q_spec, q_spec, kv_spec],
        out_shape=[
            jax.ShapeDtypeStruct((rows, q_width), jnp.bfloat16),
            jax.ShapeDtypeStruct((rows, q_width), jnp.bfloat16),
            jax.ShapeDtypeStruct((span, kv_width), jnp.bfloat16),
        ],
        cost_estimate=pl.CostEstimate(
            flops=10 * rows * GROUP * span * HD * heads,
            transcendentals=rows * GROUP * span * heads,
            bytes_accessed=2 * (4 * rows * q_width + 3 * span * kv_width),
        ),
    )(queries, keys, values, grads, query_tags, key_tags)


def peer_gather_kernel(axis, n, x_ref, o_ref, send_sem, recv_sem, local_sem):
    me = lax.axis_index(axis)
    barrier = pltpu.get_barrier_semaphore()
    for k in range(1, n):
        pl.semaphore_signal(
            barrier, inc=1, device_id={axis: lax.rem(me + k, n)}, device_id_type=pl.DeviceIdType.MESH
        )
    pl.semaphore_wait(barrier, n - 1)
    local = pltpu.make_async_copy(x_ref, o_ref.at[me], local_sem)
    local.start()
    copies = []
    for k in range(1, n):
        copy = pltpu.make_async_remote_copy(
            src_ref=x_ref,
            dst_ref=o_ref.at[me],
            send_sem=send_sem.at[k],
            recv_sem=recv_sem.at[k],
            device_id={axis: lax.rem(me + k, n)},
            device_id_type=pl.DeviceIdType.MESH,
        )
        copy.start()
        copies.append(copy)
    for copy in copies:
        copy.wait()
    local.wait()


def peer_gather(x, axis, collective_id):
    n = lax.axis_size(axis)
    return pl.pallas_call(
        functools.partial(peer_gather_kernel, axis, n),
        out_shape=jax.ShapeDtypeStruct((n,) + x.shape, x.dtype),
        in_specs=[pl.BlockSpec(memory_space=pl.ANY)],
        out_specs=pl.BlockSpec(memory_space=pl.ANY),
        scratch_shapes=[
            pltpu.SemaphoreType.DMA((n,)),
            pltpu.SemaphoreType.DMA((n,)),
            pltpu.SemaphoreType.DMA,
        ],
        compiler_params=pltpu.CompilerParams(collective_id=collective_id, has_side_effects=True),
    )(x)


def peer_sum_kernel(axis, n, x_ref, o_ref, landed, send_sem, recv_sem, local_sem):
    me = lax.axis_index(axis)
    barrier = pltpu.get_barrier_semaphore()
    for k in range(1, n):
        pl.semaphore_signal(
            barrier, inc=1, device_id={axis: lax.rem(me + k, n)}, device_id_type=pl.DeviceIdType.MESH
        )
    pl.semaphore_wait(barrier, n - 1)
    local = pltpu.make_async_copy(x_ref.at[me], landed.at[0], local_sem)
    local.start()
    copies = []
    for k in range(1, n):
        peer = lax.rem(me + k, n)
        copy = pltpu.make_async_remote_copy(
            src_ref=x_ref.at[peer],
            dst_ref=landed.at[k],
            send_sem=send_sem.at[k],
            recv_sem=recv_sem.at[k],
            device_id={axis: peer},
            device_id_type=pl.DeviceIdType.MESH,
        )
        copy.start()
        copies.append(copy)
    local.wait()
    total = landed[0].astype(jnp.float32)
    for k in range(1, n):
        copies[k - 1].wait()
        total = total + landed[k].astype(jnp.float32)
    o_ref[...] = total


def peer_sum_scatter(x, axis, collective_id):
    n = lax.axis_size(axis)
    return pl.pallas_call(
        functools.partial(peer_sum_kernel, axis, n),
        out_shape=jax.ShapeDtypeStruct(x.shape[1:], jnp.float32),
        in_specs=[pl.BlockSpec(memory_space=pl.ANY)],
        out_specs=pl.BlockSpec(memory_space=pltpu.VMEM),
        scratch_shapes=[
            pltpu.VMEM(x.shape, x.dtype),
            pltpu.SemaphoreType.DMA((n,)),
            pltpu.SemaphoreType.DMA((n,)),
            pltpu.SemaphoreType.DMA,
        ],
        compiler_params=pltpu.CompilerParams(collective_id=collective_id, has_side_effects=True),
    )(x)


def shifted(x, axis, by):
    length = lax.axis_size(axis)
    pairs = [(i, i + by) for i in range(length) if 0 <= i + by < length]
    return lax.ppermute(x, axis, pairs)


def shards(hidden, queries, key_heads, w_value, d_out, segments):
    shard_rows = hidden.shape[1]
    kv_width = w_value.shape[1]
    n_hops = WINDOW // shard_rows
    span_rows = (n_hops + 1) * shard_rows
    tokens_in = hidden[0]
    own_keys = key_heads[0]
    own_segments = segments[0]
    n_fsdp = lax.axis_size("fsdp")
    n_ctx = lax.axis_size("ctx")
    model_width = tokens_in.shape[1]
    half_rows = w_value.shape[0] // 2
    core = lax.axis_index("ctx") % 2
    w_mine = lax.all_gather(
        lax.dynamic_slice_in_dim(w_value, core * half_rows, half_rows, 0), "fsdp", axis=0, tiled=False
    )
    partner = [(i, i ^ 1) for i in range(n_ctx)]
    token_halves = tokens_in.reshape(shard_rows, n_fsdp, 2, half_rows)
    tokens_mine = lax.dynamic_index_in_dim(token_halves, core, axis=2, keepdims=False)
    partner_tokens = lax.ppermute(
        lax.dynamic_index_in_dim(token_halves, 1 - core, axis=2, keepdims=False), "ctx", partner
    )
    out_rows = model_width // (n_ctx * n_fsdp)
    token_cols = (
        tokens_in.reshape(shard_rows, n_ctx, n_fsdp, out_rows).transpose(2, 0, 1, 3)
    )
    token_cols = lax.all_to_all(token_cols, "fsdp", 0, 0, tiled=True)
    tag_columns = jnp.broadcast_to(own_segments.astype(jnp.bfloat16)[:, None], (shard_rows, HD))
    parcel = jnp.concatenate([own_keys, tag_columns], 1)
    arrived = [shifted(parcel, "ctx", hop) for hop in range(1, n_hops + 1)]
    window_parcel = jnp.concatenate(arrived[::-1] + [parcel], 0)
    window_keys = window_parcel[:, :kv_width]
    window_tags = window_parcel[:, kv_width].astype(jnp.int32)
    first_query = lax.axis_index("ctx") * shard_rows
    key_pos = first_query - WINDOW + jnp.arange(span_rows, dtype=jnp.int32)
    key_tags = jnp.where(key_pos >= 0, window_tags, -1)
    query_tags = own_segments.astype(jnp.int32)[:, None]
    own_start = n_hops * shard_rows

    def returned_sum(terms):
        total = terms[own_start:].astype(jnp.float32)
        for hop in range(1, n_hops + 1):
            low_edge = (n_hops - hop) * shard_rows
            total = total + shifted(terms[low_edge : low_edge + shard_rows], "ctx", -hop).astype(jnp.float32)
        return total.astype(jnp.bfloat16)

    value_terms = value_grads(queries[0], window_keys, d_out[0], query_tags, key_tags[None, :])
    d_values_low = returned_sum(value_terms)
    w_mine, _ = lax.optimization_barrier((w_mine, d_values_low))
    grads_all = peer_gather(d_values_low, "fsdp", 2)
    weight_part = jnp.einsum(
        "ftcr,ftn->crn", token_cols, grads_all, preferred_element_type=jnp.float32
    )
    d_weight = peer_sum_scatter(weight_part.astype(jnp.bfloat16), "ctx", 3)

    partner_part = jnp.einsum("tfr,frn->tn", partner_tokens, w_mine, preferred_element_type=jnp.float32)
    values = (
        jnp.einsum("tfr,frn->tn", tokens_mine, w_mine, preferred_element_type=jnp.float32)
        + lax.ppermute(partner_part, "ctx", partner)
    ).astype(jnp.bfloat16)
    arrived_values = [shifted(values, "ctx", hop) for hop in range(1, n_hops + 1)]
    window_values = jnp.concatenate(arrived_values[::-1] + [values], 0)
    out_rows_attn, d_query_heads, key_terms = fused_attention(
        queries[0], window_keys, window_values, d_out[0], query_tags, key_tags[None, :]
    )
    d_key_rows = returned_sum(key_terms)
    d_mine = jnp.einsum("tn,frn->tfr", d_values_low, w_mine, preferred_element_type=jnp.float32).astype(jnp.bfloat16)
    partner_grads = lax.ppermute(d_values_low, "ctx", partner)
    d_other = lax.ppermute(
        jnp.einsum("tn,frn->tfr", partner_grads, w_mine, preferred_element_type=jnp.float32).astype(jnp.bfloat16),
        "ctx",
        partner,
    )
    d_tokens = jnp.where(
        core == 0, jnp.stack([d_mine, d_other], 2), jnp.stack([d_other, d_mine], 2)
    ).reshape(shard_rows, model_width)
    return (
        out_rows_attn[None],
        d_query_heads[None],
        d_key_rows[None],
        d_tokens[None],
        d_weight,
    )


def solution(mesh):
    in_specs = (
        P("fsdp", "ctx", None),
        P("fsdp", "ctx", None),
        P("fsdp", "ctx", None),
        P("fsdp", None),
        P("fsdp", "ctx", None),
        P("fsdp", "ctx"),
    )
    out_specs = (
        P("fsdp", "ctx", None),
        P("fsdp", "ctx", None),
        P("fsdp", "ctx", None),
        P("fsdp", "ctx", None),
        P(("ctx", "fsdp"), None),
    )
    return jax.shard_map(shards, mesh=mesh, in_specs=in_specs, out_specs=out_specs, check_vma=False)
```

```python
import functools
import math

import jax
import jax.numpy as jnp
from jax import lax
from jax.experimental import pallas as pl
from jax.experimental.pallas import tpu as pltpu
from jax.sharding import PartitionSpec as P

HQ = 16
HK = 8
HD = 128
WINDOW = 1024
GROUP = 2


score_scale = 1.0 / math.sqrt(168.0)


def window_probs(q, keys, qtag_ref, ktag_ref):
    rows = qtag_ref.shape[0]
    span = keys.shape[0]
    reach = span - rows
    t_idx = lax.broadcasted_iota(jnp.int32, (rows, span), 0)
    l_idx = lax.broadcasted_iota(jnp.int32, (rows, span), 1)
    allowed = (qtag_ref[...] == ktag_ref[...]) & (l_idx > t_idx) & (l_idx <= t_idx + reach)
    allowed = jnp.concatenate([allowed] * GROUP, axis=0)
    scores = lax.dot_general(q, keys, (((1,), (1,)), ((), ())), preferred_element_type=jnp.float32) * score_scale
    scores = jnp.where(allowed, scores, -jnp.inf)
    highest = jnp.max(scores, axis=-1, keepdims=True)
    raw = jnp.exp(scores - highest)
    return raw / jnp.sum(raw, axis=-1, keepdims=True)


def stacked_heads(ref):
    return jnp.concatenate([ref[:, r * HD:(r + 1) * HD] for r in range(GROUP)], axis=0)


def value_grad_kernel(q_ref, k_ref, do_ref, qtag_ref, ktag_ref, dv_ref):
    probs_low = window_probs(stacked_heads(q_ref), k_ref[...], qtag_ref, ktag_ref).astype(jnp.bfloat16)
    grad = stacked_heads(do_ref)
    dv = lax.dot_general(probs_low, grad, (((0,), (0,)), ((), ())), preferred_element_type=jnp.float32)
    dv_ref[...] = dv.astype(jnp.bfloat16)


def attention_kernel(q_ref, k_ref, v_ref, do_ref, qtag_ref, ktag_ref, out_ref, dq_ref, dk_ref):
    rows = q_ref.shape[0]
    q = stacked_heads(q_ref)
    grad = stacked_heads(do_ref)
    keys = k_ref[...]
    vals = v_ref[...]
    probs = window_probs(q, keys, qtag_ref, ktag_ref)
    probs_low = probs.astype(jnp.bfloat16)
    out = jnp.dot(probs_low, vals, preferred_element_type=jnp.float32).astype(jnp.bfloat16)
    grad_probs = lax.dot_general(grad, vals, (((1,), (1,)), ((), ())), preferred_element_type=jnp.float32)
    delta = jnp.sum(grad.astype(jnp.float32) * out.astype(jnp.float32), axis=-1, keepdims=True)
    grad_scores = (probs * (grad_probs - delta)).astype(jnp.bfloat16)
    dq = (score_scale * jnp.dot(grad_scores, keys, preferred_element_type=jnp.float32)).astype(jnp.bfloat16)
    dk = score_scale * lax.dot_general(grad_scores, q, (((0,), (0,)), ((), ())), preferred_element_type=jnp.float32)
    for r in range(GROUP):
        out_ref[:, r * HD:(r + 1) * HD] = out[r * rows:(r + 1) * rows]
        dq_ref[:, r * HD:(r + 1) * HD] = dq[r * rows:(r + 1) * rows]
    dk_ref[...] = dk.astype(jnp.bfloat16)


def head_specs(rows, span):
    q_spec = pl.BlockSpec((rows, GROUP * HD), lambda g: (0, g))
    kv_spec = pl.BlockSpec((span, HD), lambda g: (0, g))
    tag_specs = [pl.BlockSpec((rows, 1), lambda g: (0, 0)), pl.BlockSpec((1, span), lambda g: (0, 0))]
    return q_spec, kv_spec, tag_specs


def value_grads(queries, keys, grads, query_tags, key_tags):
    rows, q_width = queries.shape
    span, kv_width = keys.shape
    heads = kv_width // HD
    q_spec, kv_spec, tag_specs = head_specs(rows, span)
    return pl.pallas_call(
        value_grad_kernel,
        grid=(heads,),
        in_specs=[q_spec, kv_spec, q_spec] + tag_specs,
        out_specs=kv_spec,
        out_shape=jax.ShapeDtypeStruct((span, kv_width), jnp.bfloat16),
        cost_estimate=pl.CostEstimate(
            flops=4 * rows * GROUP * span * HD * heads,
            transcendentals=rows * GROUP * span * heads,
            bytes_accessed=2 * (2 * rows * q_width + 2 * span * kv_width),
        ),
    )(queries, keys, grads, query_tags, key_tags)


def fused_attention(queries, keys, values, grads, query_tags, key_tags):
    rows, q_width = queries.shape
    span, kv_width = keys.shape
    heads = kv_width // HD
    q_spec, kv_spec, tag_specs = head_specs(rows, span)
    return pl.pallas_call(
        attention_kernel,
        grid=(heads,),
        in_specs=[q_spec, kv_spec, kv_spec, q_spec] + tag_specs,
        out_specs=[q_spec, q_spec, kv_spec],
        out_shape=[
            jax.ShapeDtypeStruct((rows, q_width), jnp.bfloat16),
            jax.ShapeDtypeStruct((rows, q_width), jnp.bfloat16),
            jax.ShapeDtypeStruct((span, kv_width), jnp.bfloat16),
        ],
        cost_estimate=pl.CostEstimate(
            flops=10 * rows * GROUP * span * HD * heads,
            transcendentals=rows * GROUP * span * heads,
            bytes_accessed=2 * (4 * rows * q_width + 3 * span * kv_width),
        ),
    )(queries, keys, values, grads, query_tags, key_tags)


def peer_gather_kernel(axis, n, x_ref, o_ref, send_sem, recv_sem, local_sem):
    me = lax.axis_index(axis)
    barrier = pltpu.get_barrier_semaphore()
    for k in range(1, n):
        pl.semaphore_signal(
            barrier, inc=1, device_id={axis: lax.rem(me + k, n)}, device_id_type=pl.DeviceIdType.MESH
        )
    pl.semaphore_wait(barrier, n - 1)
    local = pltpu.make_async_copy(x_ref, o_ref.at[me], local_sem)
    local.start()
    copies = []
    for k in range(1, n):
        copy = pltpu.make_async_remote_copy(
            src_ref=x_ref,
            dst_ref=o_ref.at[me],
            send_sem=send_sem.at[k],
            recv_sem=recv_sem.at[k],
            device_id={axis: lax.rem(me + k, n)},
            device_id_type=pl.DeviceIdType.MESH,
        )
        copy.start()
        copies.append(copy)
    for copy in copies:
        copy.wait()
    local.wait()


def peer_gather(x, axis, collective_id):
    n = lax.axis_size(axis)
    return pl.pallas_call(
        functools.partial(peer_gather_kernel, axis, n),
        out_shape=jax.ShapeDtypeStruct((n,) + x.shape, x.dtype),
        in_specs=[pl.BlockSpec(memory_space=pl.ANY)],
        out_specs=pl.BlockSpec(memory_space=pl.ANY),
        scratch_shapes=[
            pltpu.SemaphoreType.DMA((n,)),
            pltpu.SemaphoreType.DMA((n,)),
            pltpu.SemaphoreType.DMA,
        ],
        compiler_params=pltpu.CompilerParams(collective_id=collective_id, has_side_effects=True),
    )(x)


def peer_sum_kernel(axis, n, x_ref, o_ref, landed, send_sem, recv_sem, local_sem):
    me = lax.axis_index(axis)
    barrier = pltpu.get_barrier_semaphore()
    for k in range(1, n):
        pl.semaphore_signal(
            barrier, inc=1, device_id={axis: lax.rem(me + k, n)}, device_id_type=pl.DeviceIdType.MESH
        )
    pl.semaphore_wait(barrier, n - 1)
    local = pltpu.make_async_copy(x_ref.at[me], landed.at[0], local_sem)
    local.start()
    copies = []
    for k in range(1, n):
        peer = lax.rem(me + k, n)
        copy = pltpu.make_async_remote_copy(
            src_ref=x_ref.at[peer],
            dst_ref=landed.at[k],
            send_sem=send_sem.at[k],
            recv_sem=recv_sem.at[k],
            device_id={axis: peer},
            device_id_type=pl.DeviceIdType.MESH,
        )
        copy.start()
        copies.append(copy)
    local.wait()
    total = landed[0].astype(jnp.float32)
    for k in range(1, n):
        copies[k - 1].wait()
        total = total + landed[k].astype(jnp.float32)
    o_ref[...] = total


def peer_sum_scatter(x, axis, collective_id):
    n = lax.axis_size(axis)
    return pl.pallas_call(
        functools.partial(peer_sum_kernel, axis, n),
        out_shape=jax.ShapeDtypeStruct(x.shape[1:], jnp.float32),
        in_specs=[pl.BlockSpec(memory_space=pl.ANY)],
        out_specs=pl.BlockSpec(memory_space=pltpu.VMEM),
        scratch_shapes=[
            pltpu.VMEM(x.shape, x.dtype),
            pltpu.SemaphoreType.DMA((n,)),
            pltpu.SemaphoreType.DMA((n,)),
            pltpu.SemaphoreType.DMA,
        ],
        compiler_params=pltpu.CompilerParams(collective_id=collective_id, has_side_effects=True),
    )(x)


def shifted(x, axis, by):
    length = lax.axis_size(axis)
    pairs = [(i, i + by) for i in range(length) if 0 <= i + by < length]
    return lax.ppermute(x, axis, pairs)


def shards(hidden, queries, key_heads, w_value, d_out, segments):
    shard_rows = hidden.shape[1]
    kv_width = w_value.shape[1]
    n_hops = WINDOW // shard_rows
    span_rows = (n_hops + 1) * shard_rows
    tokens_in = hidden[0]
    own_keys = key_heads[0]
    own_segments = segments[0]
    n_fsdp = lax.axis_size("fsdp")
    n_ctx = lax.axis_size("ctx")
    model_width = tokens_in.shape[1]
    half_rows = w_value.shape[0] // 2
    core = lax.axis_index("ctx") % 2
    w_mine = lax.all_gather(
        lax.dynamic_slice_in_dim(w_value, core * half_rows, half_rows, 0), "fsdp", axis=0, tiled=False
    )
    partner = [(i, i ^ 1) for i in range(n_ctx)]
    token_halves = tokens_in.reshape(shard_rows, n_fsdp, 2, half_rows)
    tokens_mine = lax.dynamic_index_in_dim(token_halves, core, axis=2, keepdims=False)
    partner_tokens = lax.ppermute(
        lax.dynamic_index_in_dim(token_halves, 1 - core, axis=2, keepdims=False), "ctx", partner
    )
    out_rows = model_width // (n_ctx * n_fsdp)
    token_cols = (
        tokens_in.reshape(shard_rows, n_ctx, n_fsdp, out_rows).transpose(2, 0, 1, 3)
    )
    token_cols = lax.all_to_all(token_cols, "fsdp", 0, 0, tiled=True)
    tag_columns = jnp.broadcast_to(own_segments.astype(jnp.bfloat16)[:, None], (shard_rows, HD))
    parcel = jnp.concatenate([own_keys, tag_columns], 1)
    arrived = [shifted(parcel, "ctx", hop) for hop in range(1, n_hops + 1)]
    window_parcel = jnp.concatenate(arrived[::-1] + [parcel], 0)
    window_keys = window_parcel[:, :kv_width]
    window_tags = window_parcel[:, kv_width].astype(jnp.int32)
    first_query = lax.axis_index("ctx") * shard_rows
    key_pos = first_query - WINDOW + jnp.arange(span_rows, dtype=jnp.int32)
    key_tags = jnp.where(key_pos >= 0, window_tags, -1)
    query_tags = own_segments.astype(jnp.int32)[:, None]
    own_start = n_hops * shard_rows

    def returned_sum(terms):
        total = terms[own_start:].astype(jnp.float32)
        for hop in range(1, n_hops + 1):
            low_edge = (n_hops - hop) * shard_rows
            total = total + shifted(terms[low_edge : low_edge + shard_rows], "ctx", -hop).astype(jnp.float32)
        return total.astype(jnp.bfloat16)

    value_terms = value_grads(queries[0], window_keys, d_out[0], query_tags, key_tags[None, :])
    d_values_low = returned_sum(value_terms)
    w_mine, _ = lax.optimization_barrier((w_mine, d_values_low))

    partner_part = jnp.einsum("tfr,frn->tn", partner_tokens, w_mine, preferred_element_type=jnp.float32)
    values = (
        jnp.einsum("tfr,frn->tn", tokens_mine, w_mine, preferred_element_type=jnp.float32)
        + lax.ppermute(partner_part, "ctx", partner)
    ).astype(jnp.bfloat16)
    arrived_values = [shifted(values, "ctx", hop) for hop in range(1, n_hops + 1)]
    window_values = jnp.concatenate(arrived_values[::-1] + [values], 0)
    out_rows_attn, d_query_heads, key_terms = fused_attention(
        queries[0], window_keys, window_values, d_out[0], query_tags, key_tags[None, :]
    )
    d_key_rows = returned_sum(key_terms)
    grads_for_weight, _ = lax.optimization_barrier((d_values_low, key_terms))
    grads_all = peer_gather(grads_for_weight, "fsdp", 2)
    weight_part = jnp.einsum(
        "ftcr,ftn->crn", token_cols, grads_all, preferred_element_type=jnp.float32
    )
    d_weight = peer_sum_scatter(weight_part.astype(jnp.bfloat16), "ctx", 3)
    d_mine = jnp.einsum("tn,frn->tfr", d_values_low, w_mine, preferred_element_type=jnp.float32).astype(jnp.bfloat16)
    partner_grads = lax.ppermute(d_values_low, "ctx", partner)
    d_other = lax.ppermute(
        jnp.einsum("tn,frn->tfr", partner_grads, w_mine, preferred_element_type=jnp.float32).astype(jnp.bfloat16),
        "ctx",
        partner,
    )
    d_tokens = jnp.where(
        core == 0, jnp.stack([d_mine, d_other], 2), jnp.stack([d_other, d_mine], 2)
    ).reshape(shard_rows, model_width)
    return (
        out_rows_attn[None],
        d_query_heads[None],
        d_key_rows[None],
        d_tokens[None],
        d_weight,
    )


def solution(mesh):
    in_specs = (
        P("fsdp", "ctx", None),
        P("fsdp", "ctx", None),
        P("fsdp", "ctx", None),
        P("fsdp", None),
        P("fsdp", "ctx", None),
        P("fsdp", "ctx"),
    )
    out_specs = (
        P("fsdp", "ctx", None),
        P("fsdp", "ctx", None),
        P("fsdp", "ctx", None),
        P("fsdp", "ctx", None),
        P(("ctx", "fsdp"), None),
    )
    return jax.shard_map(shards, mesh=mesh, in_specs=in_specs, out_specs=out_specs, check_vma=False)
```

```python
import functools
import math

import jax
import jax.numpy as jnp
from jax import lax
from jax.experimental import pallas as pl
from jax.experimental.pallas import tpu as pltpu
from jax.sharding import PartitionSpec as P

HQ = 16
HK = 8
HD = 128
WINDOW = 1024
GROUP = 2


score_scale = 1.0 / math.sqrt(168.0)


def window_probs(q, keys, qtag_ref, ktag_ref):
    rows = qtag_ref.shape[0]
    span = keys.shape[0]
    reach = span - rows
    t_idx = lax.broadcasted_iota(jnp.int32, (rows, span), 0)
    l_idx = lax.broadcasted_iota(jnp.int32, (rows, span), 1)
    allowed = (qtag_ref[...] == ktag_ref[...]) & (l_idx > t_idx) & (l_idx <= t_idx + reach)
    allowed = jnp.concatenate([allowed] * GROUP, axis=0)
    scores = lax.dot_general(q, keys, (((1,), (1,)), ((), ())), preferred_element_type=jnp.float32) * score_scale
    scores = jnp.where(allowed, scores, -jnp.inf)
    highest = jnp.max(scores, axis=-1, keepdims=True)
    raw = jnp.exp(scores - highest)
    return raw / jnp.sum(raw, axis=-1, keepdims=True)


def stacked_heads(ref):
    return jnp.concatenate([ref[:, r * HD:(r + 1) * HD] for r in range(GROUP)], axis=0)


def value_grad_kernel(q_ref, k_ref, do_ref, qtag_ref, ktag_ref, dv_ref):
    probs_low = window_probs(stacked_heads(q_ref), k_ref[...], qtag_ref, ktag_ref).astype(jnp.bfloat16)
    grad = stacked_heads(do_ref)
    dv = lax.dot_general(probs_low, grad, (((0,), (0,)), ((), ())), preferred_element_type=jnp.float32)
    dv_ref[...] = dv.astype(jnp.bfloat16)


def attention_kernel(q_ref, k_ref, v_ref, do_ref, qtag_ref, ktag_ref, out_ref, dq_ref, dk_ref):
    rows = q_ref.shape[0]
    q = stacked_heads(q_ref)
    grad = stacked_heads(do_ref)
    keys = k_ref[...]
    vals = v_ref[...]
    probs = window_probs(q, keys, qtag_ref, ktag_ref)
    probs_low = probs.astype(jnp.bfloat16)
    out = jnp.dot(probs_low, vals, preferred_element_type=jnp.float32).astype(jnp.bfloat16)
    grad_probs = lax.dot_general(grad, vals, (((1,), (1,)), ((), ())), preferred_element_type=jnp.float32)
    delta = jnp.sum(grad.astype(jnp.float32) * out.astype(jnp.float32), axis=-1, keepdims=True)
    grad_scores = (probs * (grad_probs - delta)).astype(jnp.bfloat16)
    dq = (score_scale * jnp.dot(grad_scores, keys, preferred_element_type=jnp.float32)).astype(jnp.bfloat16)
    dk = score_scale * lax.dot_general(grad_scores, q, (((0,), (0,)), ((), ())), preferred_element_type=jnp.float32)
    for r in range(GROUP):
        out_ref[:, r * HD:(r + 1) * HD] = out[r * rows:(r + 1) * rows]
        dq_ref[:, r * HD:(r + 1) * HD] = dq[r * rows:(r + 1) * rows]
    dk_ref[...] = dk.astype(jnp.bfloat16)


def head_specs(rows, span):
    q_spec = pl.BlockSpec((rows, GROUP * HD), lambda g: (0, g))
    kv_spec = pl.BlockSpec((span, HD), lambda g: (0, g))
    tag_specs = [pl.BlockSpec((rows, 1), lambda g: (0, 0)), pl.BlockSpec((1, span), lambda g: (0, 0))]
    return q_spec, kv_spec, tag_specs


def value_grads(queries, keys, grads, query_tags, key_tags):
    rows, q_width = queries.shape
    span, kv_width = keys.shape
    heads = kv_width // HD
    q_spec, kv_spec, tag_specs = head_specs(rows, span)
    return pl.pallas_call(
        value_grad_kernel,
        grid=(heads,),
        in_specs=[q_spec, kv_spec, q_spec] + tag_specs,
        out_specs=kv_spec,
        out_shape=jax.ShapeDtypeStruct((span, kv_width), jnp.bfloat16),
        cost_estimate=pl.CostEstimate(
            flops=4 * rows * GROUP * span * HD * heads,
            transcendentals=rows * GROUP * span * heads,
            bytes_accessed=2 * (2 * rows * q_width + 2 * span * kv_width),
        ),
    )(queries, keys, grads, query_tags, key_tags)


def fused_attention(queries, keys, values, grads, query_tags, key_tags):
    rows, q_width = queries.shape
    span, kv_width = keys.shape
    heads = kv_width // HD
    q_spec, kv_spec, tag_specs = head_specs(rows, span)
    return pl.pallas_call(
        attention_kernel,
        grid=(heads,),
        in_specs=[q_spec, kv_spec, kv_spec, q_spec] + tag_specs,
        out_specs=[q_spec, q_spec, kv_spec],
        out_shape=[
            jax.ShapeDtypeStruct((rows, q_width), jnp.bfloat16),
            jax.ShapeDtypeStruct((rows, q_width), jnp.bfloat16),
            jax.ShapeDtypeStruct((span, kv_width), jnp.bfloat16),
        ],
        cost_estimate=pl.CostEstimate(
            flops=10 * rows * GROUP * span * HD * heads,
            transcendentals=rows * GROUP * span * heads,
            bytes_accessed=2 * (4 * rows * q_width + 3 * span * kv_width),
        ),
    )(queries, keys, values, grads, query_tags, key_tags)


def peer_gather_kernel(axis, n, x_ref, o_ref, send_sem, recv_sem, local_sem):
    me = lax.axis_index(axis)
    barrier = pltpu.get_barrier_semaphore()
    for k in range(1, n):
        pl.semaphore_signal(
            barrier, inc=1, device_id={axis: lax.rem(me + k, n)}, device_id_type=pl.DeviceIdType.MESH
        )
    pl.semaphore_wait(barrier, n - 1)
    local = pltpu.make_async_copy(x_ref, o_ref.at[me], local_sem)
    local.start()
    copies = []
    for k in range(1, n):
        copy = pltpu.make_async_remote_copy(
            src_ref=x_ref,
            dst_ref=o_ref.at[me],
            send_sem=send_sem.at[k],
            recv_sem=recv_sem.at[k],
            device_id={axis: lax.rem(me + k, n)},
            device_id_type=pl.DeviceIdType.MESH,
        )
        copy.start()
        copies.append(copy)
    for copy in copies:
        copy.wait()
    local.wait()


def peer_gather(x, axis, collective_id):
    n = lax.axis_size(axis)
    return pl.pallas_call(
        functools.partial(peer_gather_kernel, axis, n),
        out_shape=jax.ShapeDtypeStruct((n,) + x.shape, x.dtype),
        in_specs=[pl.BlockSpec(memory_space=pl.ANY)],
        out_specs=pl.BlockSpec(memory_space=pl.ANY),
        scratch_shapes=[
            pltpu.SemaphoreType.DMA((n,)),
            pltpu.SemaphoreType.DMA((n,)),
            pltpu.SemaphoreType.DMA,
        ],
        compiler_params=pltpu.CompilerParams(collective_id=collective_id, has_side_effects=True),
    )(x)


def peer_sum_kernel(axis, n, x_ref, o_ref, landed, send_sem, recv_sem, local_sem):
    me = lax.axis_index(axis)
    barrier = pltpu.get_barrier_semaphore()
    for k in range(1, n):
        pl.semaphore_signal(
            barrier, inc=1, device_id={axis: lax.rem(me + k, n)}, device_id_type=pl.DeviceIdType.MESH
        )
    pl.semaphore_wait(barrier, n - 1)
    local = pltpu.make_async_copy(x_ref.at[me], landed.at[0], local_sem)
    local.start()
    copies = []
    for k in range(1, n):
        peer = lax.rem(me + k, n)
        copy = pltpu.make_async_remote_copy(
            src_ref=x_ref.at[peer],
            dst_ref=landed.at[k],
            send_sem=send_sem.at[k],
            recv_sem=recv_sem.at[k],
            device_id={axis: peer},
            device_id_type=pl.DeviceIdType.MESH,
        )
        copy.start()
        copies.append(copy)
    local.wait()
    total = landed[0].astype(jnp.float32)
    for k in range(1, n):
        copies[k - 1].wait()
        total = total + landed[k].astype(jnp.float32)
    o_ref[...] = total


def peer_sum_scatter(x, axis, collective_id):
    n = lax.axis_size(axis)
    return pl.pallas_call(
        functools.partial(peer_sum_kernel, axis, n),
        out_shape=jax.ShapeDtypeStruct(x.shape[1:], jnp.float32),
        in_specs=[pl.BlockSpec(memory_space=pl.ANY)],
        out_specs=pl.BlockSpec(memory_space=pltpu.VMEM),
        scratch_shapes=[
            pltpu.VMEM(x.shape, x.dtype),
            pltpu.SemaphoreType.DMA((n,)),
            pltpu.SemaphoreType.DMA((n,)),
            pltpu.SemaphoreType.DMA,
        ],
        compiler_params=pltpu.CompilerParams(collective_id=collective_id, has_side_effects=True),
    )(x)


def shifted(x, axis, by):
    length = lax.axis_size(axis)
    pairs = [(i, i + by) for i in range(length) if 0 <= i + by < length]
    return lax.ppermute(x, axis, pairs)


def shards(hidden, queries, key_heads, w_value, d_out, segments):
    shard_rows = hidden.shape[1]
    kv_width = w_value.shape[1]
    n_hops = WINDOW // shard_rows
    span_rows = (n_hops + 1) * shard_rows
    tokens_in = hidden[0]
    own_keys = key_heads[0]
    own_segments = segments[0]
    n_fsdp = lax.axis_size("fsdp")
    n_ctx = lax.axis_size("ctx")
    model_width = tokens_in.shape[1]
    half_rows = w_value.shape[0] // 2
    core = lax.axis_index("ctx") % 2
    w_mine = lax.all_gather(
        lax.dynamic_slice_in_dim(w_value, core * half_rows, half_rows, 0), "fsdp", axis=0, tiled=False
    )
    partner = [(i, i ^ 1) for i in range(n_ctx)]
    token_halves = tokens_in.reshape(shard_rows, n_fsdp, 2, half_rows)
    tokens_mine = lax.dynamic_index_in_dim(token_halves, core, axis=2, keepdims=False)
    partner_tokens = lax.ppermute(
        lax.dynamic_index_in_dim(token_halves, 1 - core, axis=2, keepdims=False), "ctx", partner
    )
    out_rows = model_width // (n_ctx * n_fsdp)
    token_cols = (
        tokens_in.reshape(shard_rows, n_ctx, n_fsdp, out_rows).transpose(2, 0, 1, 3)
    )
    token_cols = lax.all_to_all(token_cols, "fsdp", 0, 0, tiled=True)
    tag_columns = jnp.broadcast_to(own_segments.astype(jnp.bfloat16)[:, None], (shard_rows, HD))
    parcel = jnp.concatenate([own_keys, tag_columns], 1)
    arrived = [shifted(parcel, "ctx", hop) for hop in range(1, n_hops + 1)]
    window_parcel = jnp.concatenate(arrived[::-1] + [parcel], 0)
    window_keys = window_parcel[:, :kv_width]
    window_tags = window_parcel[:, kv_width].astype(jnp.int32)
    first_query = lax.axis_index("ctx") * shard_rows
    key_pos = first_query - WINDOW + jnp.arange(span_rows, dtype=jnp.int32)
    key_tags = jnp.where(key_pos >= 0, window_tags, -1)
    query_tags = own_segments.astype(jnp.int32)[:, None]
    own_start = n_hops * shard_rows

    def returned_sum(terms):
        total = terms[own_start:].astype(jnp.float32)
        for hop in range(1, n_hops + 1):
            low_edge = (n_hops - hop) * shard_rows
            total = total + shifted(terms[low_edge : low_edge + shard_rows], "ctx", -hop).astype(jnp.float32)
        return total.astype(jnp.bfloat16)

    value_terms = value_grads(queries[0], window_keys, d_out[0], query_tags, key_tags[None, :])
    d_values_low = returned_sum(value_terms)
    w_mine, _ = lax.optimization_barrier((w_mine, d_values_low))
    grads_all = lax.all_gather(d_values_low, "fsdp", axis=0, tiled=False)

    partner_part = jnp.einsum("tfr,frn->tn", partner_tokens, w_mine, preferred_element_type=jnp.float32)
    values = (
        jnp.einsum("tfr,frn->tn", tokens_mine, w_mine, preferred_element_type=jnp.float32)
        + lax.ppermute(partner_part, "ctx", partner)
    ).astype(jnp.bfloat16)
    arrived_values = [shifted(values, "ctx", hop) for hop in range(1, n_hops + 1)]
    window_values = jnp.concatenate(arrived_values[::-1] + [values], 0)
    out_rows_attn, d_query_heads, key_terms = fused_attention(
        queries[0], window_keys, window_values, d_out[0], query_tags, key_tags[None, :]
    )
    d_key_rows = returned_sum(key_terms)
    grads_all, _ = lax.optimization_barrier((grads_all, key_terms))
    weight_part = jnp.einsum(
        "ftcr,ftn->crn", token_cols, grads_all, preferred_element_type=jnp.float32
    )
    d_weight = peer_sum_scatter(weight_part.astype(jnp.bfloat16), "ctx", 3)
    d_mine = jnp.einsum("tn,frn->tfr", d_values_low, w_mine, preferred_element_type=jnp.float32).astype(jnp.bfloat16)
    partner_grads = lax.ppermute(d_values_low, "ctx", partner)
    d_other = lax.ppermute(
        jnp.einsum("tn,frn->tfr", partner_grads, w_mine, preferred_element_type=jnp.float32).astype(jnp.bfloat16),
        "ctx",
        partner,
    )
    d_tokens = jnp.where(
        core == 0, jnp.stack([d_mine, d_other], 2), jnp.stack([d_other, d_mine], 2)
    ).reshape(shard_rows, model_width)
    return (
        out_rows_attn[None],
        d_query_heads[None],
        d_key_rows[None],
        d_tokens[None],
        d_weight,
    )


def solution(mesh):
    in_specs = (
        P("fsdp", "ctx", None),
        P("fsdp", "ctx", None),
        P("fsdp", "ctx", None),
        P("fsdp", None),
        P("fsdp", "ctx", None),
        P("fsdp", "ctx"),
    )
    out_specs = (
        P("fsdp", "ctx", None),
        P("fsdp", "ctx", None),
        P("fsdp", "ctx", None),
        P("fsdp", "ctx", None),
        P(("ctx", "fsdp"), None),
    )
    return jax.shard_map(shards, mesh=mesh, in_specs=in_specs, out_specs=out_specs, check_vma=False)
```

```python
import functools
import math

import jax
import jax.numpy as jnp
from jax import lax
from jax.experimental import pallas as pl
from jax.experimental.pallas import tpu as pltpu
from jax.sharding import PartitionSpec as P

HQ = 16
HK = 8
HD = 128
WINDOW = 1024
GROUP = 2


score_scale = 1.0 / math.sqrt(168.0)


def window_probs(q, keys, qtag_ref, ktag_ref):
    rows = qtag_ref.shape[0]
    span = keys.shape[0]
    reach = span - rows
    t_idx = lax.broadcasted_iota(jnp.int32, (rows, span), 0)
    l_idx = lax.broadcasted_iota(jnp.int32, (rows, span), 1)
    allowed = (qtag_ref[...] == ktag_ref[...]) & (l_idx > t_idx) & (l_idx <= t_idx + reach)
    allowed = jnp.concatenate([allowed] * GROUP, axis=0)
    scores = lax.dot_general(q, keys, (((1,), (1,)), ((), ())), preferred_element_type=jnp.float32) * score_scale
    scores = jnp.where(allowed, scores, -jnp.inf)
    highest = jnp.max(scores, axis=-1, keepdims=True)
    raw = jnp.exp(scores - highest)
    return raw / jnp.sum(raw, axis=-1, keepdims=True)


def stacked_heads(ref):
    return jnp.concatenate([ref[:, r * HD:(r + 1) * HD] for r in range(GROUP)], axis=0)


def value_grad_kernel(q_ref, k_ref, do_ref, qtag_ref, ktag_ref, dv_ref):
    probs_low = window_probs(stacked_heads(q_ref), k_ref[...], qtag_ref, ktag_ref).astype(jnp.bfloat16)
    grad = stacked_heads(do_ref)
    dv = lax.dot_general(probs_low, grad, (((0,), (0,)), ((), ())), preferred_element_type=jnp.float32)
    dv_ref[...] = dv.astype(jnp.bfloat16)


def attention_kernel(q_ref, k_ref, v_ref, do_ref, qtag_ref, ktag_ref, out_ref, dq_ref, dk_ref):
    rows = q_ref.shape[0]
    q = stacked_heads(q_ref)
    grad = stacked_heads(do_ref)
    keys = k_ref[...]
    vals = v_ref[...]
    probs = window_probs(q, keys, qtag_ref, ktag_ref)
    probs_low = probs.astype(jnp.bfloat16)
    out = jnp.dot(probs_low, vals, preferred_element_type=jnp.float32).astype(jnp.bfloat16)
    grad_probs = lax.dot_general(grad, vals, (((1,), (1,)), ((), ())), preferred_element_type=jnp.float32)
    delta = jnp.sum(grad.astype(jnp.float32) * out.astype(jnp.float32), axis=-1, keepdims=True)
    grad_scores = (probs * (grad_probs - delta)).astype(jnp.bfloat16)
    dq = (score_scale * jnp.dot(grad_scores, keys, preferred_element_type=jnp.float32)).astype(jnp.bfloat16)
    dk = score_scale * lax.dot_general(grad_scores, q, (((0,), (0,)), ((), ())), preferred_element_type=jnp.float32)
    for r in range(GROUP):
        out_ref[:, r * HD:(r + 1) * HD] = out[r * rows:(r + 1) * rows]
        dq_ref[:, r * HD:(r + 1) * HD] = dq[r * rows:(r + 1) * rows]
    dk_ref[...] = dk.astype(jnp.bfloat16)


def head_specs(rows, span):
    q_spec = pl.BlockSpec((rows, GROUP * HD), lambda g: (0, g))
    kv_spec = pl.BlockSpec((span, HD), lambda g: (0, g))
    tag_specs = [pl.BlockSpec((rows, 1), lambda g: (0, 0)), pl.BlockSpec((1, span), lambda g: (0, 0))]
    return q_spec, kv_spec, tag_specs


def value_grads(queries, keys, grads, query_tags, key_tags):
    rows, q_width = queries.shape
    span, kv_width = keys.shape
    heads = kv_width // HD
    q_spec, kv_spec, tag_specs = head_specs(rows, span)
    return pl.pallas_call(
        value_grad_kernel,
        grid=(heads,),
        in_specs=[q_spec, kv_spec, q_spec] + tag_specs,
        out_specs=kv_spec,
        out_shape=jax.ShapeDtypeStruct((span, kv_width), jnp.bfloat16),
        cost_estimate=pl.CostEstimate(
            flops=4 * rows * GROUP * span * HD * heads,
            transcendentals=rows * GROUP * span * heads,
            bytes_accessed=2 * (2 * rows * q_width + 2 * span * kv_width),
        ),
    )(queries, keys, grads, query_tags, key_tags)


def fused_attention(queries, keys, values, grads, query_tags, key_tags):
    rows, q_width = queries.shape
    span, kv_width = keys.shape
    heads = kv_width // HD
    q_spec, kv_spec, tag_specs = head_specs(rows, span)
    return pl.pallas_call(
        attention_kernel,
        grid=(heads,),
        in_specs=[q_spec, kv_spec, kv_spec, q_spec] + tag_specs,
        out_specs=[q_spec, q_spec, kv_spec],
        out_shape=[
            jax.ShapeDtypeStruct((rows, q_width), jnp.bfloat16),
            jax.ShapeDtypeStruct((rows, q_width), jnp.bfloat16),
            jax.ShapeDtypeStruct((span, kv_width), jnp.bfloat16),
        ],
        cost_estimate=pl.CostEstimate(
            flops=10 * rows * GROUP * span * HD * heads,
            transcendentals=rows * GROUP * span * heads,
            bytes_accessed=2 * (4 * rows * q_width + 3 * span * kv_width),
        ),
    )(queries, keys, values, grads, query_tags, key_tags)


def peer_gather_kernel(axis, n, x_ref, o_ref, send_sem, recv_sem, local_sem):
    me = lax.axis_index(axis)
    barrier = pltpu.get_barrier_semaphore()
    for k in range(1, n):
        pl.semaphore_signal(
            barrier, inc=1, device_id={axis: lax.rem(me + k, n)}, device_id_type=pl.DeviceIdType.MESH
        )
    pl.semaphore_wait(barrier, n - 1)
    local = pltpu.make_async_copy(x_ref, o_ref.at[me], local_sem)
    local.start()
    copies = []
    for k in range(1, n):
        copy = pltpu.make_async_remote_copy(
            src_ref=x_ref,
            dst_ref=o_ref.at[me],
            send_sem=send_sem.at[k],
            recv_sem=recv_sem.at[k],
            device_id={axis: lax.rem(me + k, n)},
            device_id_type=pl.DeviceIdType.MESH,
        )
        copy.start()
        copies.append(copy)
    for copy in copies:
        copy.wait()
    local.wait()


def peer_gather(x, axis, collective_id):
    n = lax.axis_size(axis)
    return pl.pallas_call(
        functools.partial(peer_gather_kernel, axis, n),
        out_shape=jax.ShapeDtypeStruct((n,) + x.shape, x.dtype),
        in_specs=[pl.BlockSpec(memory_space=pl.ANY)],
        out_specs=pl.BlockSpec(memory_space=pl.ANY),
        scratch_shapes=[
            pltpu.SemaphoreType.DMA((n,)),
            pltpu.SemaphoreType.DMA((n,)),
            pltpu.SemaphoreType.DMA,
        ],
        compiler_params=pltpu.CompilerParams(collective_id=collective_id, has_side_effects=True),
    )(x)


def peer_sum_kernel(axis, n, x_ref, o_ref, landed, send_sem, recv_sem, local_sem):
    me = lax.axis_index(axis)
    barrier = pltpu.get_barrier_semaphore()
    for k in range(1, n):
        pl.semaphore_signal(
            barrier, inc=1, device_id={axis: lax.rem(me + k, n)}, device_id_type=pl.DeviceIdType.MESH
        )
    pl.semaphore_wait(barrier, n - 1)
    local = pltpu.make_async_copy(x_ref.at[me], landed.at[0], local_sem)
    local.start()
    copies = []
    for k in range(1, n):
        peer = lax.rem(me + k, n)
        copy = pltpu.make_async_remote_copy(
            src_ref=x_ref.at[peer],
            dst_ref=landed.at[k],
            send_sem=send_sem.at[k],
            recv_sem=recv_sem.at[k],
            device_id={axis: peer},
            device_id_type=pl.DeviceIdType.MESH,
        )
        copy.start()
        copies.append(copy)
    local.wait()
    total = landed[0].astype(jnp.float32)
    for k in range(1, n):
        copies[k - 1].wait()
        total = total + landed[k].astype(jnp.float32)
    o_ref[...] = total


def peer_sum_scatter(x, axis, collective_id):
    n = lax.axis_size(axis)
    return pl.pallas_call(
        functools.partial(peer_sum_kernel, axis, n),
        out_shape=jax.ShapeDtypeStruct(x.shape[1:], jnp.float32),
        in_specs=[pl.BlockSpec(memory_space=pl.ANY)],
        out_specs=pl.BlockSpec(memory_space=pltpu.VMEM),
        scratch_shapes=[
            pltpu.VMEM(x.shape, x.dtype),
            pltpu.SemaphoreType.DMA((n,)),
            pltpu.SemaphoreType.DMA((n,)),
            pltpu.SemaphoreType.DMA,
        ],
        compiler_params=pltpu.CompilerParams(collective_id=collective_id, has_side_effects=True),
    )(x)


def shifted(x, axis, by):
    length = lax.axis_size(axis)
    pairs = [(i, i + by) for i in range(length) if 0 <= i + by < length]
    return lax.ppermute(x, axis, pairs)


def shards(hidden, queries, key_heads, w_value, d_out, segments):
    shard_rows = hidden.shape[1]
    kv_width = w_value.shape[1]
    n_hops = WINDOW // shard_rows
    span_rows = (n_hops + 1) * shard_rows
    tokens_in = hidden[0]
    own_keys = key_heads[0]
    own_segments = segments[0]
    n_fsdp = lax.axis_size("fsdp")
    n_ctx = lax.axis_size("ctx")
    model_width = tokens_in.shape[1]
    half_rows = w_value.shape[0] // 2
    core = lax.axis_index("ctx") % 2
    w_mine = lax.all_gather(
        lax.dynamic_slice_in_dim(w_value, core * half_rows, half_rows, 0), "fsdp", axis=0, tiled=False
    )
    partner = [(i, i ^ 1) for i in range(n_ctx)]
    token_halves = tokens_in.reshape(shard_rows, n_fsdp, 2, half_rows)
    tokens_mine = lax.dynamic_index_in_dim(token_halves, core, axis=2, keepdims=False)
    partner_tokens = lax.ppermute(
        lax.dynamic_index_in_dim(token_halves, 1 - core, axis=2, keepdims=False), "ctx", partner
    )
    out_rows = model_width // (n_ctx * n_fsdp)
    token_cols = (
        tokens_in.reshape(shard_rows, n_ctx, n_fsdp, out_rows).transpose(2, 0, 1, 3)
    )
    token_cols = lax.all_to_all(token_cols, "fsdp", 0, 0, tiled=True)
    tag_columns = jnp.broadcast_to(own_segments.astype(jnp.bfloat16)[:, None], (shard_rows, HD))
    parcel = jnp.concatenate([own_keys, tag_columns], 1)
    arrived = [shifted(parcel, "ctx", hop) for hop in range(1, n_hops + 1)]
    window_parcel = jnp.concatenate(arrived[::-1] + [parcel], 0)
    window_parcel, token_cols = lax.optimization_barrier((window_parcel, token_cols))
    window_keys = window_parcel[:, :kv_width]
    window_tags = window_parcel[:, kv_width].astype(jnp.int32)
    first_query = lax.axis_index("ctx") * shard_rows
    key_pos = first_query - WINDOW + jnp.arange(span_rows, dtype=jnp.int32)
    key_tags = jnp.where(key_pos >= 0, window_tags, -1)
    query_tags = own_segments.astype(jnp.int32)[:, None]
    own_start = n_hops * shard_rows

    def returned_sum(terms):
        total = terms[own_start:].astype(jnp.float32)
        for hop in range(1, n_hops + 1):
            low_edge = (n_hops - hop) * shard_rows
            total = total + shifted(terms[low_edge : low_edge + shard_rows], "ctx", -hop).astype(jnp.float32)
        return total.astype(jnp.bfloat16)

    value_terms = value_grads(queries[0], window_keys, d_out[0], query_tags, key_tags[None, :])
    d_values_low = returned_sum(value_terms)
    w_mine, _ = lax.optimization_barrier((w_mine, d_values_low))
    grads_all = lax.all_gather(d_values_low, "fsdp", axis=0, tiled=False)

    partner_part = jnp.einsum("tfr,frn->tn", partner_tokens, w_mine, preferred_element_type=jnp.float32)
    values = (
        jnp.einsum("tfr,frn->tn", tokens_mine, w_mine, preferred_element_type=jnp.float32)
        + lax.ppermute(partner_part, "ctx", partner)
    ).astype(jnp.bfloat16)
    arrived_values = [shifted(values, "ctx", hop) for hop in range(1, n_hops + 1)]
    window_values = jnp.concatenate(arrived_values[::-1] + [values], 0)
    out_rows_attn, d_query_heads, key_terms = fused_attention(
        queries[0], window_keys, window_values, d_out[0], query_tags, key_tags[None, :]
    )
    d_key_rows = returned_sum(key_terms)
    grads_all, _ = lax.optimization_barrier((grads_all, key_terms))
    weight_part = jnp.einsum(
        "ftcr,ftn->crn", token_cols, grads_all, preferred_element_type=jnp.float32
    )
    d_weight = peer_sum_scatter(weight_part.astype(jnp.bfloat16), "ctx", 3)
    d_mine = jnp.einsum("tn,frn->tfr", d_values_low, w_mine, preferred_element_type=jnp.float32).astype(jnp.bfloat16)
    partner_grads = lax.ppermute(d_values_low, "ctx", partner)
    d_other = lax.ppermute(
        jnp.einsum("tn,frn->tfr", partner_grads, w_mine, preferred_element_type=jnp.float32).astype(jnp.bfloat16),
        "ctx",
        partner,
    )
    d_tokens = jnp.where(
        core == 0, jnp.stack([d_mine, d_other], 2), jnp.stack([d_other, d_mine], 2)
    ).reshape(shard_rows, model_width)
    return (
        out_rows_attn[None],
        d_query_heads[None],
        d_key_rows[None],
        d_tokens[None],
        d_weight,
    )


def solution(mesh):
    in_specs = (
        P("fsdp", "ctx", None),
        P("fsdp", "ctx", None),
        P("fsdp", "ctx", None),
        P("fsdp", None),
        P("fsdp", "ctx", None),
        P("fsdp", "ctx"),
    )
    out_specs = (
        P("fsdp", "ctx", None),
        P("fsdp", "ctx", None),
        P("fsdp", "ctx", None),
        P("fsdp", "ctx", None),
        P(("ctx", "fsdp"), None),
    )
    return jax.shard_map(shards, mesh=mesh, in_specs=in_specs, out_specs=out_specs, check_vma=False)
```

```python
import functools
import math

import jax
import jax.numpy as jnp
from jax import lax
from jax.experimental import pallas as pl
from jax.experimental.pallas import tpu as pltpu
from jax.sharding import PartitionSpec as P

HQ = 16
HK = 8
HD = 128
WINDOW = 1024
GROUP = 2


score_scale = 1.0 / math.sqrt(168.0)


def window_probs(q, keys, qtag_ref, ktag_ref):
    rows = qtag_ref.shape[0]
    span = keys.shape[0]
    reach = span - rows
    t_idx = lax.broadcasted_iota(jnp.int32, (rows, span), 0)
    l_idx = lax.broadcasted_iota(jnp.int32, (rows, span), 1)
    allowed = (qtag_ref[...] == ktag_ref[...]) & (l_idx > t_idx) & (l_idx <= t_idx + reach)
    allowed = jnp.concatenate([allowed] * GROUP, axis=0)
    scores = lax.dot_general(q, keys, (((1,), (1,)), ((), ())), preferred_element_type=jnp.float32) * score_scale
    scores = jnp.where(allowed, scores, -jnp.inf)
    highest = jnp.max(scores, axis=-1, keepdims=True)
    raw = jnp.exp(scores - highest)
    return raw / jnp.sum(raw, axis=-1, keepdims=True)


def stacked_heads(ref):
    return jnp.concatenate([ref[:, r * HD:(r + 1) * HD] for r in range(GROUP)], axis=0)


def value_grad_kernel(q_ref, k_ref, do_ref, qtag_ref, ktag_ref, dv_ref):
    probs_low = window_probs(stacked_heads(q_ref), k_ref[...], qtag_ref, ktag_ref).astype(jnp.bfloat16)
    grad = stacked_heads(do_ref)
    dv = lax.dot_general(probs_low, grad, (((0,), (0,)), ((), ())), preferred_element_type=jnp.float32)
    dv_ref[...] = dv.astype(jnp.bfloat16)


def attention_kernel(q_ref, k_ref, v_ref, do_ref, qtag_ref, ktag_ref, out_ref, dq_ref, dk_ref):
    rows = q_ref.shape[0]
    q = stacked_heads(q_ref)
    grad = stacked_heads(do_ref)
    keys = k_ref[...]
    vals = v_ref[...]
    probs = window_probs(q, keys, qtag_ref, ktag_ref)
    probs_low = probs.astype(jnp.bfloat16)
    out = jnp.dot(probs_low, vals, preferred_element_type=jnp.float32).astype(jnp.bfloat16)
    grad_probs = lax.dot_general(grad, vals, (((1,), (1,)), ((), ())), preferred_element_type=jnp.float32)
    delta = jnp.sum(grad.astype(jnp.float32) * out.astype(jnp.float32), axis=-1, keepdims=True)
    grad_scores = (probs * (grad_probs - delta)).astype(jnp.bfloat16)
    dq = (score_scale * jnp.dot(grad_scores, keys, preferred_element_type=jnp.float32)).astype(jnp.bfloat16)
    dk = score_scale * lax.dot_general(grad_scores, q, (((0,), (0,)), ((), ())), preferred_element_type=jnp.float32)
    for r in range(GROUP):
        out_ref[:, r * HD:(r + 1) * HD] = out[r * rows:(r + 1) * rows]
        dq_ref[:, r * HD:(r + 1) * HD] = dq[r * rows:(r + 1) * rows]
    dk_ref[...] = dk.astype(jnp.bfloat16)


def head_specs(rows, span):
    q_spec = pl.BlockSpec((rows, GROUP * HD), lambda g: (0, g))
    kv_spec = pl.BlockSpec((span, HD), lambda g: (0, g))
    tag_specs = [pl.BlockSpec((rows, 1), lambda g: (0, 0)), pl.BlockSpec((1, span), lambda g: (0, 0))]
    return q_spec, kv_spec, tag_specs


def value_grads(queries, keys, grads, query_tags, key_tags):
    rows, q_width = queries.shape
    span, kv_width = keys.shape
    heads = kv_width // HD
    q_spec, kv_spec, tag_specs = head_specs(rows, span)
    return pl.pallas_call(
        value_grad_kernel,
        grid=(heads,),
        in_specs=[q_spec, kv_spec, q_spec] + tag_specs,
        out_specs=kv_spec,
        out_shape=jax.ShapeDtypeStruct((span, kv_width), jnp.bfloat16),
        cost_estimate=pl.CostEstimate(
            flops=4 * rows * GROUP * span * HD * heads,
            transcendentals=rows * GROUP * span * heads,
            bytes_accessed=2 * (2 * rows * q_width + 2 * span * kv_width),
        ),
    )(queries, keys, grads, query_tags, key_tags)


def fused_attention(queries, keys, values, grads, query_tags, key_tags):
    rows, q_width = queries.shape
    span, kv_width = keys.shape
    heads = kv_width // HD
    q_spec, kv_spec, tag_specs = head_specs(rows, span)
    return pl.pallas_call(
        attention_kernel,
        grid=(heads,),
        in_specs=[q_spec, kv_spec, kv_spec, q_spec] + tag_specs,
        out_specs=[q_spec, q_spec, kv_spec],
        out_shape=[
            jax.ShapeDtypeStruct((rows, q_width), jnp.bfloat16),
            jax.ShapeDtypeStruct((rows, q_width), jnp.bfloat16),
            jax.ShapeDtypeStruct((span, kv_width), jnp.bfloat16),
        ],
        cost_estimate=pl.CostEstimate(
            flops=10 * rows * GROUP * span * HD * heads,
            transcendentals=rows * GROUP * span * heads,
            bytes_accessed=2 * (4 * rows * q_width + 3 * span * kv_width),
        ),
    )(queries, keys, values, grads, query_tags, key_tags)


def peer_gather_kernel(axis, n, x_ref, o_ref, send_sem, recv_sem, local_sem):
    me = lax.axis_index(axis)
    barrier = pltpu.get_barrier_semaphore()
    for k in range(1, n):
        pl.semaphore_signal(
            barrier, inc=1, device_id={axis: lax.rem(me + k, n)}, device_id_type=pl.DeviceIdType.MESH
        )
    pl.semaphore_wait(barrier, n - 1)
    local = pltpu.make_async_copy(x_ref, o_ref.at[me], local_sem)
    local.start()
    copies = []
    for k in range(1, n):
        copy = pltpu.make_async_remote_copy(
            src_ref=x_ref,
            dst_ref=o_ref.at[me],
            send_sem=send_sem.at[k],
            recv_sem=recv_sem.at[k],
            device_id={axis: lax.rem(me + k, n)},
            device_id_type=pl.DeviceIdType.MESH,
        )
        copy.start()
        copies.append(copy)
    for copy in copies:
        copy.wait()
    local.wait()


def peer_gather(x, axis, collective_id):
    n = lax.axis_size(axis)
    return pl.pallas_call(
        functools.partial(peer_gather_kernel, axis, n),
        out_shape=jax.ShapeDtypeStruct((n,) + x.shape, x.dtype),
        in_specs=[pl.BlockSpec(memory_space=pl.ANY)],
        out_specs=pl.BlockSpec(memory_space=pl.ANY),
        scratch_shapes=[
            pltpu.SemaphoreType.DMA((n,)),
            pltpu.SemaphoreType.DMA((n,)),
            pltpu.SemaphoreType.DMA,
        ],
        compiler_params=pltpu.CompilerParams(collective_id=collective_id, has_side_effects=True),
    )(x)


def peer_sum_kernel(axis, n, x_ref, o_ref, landed, send_sem, recv_sem, local_sem):
    me = lax.axis_index(axis)
    barrier = pltpu.get_barrier_semaphore()
    for k in range(1, n):
        pl.semaphore_signal(
            barrier, inc=1, device_id={axis: lax.rem(me + k, n)}, device_id_type=pl.DeviceIdType.MESH
        )
    pl.semaphore_wait(barrier, n - 1)
    local = pltpu.make_async_copy(x_ref.at[me], landed.at[0], local_sem)
    local.start()
    copies = []
    for k in range(1, n):
        peer = lax.rem(me + k, n)
        copy = pltpu.make_async_remote_copy(
            src_ref=x_ref.at[peer],
            dst_ref=landed.at[k],
            send_sem=send_sem.at[k],
            recv_sem=recv_sem.at[k],
            device_id={axis: peer},
            device_id_type=pl.DeviceIdType.MESH,
        )
        copy.start()
        copies.append(copy)
    local.wait()
    total = landed[0].astype(jnp.float32)
    for k in range(1, n):
        copies[k - 1].wait()
        total = total + landed[k].astype(jnp.float32)
    o_ref[...] = total


def peer_sum_scatter(x, axis, collective_id):
    n = lax.axis_size(axis)
    return pl.pallas_call(
        functools.partial(peer_sum_kernel, axis, n),
        out_shape=jax.ShapeDtypeStruct(x.shape[1:], jnp.float32),
        in_specs=[pl.BlockSpec(memory_space=pl.ANY)],
        out_specs=pl.BlockSpec(memory_space=pltpu.VMEM),
        scratch_shapes=[
            pltpu.VMEM(x.shape, x.dtype),
            pltpu.SemaphoreType.DMA((n,)),
            pltpu.SemaphoreType.DMA((n,)),
            pltpu.SemaphoreType.DMA,
        ],
        compiler_params=pltpu.CompilerParams(collective_id=collective_id, has_side_effects=True),
    )(x)


def shifted(x, axis, by):
    length = lax.axis_size(axis)
    pairs = [(i, i + by) for i in range(length) if 0 <= i + by < length]
    return lax.ppermute(x, axis, pairs)


def shards(hidden, queries, key_heads, w_value, d_out, segments):
    shard_rows = hidden.shape[1]
    kv_width = w_value.shape[1]
    n_hops = WINDOW // shard_rows
    span_rows = (n_hops + 1) * shard_rows
    tokens_in = hidden[0]
    own_keys = key_heads[0]
    own_segments = segments[0]
    n_fsdp = lax.axis_size("fsdp")
    n_ctx = lax.axis_size("ctx")
    model_width = tokens_in.shape[1]
    half_rows = w_value.shape[0] // 2
    core = lax.axis_index("ctx") % 2
    w_mine = lax.all_gather(
        lax.dynamic_slice_in_dim(w_value, core * half_rows, half_rows, 0), "fsdp", axis=0, tiled=False
    )
    partner = [(i, i ^ 1) for i in range(n_ctx)]
    token_halves = tokens_in.reshape(shard_rows, n_fsdp, 2, half_rows)
    tokens_mine = lax.dynamic_index_in_dim(token_halves, core, axis=2, keepdims=False)
    partner_tokens = lax.ppermute(
        lax.dynamic_index_in_dim(token_halves, 1 - core, axis=2, keepdims=False), "ctx", partner
    )
    out_rows = model_width // (n_ctx * n_fsdp)
    token_cols = (
        tokens_in.reshape(shard_rows, n_ctx, n_fsdp, out_rows).transpose(2, 0, 1, 3)
    )
    token_cols = lax.all_to_all(token_cols, "fsdp", 0, 0, tiled=True)
    tag_columns = jnp.broadcast_to(own_segments.astype(jnp.bfloat16)[:, None], (shard_rows, HD))
    parcel = jnp.concatenate([own_keys, tag_columns], 1)
    arrived = [shifted(parcel, "ctx", hop) for hop in range(1, n_hops + 1)]
    window_parcel = jnp.concatenate(arrived[::-1] + [parcel], 0)
    window_parcel, partner_tokens = lax.optimization_barrier((window_parcel, partner_tokens))
    window_keys = window_parcel[:, :kv_width]
    window_tags = window_parcel[:, kv_width].astype(jnp.int32)
    first_query = lax.axis_index("ctx") * shard_rows
    key_pos = first_query - WINDOW + jnp.arange(span_rows, dtype=jnp.int32)
    key_tags = jnp.where(key_pos >= 0, window_tags, -1)
    query_tags = own_segments.astype(jnp.int32)[:, None]
    own_start = n_hops * shard_rows

    def returned_sum(terms):
        total = terms[own_start:].astype(jnp.float32)
        for hop in range(1, n_hops + 1):
            low_edge = (n_hops - hop) * shard_rows
            total = total + shifted(terms[low_edge : low_edge + shard_rows], "ctx", -hop).astype(jnp.float32)
        return total.astype(jnp.bfloat16)

    value_terms = value_grads(queries[0], window_keys, d_out[0], query_tags, key_tags[None, :])
    d_values_low = returned_sum(value_terms)
    w_mine, _ = lax.optimization_barrier((w_mine, d_values_low))
    grads_all = lax.all_gather(d_values_low, "fsdp", axis=0, tiled=False)

    partner_part = jnp.einsum("tfr,frn->tn", partner_tokens, w_mine, preferred_element_type=jnp.float32)
    values = (
        jnp.einsum("tfr,frn->tn", tokens_mine, w_mine, preferred_element_type=jnp.float32)
        + lax.ppermute(partner_part, "ctx", partner)
    ).astype(jnp.bfloat16)
    arrived_values = [shifted(values, "ctx", hop) for hop in range(1, n_hops + 1)]
    window_values = jnp.concatenate(arrived_values[::-1] + [values], 0)
    out_rows_attn, d_query_heads, key_terms = fused_attention(
        queries[0], window_keys, window_values, d_out[0], query_tags, key_tags[None, :]
    )
    d_key_rows = returned_sum(key_terms)
    grads_all, _ = lax.optimization_barrier((grads_all, key_terms))
    weight_part = jnp.einsum(
        "ftcr,ftn->crn", token_cols, grads_all, preferred_element_type=jnp.float32
    )
    d_weight = peer_sum_scatter(weight_part.astype(jnp.bfloat16), "ctx", 3)
    d_mine = jnp.einsum("tn,frn->tfr", d_values_low, w_mine, preferred_element_type=jnp.float32).astype(jnp.bfloat16)
    partner_grads = lax.ppermute(d_values_low, "ctx", partner)
    d_other = lax.ppermute(
        jnp.einsum("tn,frn->tfr", partner_grads, w_mine, preferred_element_type=jnp.float32).astype(jnp.bfloat16),
        "ctx",
        partner,
    )
    d_tokens = jnp.where(
        core == 0, jnp.stack([d_mine, d_other], 2), jnp.stack([d_other, d_mine], 2)
    ).reshape(shard_rows, model_width)
    return (
        out_rows_attn[None],
        d_query_heads[None],
        d_key_rows[None],
        d_tokens[None],
        d_weight,
    )


def solution(mesh):
    in_specs = (
        P("fsdp", "ctx", None),
        P("fsdp", "ctx", None),
        P("fsdp", "ctx", None),
        P("fsdp", None),
        P("fsdp", "ctx", None),
        P("fsdp", "ctx"),
    )
    out_specs = (
        P("fsdp", "ctx", None),
        P("fsdp", "ctx", None),
        P("fsdp", "ctx", None),
        P("fsdp", "ctx", None),
        P(("ctx", "fsdp"), None),
    )
    return jax.shard_map(shards, mesh=mesh, in_specs=in_specs, out_specs=out_specs, check_vma=False)
```

```python
import functools
import math

import jax
import jax.numpy as jnp
from jax import lax
from jax.experimental import pallas as pl
from jax.experimental.pallas import tpu as pltpu
from jax.sharding import PartitionSpec as P

HQ = 16
HK = 8
HD = 128
WINDOW = 1024
GROUP = 2


score_scale = 1.0 / math.sqrt(168.0)


def window_probs(q, keys, qtag_ref, ktag_ref):
    rows = qtag_ref.shape[0]
    span = keys.shape[0]
    reach = span - rows
    t_idx = lax.broadcasted_iota(jnp.int32, (rows, span), 0)
    l_idx = lax.broadcasted_iota(jnp.int32, (rows, span), 1)
    allowed = (qtag_ref[...] == ktag_ref[...]) & (l_idx > t_idx) & (l_idx <= t_idx + reach)
    allowed = jnp.concatenate([allowed] * GROUP, axis=0)
    scores = lax.dot_general(q, keys, (((1,), (1,)), ((), ())), preferred_element_type=jnp.float32) * score_scale
    scores = jnp.where(allowed, scores, -jnp.inf)
    highest = jnp.max(scores, axis=-1, keepdims=True)
    raw = jnp.exp(scores - highest)
    return raw / jnp.sum(raw, axis=-1, keepdims=True)


def stacked_heads(ref):
    return jnp.concatenate([ref[:, r * HD:(r + 1) * HD] for r in range(GROUP)], axis=0)


def value_grad_kernel(q_ref, k_ref, do_ref, qtag_ref, ktag_ref, dv_ref):
    probs_low = window_probs(stacked_heads(q_ref), k_ref[...], qtag_ref, ktag_ref).astype(jnp.bfloat16)
    grad = stacked_heads(do_ref)
    dv = lax.dot_general(probs_low, grad, (((0,), (0,)), ((), ())), preferred_element_type=jnp.float32)
    dv_ref[...] = dv.astype(jnp.bfloat16)


def attention_kernel(q_ref, k_ref, v_ref, do_ref, qtag_ref, ktag_ref, out_ref, dq_ref, dk_ref):
    rows = q_ref.shape[0]
    q = stacked_heads(q_ref)
    grad = stacked_heads(do_ref)
    keys = k_ref[...]
    vals = v_ref[...]
    probs = window_probs(q, keys, qtag_ref, ktag_ref)
    probs_low = probs.astype(jnp.bfloat16)
    out = jnp.dot(probs_low, vals, preferred_element_type=jnp.float32).astype(jnp.bfloat16)
    grad_probs = lax.dot_general(grad, vals, (((1,), (1,)), ((), ())), preferred_element_type=jnp.float32)
    delta = jnp.sum(grad.astype(jnp.float32) * out.astype(jnp.float32), axis=-1, keepdims=True)
    grad_scores = (probs * (grad_probs - delta)).astype(jnp.bfloat16)
    dq = (score_scale * jnp.dot(grad_scores, keys, preferred_element_type=jnp.float32)).astype(jnp.bfloat16)
    dk = score_scale * lax.dot_general(grad_scores, q, (((0,), (0,)), ((), ())), preferred_element_type=jnp.float32)
    for r in range(GROUP):
        out_ref[:, r * HD:(r + 1) * HD] = out[r * rows:(r + 1) * rows]
        dq_ref[:, r * HD:(r + 1) * HD] = dq[r * rows:(r + 1) * rows]
    dk_ref[...] = dk.astype(jnp.bfloat16)


def head_specs(rows, span):
    q_spec = pl.BlockSpec((rows, GROUP * HD), lambda g: (0, g))
    kv_spec = pl.BlockSpec((span, HD), lambda g: (0, g))
    tag_specs = [pl.BlockSpec((rows, 1), lambda g: (0, 0)), pl.BlockSpec((1, span), lambda g: (0, 0))]
    return q_spec, kv_spec, tag_specs


def value_grads(queries, keys, grads, query_tags, key_tags):
    rows, q_width = queries.shape
    span, kv_width = keys.shape
    heads = kv_width // HD
    q_spec, kv_spec, tag_specs = head_specs(rows, span)
    return pl.pallas_call(
        value_grad_kernel,
        grid=(heads,),
        in_specs=[q_spec, kv_spec, q_spec] + tag_specs,
        out_specs=kv_spec,
        out_shape=jax.ShapeDtypeStruct((span, kv_width), jnp.bfloat16),
        cost_estimate=pl.CostEstimate(
            flops=4 * rows * GROUP * span * HD * heads,
            transcendentals=rows * GROUP * span * heads,
            bytes_accessed=2 * (2 * rows * q_width + 2 * span * kv_width),
        ),
    )(queries, keys, grads, query_tags, key_tags)


def fused_attention(queries, keys, values, grads, query_tags, key_tags):
    rows, q_width = queries.shape
    span, kv_width = keys.shape
    heads = kv_width // HD
    q_spec, kv_spec, tag_specs = head_specs(rows, span)
    return pl.pallas_call(
        attention_kernel,
        grid=(heads,),
        in_specs=[q_spec, kv_spec, kv_spec, q_spec] + tag_specs,
        out_specs=[q_spec, q_spec, kv_spec],
        out_shape=[
            jax.ShapeDtypeStruct((rows, q_width), jnp.bfloat16),
            jax.ShapeDtypeStruct((rows, q_width), jnp.bfloat16),
            jax.ShapeDtypeStruct((span, kv_width), jnp.bfloat16),
        ],
        cost_estimate=pl.CostEstimate(
            flops=10 * rows * GROUP * span * HD * heads,
            transcendentals=rows * GROUP * span * heads,
            bytes_accessed=2 * (4 * rows * q_width + 3 * span * kv_width),
        ),
    )(queries, keys, values, grads, query_tags, key_tags)


def peer_gather_kernel(axis, n, x_ref, o_ref, send_sem, recv_sem, local_sem):
    me = lax.axis_index(axis)
    barrier = pltpu.get_barrier_semaphore()
    for k in range(1, n):
        pl.semaphore_signal(
            barrier, inc=1, device_id={axis: lax.rem(me + k, n)}, device_id_type=pl.DeviceIdType.MESH
        )
    pl.semaphore_wait(barrier, n - 1)
    local = pltpu.make_async_copy(x_ref, o_ref.at[me], local_sem)
    local.start()
    copies = []
    for k in range(1, n):
        copy = pltpu.make_async_remote_copy(
            src_ref=x_ref,
            dst_ref=o_ref.at[me],
            send_sem=send_sem.at[k],
            recv_sem=recv_sem.at[k],
            device_id={axis: lax.rem(me + k, n)},
            device_id_type=pl.DeviceIdType.MESH,
        )
        copy.start()
        copies.append(copy)
    for copy in copies:
        copy.wait()
    local.wait()


def peer_gather(x, axis, collective_id):
    n = lax.axis_size(axis)
    return pl.pallas_call(
        functools.partial(peer_gather_kernel, axis, n),
        out_shape=jax.ShapeDtypeStruct((n,) + x.shape, x.dtype),
        in_specs=[pl.BlockSpec(memory_space=pl.ANY)],
        out_specs=pl.BlockSpec(memory_space=pl.ANY),
        scratch_shapes=[
            pltpu.SemaphoreType.DMA((n,)),
            pltpu.SemaphoreType.DMA((n,)),
            pltpu.SemaphoreType.DMA,
        ],
        compiler_params=pltpu.CompilerParams(collective_id=collective_id, has_side_effects=True),
    )(x)


def peer_sum_kernel(axis, n, x_ref, o_ref, landed, send_sem, recv_sem, local_sem):
    me = lax.axis_index(axis)
    barrier = pltpu.get_barrier_semaphore()
    for k in range(1, n):
        pl.semaphore_signal(
            barrier, inc=1, device_id={axis: lax.rem(me + k, n)}, device_id_type=pl.DeviceIdType.MESH
        )
    pl.semaphore_wait(barrier, n - 1)
    local = pltpu.make_async_copy(x_ref.at[me], landed.at[0], local_sem)
    local.start()
    copies = []
    for k in range(1, n):
        peer = lax.rem(me + k, n)
        copy = pltpu.make_async_remote_copy(
            src_ref=x_ref.at[peer],
            dst_ref=landed.at[k],
            send_sem=send_sem.at[k],
            recv_sem=recv_sem.at[k],
            device_id={axis: peer},
            device_id_type=pl.DeviceIdType.MESH,
        )
        copy.start()
        copies.append(copy)
    local.wait()
    total = landed[0].astype(jnp.float32)
    for k in range(1, n):
        copies[k - 1].wait()
        total = total + landed[k].astype(jnp.float32)
    o_ref[...] = total


def peer_sum_scatter(x, axis, collective_id):
    n = lax.axis_size(axis)
    return pl.pallas_call(
        functools.partial(peer_sum_kernel, axis, n),
        out_shape=jax.ShapeDtypeStruct(x.shape[1:], jnp.float32),
        in_specs=[pl.BlockSpec(memory_space=pl.ANY)],
        out_specs=pl.BlockSpec(memory_space=pltpu.VMEM),
        scratch_shapes=[
            pltpu.VMEM(x.shape, x.dtype),
            pltpu.SemaphoreType.DMA((n,)),
            pltpu.SemaphoreType.DMA((n,)),
            pltpu.SemaphoreType.DMA,
        ],
        compiler_params=pltpu.CompilerParams(collective_id=collective_id, has_side_effects=True),
    )(x)


def shifted(x, axis, by):
    length = lax.axis_size(axis)
    pairs = [(i, i + by) for i in range(length) if 0 <= i + by < length]
    return lax.ppermute(x, axis, pairs)


def shards(hidden, queries, key_heads, w_value, d_out, segments):
    shard_rows = hidden.shape[1]
    kv_width = w_value.shape[1]
    n_hops = WINDOW // shard_rows
    span_rows = (n_hops + 1) * shard_rows
    tokens_in = hidden[0]
    own_keys = key_heads[0]
    own_segments = segments[0]
    n_fsdp = lax.axis_size("fsdp")
    n_ctx = lax.axis_size("ctx")
    model_width = tokens_in.shape[1]
    half_rows = w_value.shape[0] // 2
    core = lax.axis_index("ctx") % 2
    w_mine = lax.all_gather(
        lax.dynamic_slice_in_dim(w_value, core * half_rows, half_rows, 0), "fsdp", axis=0, tiled=False
    )
    partner = [(i, i ^ 1) for i in range(n_ctx)]
    token_halves = tokens_in.reshape(shard_rows, n_fsdp, 2, half_rows)
    tokens_mine = lax.dynamic_index_in_dim(token_halves, core, axis=2, keepdims=False)
    partner_tokens = lax.ppermute(
        lax.dynamic_index_in_dim(token_halves, 1 - core, axis=2, keepdims=False), "ctx", partner
    )
    out_rows = model_width // (n_ctx * n_fsdp)
    token_cols = (
        tokens_in.reshape(shard_rows, n_ctx, n_fsdp, out_rows).transpose(2, 0, 1, 3)
    )
    tag_columns = jnp.broadcast_to(own_segments.astype(jnp.bfloat16)[:, None], (shard_rows, HD))
    parcel = jnp.concatenate([own_keys, tag_columns], 1)
    arrived = [shifted(parcel, "ctx", hop) for hop in range(1, n_hops + 1)]
    window_parcel = jnp.concatenate(arrived[::-1] + [parcel], 0)
    window_parcel, partner_tokens, token_cols = lax.optimization_barrier(
        (window_parcel, partner_tokens, token_cols)
    )
    window_keys = window_parcel[:, :kv_width]
    window_tags = window_parcel[:, kv_width].astype(jnp.int32)
    first_query = lax.axis_index("ctx") * shard_rows
    key_pos = first_query - WINDOW + jnp.arange(span_rows, dtype=jnp.int32)
    key_tags = jnp.where(key_pos >= 0, window_tags, -1)
    query_tags = own_segments.astype(jnp.int32)[:, None]
    own_start = n_hops * shard_rows

    def returned_sum(terms):
        total = terms[own_start:].astype(jnp.float32)
        for hop in range(1, n_hops + 1):
            low_edge = (n_hops - hop) * shard_rows
            total = total + shifted(terms[low_edge : low_edge + shard_rows], "ctx", -hop).astype(jnp.float32)
        return total.astype(jnp.bfloat16)

    value_terms = value_grads(queries[0], window_keys, d_out[0], query_tags, key_tags[None, :])
    d_values_low = returned_sum(value_terms)
    w_mine, _ = lax.optimization_barrier((w_mine, d_values_low))
    grads_all = lax.all_gather(d_values_low, "fsdp", axis=0, tiled=False)

    partner_part = jnp.einsum("tfr,frn->tn", partner_tokens, w_mine, preferred_element_type=jnp.float32)
    values = (
        jnp.einsum("tfr,frn->tn", tokens_mine, w_mine, preferred_element_type=jnp.float32)
        + lax.ppermute(partner_part, "ctx", partner)
    ).astype(jnp.bfloat16)
    arrived_values = [shifted(values, "ctx", hop) for hop in range(1, n_hops + 1)]
    token_cols, _ = lax.optimization_barrier((token_cols, values))
    token_cols = lax.all_to_all(token_cols, "fsdp", 0, 0, tiled=True)
    window_values = jnp.concatenate(arrived_values[::-1] + [values], 0)
    out_rows_attn, d_query_heads, key_terms = fused_attention(
        queries[0], window_keys, window_values, d_out[0], query_tags, key_tags[None, :]
    )
    d_key_rows = returned_sum(key_terms)
    grads_all, _ = lax.optimization_barrier((grads_all, key_terms))
    weight_part = jnp.einsum(
        "ftcr,ftn->crn", token_cols, grads_all, preferred_element_type=jnp.float32
    )
    d_weight = peer_sum_scatter(weight_part.astype(jnp.bfloat16), "ctx", 3)
    d_mine = jnp.einsum("tn,frn->tfr", d_values_low, w_mine, preferred_element_type=jnp.float32).astype(jnp.bfloat16)
    partner_grads = lax.ppermute(d_values_low, "ctx", partner)
    d_other = lax.ppermute(
        jnp.einsum("tn,frn->tfr", partner_grads, w_mine, preferred_element_type=jnp.float32).astype(jnp.bfloat16),
        "ctx",
        partner,
    )
    d_tokens = jnp.where(
        core == 0, jnp.stack([d_mine, d_other], 2), jnp.stack([d_other, d_mine], 2)
    ).reshape(shard_rows, model_width)
    return (
        out_rows_attn[None],
        d_query_heads[None],
        d_key_rows[None],
        d_tokens[None],
        d_weight,
    )


def solution(mesh):
    in_specs = (
        P("fsdp", "ctx", None),
        P("fsdp", "ctx", None),
        P("fsdp", "ctx", None),
        P("fsdp", None),
        P("fsdp", "ctx", None),
        P("fsdp", "ctx"),
    )
    out_specs = (
        P("fsdp", "ctx", None),
        P("fsdp", "ctx", None),
        P("fsdp", "ctx", None),
        P("fsdp", "ctx", None),
        P(("ctx", "fsdp"), None),
    )
    return jax.shard_map(shards, mesh=mesh, in_specs=in_specs, out_specs=out_specs, check_vma=False)
```

```python
import functools
import math

import jax
import jax.numpy as jnp
from jax import lax
from jax.experimental import pallas as pl
from jax.experimental.pallas import tpu as pltpu
from jax.sharding import PartitionSpec as P

HQ = 16
HK = 8
HD = 128
WINDOW = 1024
GROUP = 2


score_scale = 1.0 / math.sqrt(168.0)


def window_probs(q, keys, qtag_ref, ktag_ref):
    rows = qtag_ref.shape[0]
    span = keys.shape[0]
    reach = span - rows
    t_idx = lax.broadcasted_iota(jnp.int32, (rows, span), 0)
    l_idx = lax.broadcasted_iota(jnp.int32, (rows, span), 1)
    allowed = (qtag_ref[...] == ktag_ref[...]) & (l_idx > t_idx) & (l_idx <= t_idx + reach)
    allowed = jnp.concatenate([allowed] * GROUP, axis=0)
    scores = lax.dot_general(q, keys, (((1,), (1,)), ((), ())), preferred_element_type=jnp.float32) * score_scale
    scores = jnp.where(allowed, scores, -jnp.inf)
    highest = jnp.max(scores, axis=-1, keepdims=True)
    raw = jnp.exp(scores - highest)
    return raw / jnp.sum(raw, axis=-1, keepdims=True)


def stacked_heads(ref):
    return jnp.concatenate([ref[:, r * HD:(r + 1) * HD] for r in range(GROUP)], axis=0)


def value_grad_kernel(q_ref, k_ref, do_ref, qtag_ref, ktag_ref, dv_ref):
    probs_low = window_probs(stacked_heads(q_ref), k_ref[...], qtag_ref, ktag_ref).astype(jnp.bfloat16)
    grad = stacked_heads(do_ref)
    dv = lax.dot_general(probs_low, grad, (((0,), (0,)), ((), ())), preferred_element_type=jnp.float32)
    dv_ref[...] = dv.astype(jnp.bfloat16)


def attention_kernel(q_ref, k_ref, v_ref, do_ref, qtag_ref, ktag_ref, out_ref, dq_ref, dk_ref):
    rows = q_ref.shape[0]
    q = stacked_heads(q_ref)
    grad = stacked_heads(do_ref)
    keys = k_ref[...]
    vals = v_ref[...]
    probs = window_probs(q, keys, qtag_ref, ktag_ref)
    probs_low = probs.astype(jnp.bfloat16)
    out = jnp.dot(probs_low, vals, preferred_element_type=jnp.float32).astype(jnp.bfloat16)
    grad_probs = lax.dot_general(grad, vals, (((1,), (1,)), ((), ())), preferred_element_type=jnp.float32)
    delta = jnp.sum(grad.astype(jnp.float32) * out.astype(jnp.float32), axis=-1, keepdims=True)
    grad_scores = (probs * (grad_probs - delta)).astype(jnp.bfloat16)
    dq = (score_scale * jnp.dot(grad_scores, keys, preferred_element_type=jnp.float32)).astype(jnp.bfloat16)
    dk = score_scale * lax.dot_general(grad_scores, q, (((0,), (0,)), ((), ())), preferred_element_type=jnp.float32)
    for r in range(GROUP):
        out_ref[:, r * HD:(r + 1) * HD] = out[r * rows:(r + 1) * rows]
        dq_ref[:, r * HD:(r + 1) * HD] = dq[r * rows:(r + 1) * rows]
    dk_ref[...] = dk.astype(jnp.bfloat16)


def head_specs(rows, span):
    q_spec = pl.BlockSpec((rows, GROUP * HD), lambda g: (0, g))
    kv_spec = pl.BlockSpec((span, HD), lambda g: (0, g))
    tag_specs = [pl.BlockSpec((rows, 1), lambda g: (0, 0)), pl.BlockSpec((1, span), lambda g: (0, 0))]
    return q_spec, kv_spec, tag_specs


def value_grads(queries, keys, grads, query_tags, key_tags):
    rows, q_width = queries.shape
    span, kv_width = keys.shape
    heads = kv_width // HD
    q_spec, kv_spec, tag_specs = head_specs(rows, span)
    return pl.pallas_call(
        value_grad_kernel,
        grid=(heads,),
        in_specs=[q_spec, kv_spec, q_spec] + tag_specs,
        out_specs=kv_spec,
        out_shape=jax.ShapeDtypeStruct((span, kv_width), jnp.bfloat16),
        cost_estimate=pl.CostEstimate(
            flops=4 * rows * GROUP * span * HD * heads,
            transcendentals=rows * GROUP * span * heads,
            bytes_accessed=2 * (2 * rows * q_width + 2 * span * kv_width),
        ),
    )(queries, keys, grads, query_tags, key_tags)


def fused_attention(queries, keys, values, grads, query_tags, key_tags):
    rows, q_width = queries.shape
    span, kv_width = keys.shape
    heads = kv_width // HD
    q_spec, kv_spec, tag_specs = head_specs(rows, span)
    return pl.pallas_call(
        attention_kernel,
        grid=(heads,),
        in_specs=[q_spec, kv_spec, kv_spec, q_spec] + tag_specs,
        out_specs=[q_spec, q_spec, kv_spec],
        out_shape=[
            jax.ShapeDtypeStruct((rows, q_width), jnp.bfloat16),
            jax.ShapeDtypeStruct((rows, q_width), jnp.bfloat16),
            jax.ShapeDtypeStruct((span, kv_width), jnp.bfloat16),
        ],
        cost_estimate=pl.CostEstimate(
            flops=10 * rows * GROUP * span * HD * heads,
            transcendentals=rows * GROUP * span * heads,
            bytes_accessed=2 * (4 * rows * q_width + 3 * span * kv_width),
        ),
    )(queries, keys, values, grads, query_tags, key_tags)


def peer_gather_kernel(axis, n, x_ref, o_ref, send_sem, recv_sem, local_sem):
    me = lax.axis_index(axis)
    barrier = pltpu.get_barrier_semaphore()
    for k in range(1, n):
        pl.semaphore_signal(
            barrier, inc=1, device_id={axis: lax.rem(me + k, n)}, device_id_type=pl.DeviceIdType.MESH
        )
    pl.semaphore_wait(barrier, n - 1)
    local = pltpu.make_async_copy(x_ref, o_ref.at[me], local_sem)
    local.start()
    copies = []
    for k in range(1, n):
        copy = pltpu.make_async_remote_copy(
            src_ref=x_ref,
            dst_ref=o_ref.at[me],
            send_sem=send_sem.at[k],
            recv_sem=recv_sem.at[k],
            device_id={axis: lax.rem(me + k, n)},
            device_id_type=pl.DeviceIdType.MESH,
        )
        copy.start()
        copies.append(copy)
    for copy in copies:
        copy.wait()
    local.wait()


def peer_gather(x, axis, collective_id):
    n = lax.axis_size(axis)
    return pl.pallas_call(
        functools.partial(peer_gather_kernel, axis, n),
        out_shape=jax.ShapeDtypeStruct((n,) + x.shape, x.dtype),
        in_specs=[pl.BlockSpec(memory_space=pl.ANY)],
        out_specs=pl.BlockSpec(memory_space=pl.ANY),
        scratch_shapes=[
            pltpu.SemaphoreType.DMA((n,)),
            pltpu.SemaphoreType.DMA((n,)),
            pltpu.SemaphoreType.DMA,
        ],
        compiler_params=pltpu.CompilerParams(collective_id=collective_id, has_side_effects=True),
    )(x)


def peer_sum_kernel(axis, n, x_ref, o_ref, landed, send_sem, recv_sem, local_sem):
    me = lax.axis_index(axis)
    barrier = pltpu.get_barrier_semaphore()
    for k in range(1, n):
        pl.semaphore_signal(
            barrier, inc=1, device_id={axis: lax.rem(me + k, n)}, device_id_type=pl.DeviceIdType.MESH
        )
    pl.semaphore_wait(barrier, n - 1)
    local = pltpu.make_async_copy(x_ref.at[me], landed.at[0], local_sem)
    local.start()
    copies = []
    for k in range(1, n):
        peer = lax.rem(me + k, n)
        copy = pltpu.make_async_remote_copy(
            src_ref=x_ref.at[peer],
            dst_ref=landed.at[k],
            send_sem=send_sem.at[k],
            recv_sem=recv_sem.at[k],
            device_id={axis: peer},
            device_id_type=pl.DeviceIdType.MESH,
        )
        copy.start()
        copies.append(copy)
    local.wait()
    total = landed[0].astype(jnp.float32)
    for k in range(1, n):
        copies[k - 1].wait()
        total = total + landed[k].astype(jnp.float32)
    o_ref[...] = total


def peer_sum_scatter(x, axis, collective_id):
    n = lax.axis_size(axis)
    return pl.pallas_call(
        functools.partial(peer_sum_kernel, axis, n),
        out_shape=jax.ShapeDtypeStruct(x.shape[1:], jnp.float32),
        in_specs=[pl.BlockSpec(memory_space=pl.ANY)],
        out_specs=pl.BlockSpec(memory_space=pltpu.VMEM),
        scratch_shapes=[
            pltpu.VMEM(x.shape, x.dtype),
            pltpu.SemaphoreType.DMA((n,)),
            pltpu.SemaphoreType.DMA((n,)),
            pltpu.SemaphoreType.DMA,
        ],
        compiler_params=pltpu.CompilerParams(collective_id=collective_id, has_side_effects=True),
    )(x)


def shifted(x, axis, by):
    length = lax.axis_size(axis)
    pairs = [(i, i + by) for i in range(length) if 0 <= i + by < length]
    return lax.ppermute(x, axis, pairs)


def shards(hidden, queries, key_heads, w_value, d_out, segments):
    shard_rows = hidden.shape[1]
    kv_width = w_value.shape[1]
    n_hops = WINDOW // shard_rows
    span_rows = (n_hops + 1) * shard_rows
    tokens_in = hidden[0]
    own_keys = key_heads[0]
    own_segments = segments[0]
    n_fsdp = lax.axis_size("fsdp")
    n_ctx = lax.axis_size("ctx")
    model_width = tokens_in.shape[1]
    half_rows = w_value.shape[0] // 2
    core = lax.axis_index("ctx") % 2
    w_mine = lax.all_gather(
        lax.dynamic_slice_in_dim(w_value, core * half_rows, half_rows, 0), "fsdp", axis=0, tiled=False
    )
    partner = [(i, i ^ 1) for i in range(n_ctx)]
    token_halves = tokens_in.reshape(shard_rows, n_fsdp, 2, half_rows)
    tokens_mine = lax.dynamic_index_in_dim(token_halves, core, axis=2, keepdims=False)
    partner_tokens = lax.ppermute(
        lax.dynamic_index_in_dim(token_halves, 1 - core, axis=2, keepdims=False), "ctx", partner
    )
    out_rows = model_width // (n_ctx * n_fsdp)
    token_cols = (
        tokens_in.reshape(shard_rows, n_ctx, n_fsdp, out_rows).transpose(2, 0, 1, 3)
    )
    tag_columns = jnp.broadcast_to(own_segments.astype(jnp.bfloat16)[:, None], (shard_rows, HD))
    parcel = jnp.concatenate([own_keys, tag_columns], 1)
    arrived = [shifted(parcel, "ctx", hop) for hop in range(1, n_hops + 1)]
    window_parcel = jnp.concatenate(arrived[::-1] + [parcel], 0)
    window_parcel, partner_tokens, token_cols = lax.optimization_barrier(
        (window_parcel, partner_tokens, token_cols)
    )
    window_keys = window_parcel[:, :kv_width]
    window_tags = window_parcel[:, kv_width].astype(jnp.int32)
    first_query = lax.axis_index("ctx") * shard_rows
    key_pos = first_query - WINDOW + jnp.arange(span_rows, dtype=jnp.int32)
    key_tags = jnp.where(key_pos >= 0, window_tags, -1)
    query_tags = own_segments.astype(jnp.int32)[:, None]
    own_start = n_hops * shard_rows

    def returned_parts(terms):
        parts = [terms[own_start:]]
        for hop in range(1, n_hops + 1):
            low_edge = (n_hops - hop) * shard_rows
            parts.append(shifted(terms[low_edge : low_edge + shard_rows], "ctx", -hop))
        return parts

    def added(parts):
        total = parts[0].astype(jnp.float32)
        for part in parts[1:]:
            total = total + part.astype(jnp.float32)
        return total.astype(jnp.bfloat16)

    def returned_sum(terms):
        return added(returned_parts(terms))

    value_terms = value_grads(queries[0], window_keys, d_out[0], query_tags, key_tags[None, :])
    d_values_low = returned_sum(value_terms)
    w_mine, _ = lax.optimization_barrier((w_mine, d_values_low))
    grads_all = lax.all_gather(d_values_low, "fsdp", axis=0, tiled=False)

    partner_part = jnp.einsum("tfr,frn->tn", partner_tokens, w_mine, preferred_element_type=jnp.float32)
    values = (
        jnp.einsum("tfr,frn->tn", tokens_mine, w_mine, preferred_element_type=jnp.float32)
        + lax.ppermute(partner_part, "ctx", partner)
    ).astype(jnp.bfloat16)
    arrived_values = [shifted(values, "ctx", hop) for hop in range(1, n_hops + 1)]
    token_cols, _ = lax.optimization_barrier((token_cols, values))
    token_cols = lax.all_to_all(token_cols, "fsdp", 0, 0, tiled=True)
    window_values = jnp.concatenate(arrived_values[::-1] + [values], 0)
    out_rows_attn, d_query_heads, key_terms = fused_attention(
        queries[0], window_keys, window_values, d_out[0], query_tags, key_tags[None, :]
    )
    key_parts = returned_parts(key_terms)
    grads_all, _ = lax.optimization_barrier((grads_all, key_terms))
    weight_part = jnp.einsum(
        "ftcr,ftn->crn", token_cols, grads_all, preferred_element_type=jnp.float32
    )
    d_weight = peer_sum_scatter(weight_part.astype(jnp.bfloat16), "ctx", 3)
    d_weight, key_parts = lax.optimization_barrier((d_weight, key_parts))
    d_key_rows = added(key_parts)
    d_mine = jnp.einsum("tn,frn->tfr", d_values_low, w_mine, preferred_element_type=jnp.float32).astype(jnp.bfloat16)
    partner_grads = lax.ppermute(d_values_low, "ctx", partner)
    d_other = lax.ppermute(
        jnp.einsum("tn,frn->tfr", partner_grads, w_mine, preferred_element_type=jnp.float32).astype(jnp.bfloat16),
        "ctx",
        partner,
    )
    d_tokens = jnp.where(
        core == 0, jnp.stack([d_mine, d_other], 2), jnp.stack([d_other, d_mine], 2)
    ).reshape(shard_rows, model_width)
    return (
        out_rows_attn[None],
        d_query_heads[None],
        d_key_rows[None],
        d_tokens[None],
        d_weight,
    )


def solution(mesh):
    in_specs = (
        P("fsdp", "ctx", None),
        P("fsdp", "ctx", None),
        P("fsdp", "ctx", None),
        P("fsdp", None),
        P("fsdp", "ctx", None),
        P("fsdp", "ctx"),
    )
    out_specs = (
        P("fsdp", "ctx", None),
        P("fsdp", "ctx", None),
        P("fsdp", "ctx", None),
        P("fsdp", "ctx", None),
        P(("ctx", "fsdp"), None),
    )
    return jax.shard_map(shards, mesh=mesh, in_specs=in_specs, out_specs=out_specs, check_vma=False)
```

```python
import functools
import math

import jax
import jax.numpy as jnp
from jax import lax
from jax.experimental import pallas as pl
from jax.experimental.pallas import tpu as pltpu
from jax.sharding import PartitionSpec as P

HQ = 16
HK = 8
HD = 128
WINDOW = 1024
GROUP = 2


score_scale = 1.0 / math.sqrt(168.0)


def window_probs(q, keys, qtag_ref, ktag_ref):
    rows = qtag_ref.shape[0]
    span = keys.shape[0]
    reach = span - rows
    t_idx = lax.broadcasted_iota(jnp.int32, (rows, span), 0)
    l_idx = lax.broadcasted_iota(jnp.int32, (rows, span), 1)
    allowed = (qtag_ref[...] == ktag_ref[...]) & (l_idx > t_idx) & (l_idx <= t_idx + reach)
    allowed = jnp.concatenate([allowed] * GROUP, axis=0)
    scores = lax.dot_general(q, keys, (((1,), (1,)), ((), ())), preferred_element_type=jnp.float32) * score_scale
    scores = jnp.where(allowed, scores, -jnp.inf)
    highest = jnp.max(scores, axis=-1, keepdims=True)
    raw = jnp.exp(scores - highest)
    return raw / jnp.sum(raw, axis=-1, keepdims=True)


def stacked_heads(ref):
    return jnp.concatenate([ref[:, r * HD:(r + 1) * HD] for r in range(GROUP)], axis=0)


def value_grad_kernel(q_ref, k_ref, do_ref, qtag_ref, ktag_ref, dv_ref):
    probs_low = window_probs(stacked_heads(q_ref), k_ref[...], qtag_ref, ktag_ref).astype(jnp.bfloat16)
    grad = stacked_heads(do_ref)
    dv = lax.dot_general(probs_low, grad, (((0,), (0,)), ((), ())), preferred_element_type=jnp.float32)
    dv_ref[...] = dv.astype(jnp.bfloat16)


def attention_kernel(q_ref, k_ref, v_ref, do_ref, qtag_ref, ktag_ref, out_ref, dq_ref, dk_ref):
    rows = q_ref.shape[0]
    q = stacked_heads(q_ref)
    grad = stacked_heads(do_ref)
    keys = k_ref[...]
    vals = v_ref[...]
    probs = window_probs(q, keys, qtag_ref, ktag_ref)
    probs_low = probs.astype(jnp.bfloat16)
    out = jnp.dot(probs_low, vals, preferred_element_type=jnp.float32).astype(jnp.bfloat16)
    grad_probs = lax.dot_general(grad, vals, (((1,), (1,)), ((), ())), preferred_element_type=jnp.float32)
    delta = jnp.sum(grad.astype(jnp.float32) * out.astype(jnp.float32), axis=-1, keepdims=True)
    grad_scores = (probs * (grad_probs - delta)).astype(jnp.bfloat16)
    dq = (score_scale * jnp.dot(grad_scores, keys, preferred_element_type=jnp.float32)).astype(jnp.bfloat16)
    dk = score_scale * lax.dot_general(grad_scores, q, (((0,), (0,)), ((), ())), preferred_element_type=jnp.float32)
    for r in range(GROUP):
        out_ref[:, r * HD:(r + 1) * HD] = out[r * rows:(r + 1) * rows]
        dq_ref[:, r * HD:(r + 1) * HD] = dq[r * rows:(r + 1) * rows]
    dk_ref[...] = dk.astype(jnp.bfloat16)


def head_specs(rows, span):
    q_spec = pl.BlockSpec((rows, GROUP * HD), lambda g: (0, g))
    kv_spec = pl.BlockSpec((span, HD), lambda g: (0, g))
    tag_specs = [pl.BlockSpec((rows, 1), lambda g: (0, 0)), pl.BlockSpec((1, span), lambda g: (0, 0))]
    return q_spec, kv_spec, tag_specs


def value_grads(queries, keys, grads, query_tags, key_tags):
    rows, q_width = queries.shape
    span, kv_width = keys.shape
    heads = kv_width // HD
    q_spec, kv_spec, tag_specs = head_specs(rows, span)
    return pl.pallas_call(
        value_grad_kernel,
        grid=(heads,),
        in_specs=[q_spec, kv_spec, q_spec] + tag_specs,
        out_specs=kv_spec,
        out_shape=jax.ShapeDtypeStruct((span, kv_width), jnp.bfloat16),
        cost_estimate=pl.CostEstimate(
            flops=4 * rows * GROUP * span * HD * heads,
            transcendentals=rows * GROUP * span * heads,
            bytes_accessed=2 * (2 * rows * q_width + 2 * span * kv_width),
        ),
    )(queries, keys, grads, query_tags, key_tags)


def fused_attention(queries, keys, values, grads, query_tags, key_tags):
    rows, q_width = queries.shape
    span, kv_width = keys.shape
    heads = kv_width // HD
    q_spec, kv_spec, tag_specs = head_specs(rows, span)
    return pl.pallas_call(
        attention_kernel,
        grid=(heads,),
        in_specs=[q_spec, kv_spec, kv_spec, q_spec] + tag_specs,
        out_specs=[q_spec, q_spec, kv_spec],
        out_shape=[
            jax.ShapeDtypeStruct((rows, q_width), jnp.bfloat16),
            jax.ShapeDtypeStruct((rows, q_width), jnp.bfloat16),
            jax.ShapeDtypeStruct((span, kv_width), jnp.bfloat16),
        ],
        cost_estimate=pl.CostEstimate(
            flops=10 * rows * GROUP * span * HD * heads,
            transcendentals=rows * GROUP * span * heads,
            bytes_accessed=2 * (4 * rows * q_width + 3 * span * kv_width),
        ),
    )(queries, keys, values, grads, query_tags, key_tags)


def peer_gather_kernel(axis, n, x_ref, o_ref, send_sem, recv_sem, local_sem):
    me = lax.axis_index(axis)
    barrier = pltpu.get_barrier_semaphore()
    for k in range(1, n):
        pl.semaphore_signal(
            barrier, inc=1, device_id={axis: lax.rem(me + k, n)}, device_id_type=pl.DeviceIdType.MESH
        )
    pl.semaphore_wait(barrier, n - 1)
    local = pltpu.make_async_copy(x_ref, o_ref.at[me], local_sem)
    local.start()
    copies = []
    for k in range(1, n):
        copy = pltpu.make_async_remote_copy(
            src_ref=x_ref,
            dst_ref=o_ref.at[me],
            send_sem=send_sem.at[k],
            recv_sem=recv_sem.at[k],
            device_id={axis: lax.rem(me + k, n)},
            device_id_type=pl.DeviceIdType.MESH,
        )
        copy.start()
        copies.append(copy)
    for copy in copies:
        copy.wait()
    local.wait()


def peer_gather(x, axis, collective_id):
    n = lax.axis_size(axis)
    return pl.pallas_call(
        functools.partial(peer_gather_kernel, axis, n),
        out_shape=jax.ShapeDtypeStruct((n,) + x.shape, x.dtype),
        in_specs=[pl.BlockSpec(memory_space=pl.ANY)],
        out_specs=pl.BlockSpec(memory_space=pl.ANY),
        scratch_shapes=[
            pltpu.SemaphoreType.DMA((n,)),
            pltpu.SemaphoreType.DMA((n,)),
            pltpu.SemaphoreType.DMA,
        ],
        compiler_params=pltpu.CompilerParams(collective_id=collective_id, has_side_effects=True),
    )(x)


def peer_sum_kernel(axis, n, x_ref, o_ref, landed, send_sem, recv_sem, local_sem):
    me = lax.axis_index(axis)
    barrier = pltpu.get_barrier_semaphore()
    for k in range(1, n):
        pl.semaphore_signal(
            barrier, inc=1, device_id={axis: lax.rem(me + k, n)}, device_id_type=pl.DeviceIdType.MESH
        )
    pl.semaphore_wait(barrier, n - 1)
    local = pltpu.make_async_copy(x_ref.at[me], landed.at[0], local_sem)
    local.start()
    copies = []
    for k in range(1, n):
        peer = lax.rem(me + k, n)
        copy = pltpu.make_async_remote_copy(
            src_ref=x_ref.at[peer],
            dst_ref=landed.at[k],
            send_sem=send_sem.at[k],
            recv_sem=recv_sem.at[k],
            device_id={axis: peer},
            device_id_type=pl.DeviceIdType.MESH,
        )
        copy.start()
        copies.append(copy)
    local.wait()
    total = landed[0].astype(jnp.float32)
    for k in range(1, n):
        copies[k - 1].wait()
        total = total + landed[k].astype(jnp.float32)
    o_ref[...] = total


def peer_sum_scatter(x, axis, collective_id):
    n = lax.axis_size(axis)
    return pl.pallas_call(
        functools.partial(peer_sum_kernel, axis, n),
        out_shape=jax.ShapeDtypeStruct(x.shape[1:], jnp.float32),
        in_specs=[pl.BlockSpec(memory_space=pl.ANY)],
        out_specs=pl.BlockSpec(memory_space=pltpu.VMEM),
        scratch_shapes=[
            pltpu.VMEM(x.shape, x.dtype),
            pltpu.SemaphoreType.DMA((n,)),
            pltpu.SemaphoreType.DMA((n,)),
            pltpu.SemaphoreType.DMA,
        ],
        compiler_params=pltpu.CompilerParams(collective_id=collective_id, has_side_effects=True),
    )(x)


def shifted(x, axis, by):
    length = lax.axis_size(axis)
    pairs = [(i, i + by) for i in range(length) if 0 <= i + by < length]
    return lax.ppermute(x, axis, pairs)


def shards(hidden, queries, key_heads, w_value, d_out, segments):
    shard_rows = hidden.shape[1]
    kv_width = w_value.shape[1]
    n_hops = WINDOW // shard_rows
    span_rows = (n_hops + 1) * shard_rows
    tokens_in = hidden[0]
    own_keys = key_heads[0]
    own_segments = segments[0]
    n_fsdp = lax.axis_size("fsdp")
    n_ctx = lax.axis_size("ctx")
    model_width = tokens_in.shape[1]
    half_rows = w_value.shape[0] // 2
    core = lax.axis_index("ctx") % 2
    w_mine = lax.all_gather(
        lax.dynamic_slice_in_dim(w_value, core * half_rows, half_rows, 0), "fsdp", axis=0, tiled=False
    )
    partner = [(i, i ^ 1) for i in range(n_ctx)]
    token_halves = tokens_in.reshape(shard_rows, n_fsdp, 2, half_rows)
    tokens_mine = lax.dynamic_index_in_dim(token_halves, core, axis=2, keepdims=False)
    partner_tokens = lax.ppermute(
        lax.dynamic_index_in_dim(token_halves, 1 - core, axis=2, keepdims=False), "ctx", partner
    )
    out_rows = model_width // (n_ctx * n_fsdp)
    token_cols = (
        tokens_in.reshape(shard_rows, n_ctx, n_fsdp, out_rows).transpose(2, 0, 1, 3)
    )
    tag_columns = jnp.broadcast_to(own_segments.astype(jnp.bfloat16)[:, None], (shard_rows, HD))
    parcel = jnp.concatenate([own_keys, tag_columns], 1)
    arrived = [shifted(parcel, "ctx", hop) for hop in range(1, n_hops + 1)]
    window_parcel = jnp.concatenate(arrived[::-1] + [parcel], 0)
    window_parcel, partner_tokens, token_cols = lax.optimization_barrier(
        (window_parcel, partner_tokens, token_cols)
    )
    window_keys = window_parcel[:, :kv_width]
    window_tags = window_parcel[:, kv_width].astype(jnp.int32)
    first_query = lax.axis_index("ctx") * shard_rows
    key_pos = first_query - WINDOW + jnp.arange(span_rows, dtype=jnp.int32)
    key_tags = jnp.where(key_pos >= 0, window_tags, -1)
    query_tags = own_segments.astype(jnp.int32)[:, None]
    own_start = n_hops * shard_rows

    def returned_sum(terms):
        total = terms[own_start:].astype(jnp.float32)
        for hop in range(1, n_hops + 1):
            low_edge = (n_hops - hop) * shard_rows
            total = total + shifted(terms[low_edge : low_edge + shard_rows], "ctx", -hop).astype(jnp.float32)
        return total.astype(jnp.bfloat16)

    value_terms = value_grads(queries[0], window_keys, d_out[0], query_tags, key_tags[None, :])
    d_values_low = returned_sum(value_terms)
    w_mine, _ = lax.optimization_barrier((w_mine, d_values_low))
    grads_all = lax.all_gather(d_values_low, "fsdp", axis=0, tiled=False)

    partner_part = jnp.einsum("tfr,frn->tn", partner_tokens, w_mine, preferred_element_type=jnp.float32)
    values = (
        jnp.einsum("tfr,frn->tn", tokens_mine, w_mine, preferred_element_type=jnp.float32)
        + lax.ppermute(partner_part.astype(jnp.bfloat16), "ctx", partner).astype(jnp.float32)
    ).astype(jnp.bfloat16)
    arrived_values = [shifted(values, "ctx", hop) for hop in range(1, n_hops + 1)]
    token_cols, _ = lax.optimization_barrier((token_cols, values))
    token_cols = lax.all_to_all(token_cols, "fsdp", 0, 0, tiled=True)
    window_values = jnp.concatenate(arrived_values[::-1] + [values], 0)
    out_rows_attn, d_query_heads, key_terms = fused_attention(
        queries[0], window_keys, window_values, d_out[0], query_tags, key_tags[None, :]
    )
    d_key_rows = returned_sum(key_terms)
    grads_all, _ = lax.optimization_barrier((grads_all, key_terms))
    weight_part = jnp.einsum(
        "ftcr,ftn->crn", token_cols, grads_all, preferred_element_type=jnp.float32
    )
    d_weight = peer_sum_scatter(weight_part.astype(jnp.bfloat16), "ctx", 3)
    d_mine = jnp.einsum("tn,frn->tfr", d_values_low, w_mine, preferred_element_type=jnp.float32).astype(jnp.bfloat16)
    partner_grads = lax.ppermute(d_values_low, "ctx", partner)
    d_other = lax.ppermute(
        jnp.einsum("tn,frn->tfr", partner_grads, w_mine, preferred_element_type=jnp.float32).astype(jnp.bfloat16),
        "ctx",
        partner,
    )
    d_tokens = jnp.where(
        core == 0, jnp.stack([d_mine, d_other], 2), jnp.stack([d_other, d_mine], 2)
    ).reshape(shard_rows, model_width)
    return (
        out_rows_attn[None],
        d_query_heads[None],
        d_key_rows[None],
        d_tokens[None],
        d_weight,
    )


def solution(mesh):
    in_specs = (
        P("fsdp", "ctx", None),
        P("fsdp", "ctx", None),
        P("fsdp", "ctx", None),
        P("fsdp", None),
        P("fsdp", "ctx", None),
        P("fsdp", "ctx"),
    )
    out_specs = (
        P("fsdp", "ctx", None),
        P("fsdp", "ctx", None),
        P("fsdp", "ctx", None),
        P("fsdp", "ctx", None),
        P(("ctx", "fsdp"), None),
    )
    return jax.shard_map(shards, mesh=mesh, in_specs=in_specs, out_specs=out_specs, check_vma=False)
```

```python
import functools
import math

import jax
import jax.numpy as jnp
from jax import lax
from jax.experimental import pallas as pl
from jax.experimental.pallas import tpu as pltpu
from jax.sharding import PartitionSpec as P

HQ = 16
HK = 8
HD = 128
WINDOW = 1024
GROUP = 2


score_scale = 1.0 / math.sqrt(168.0)


def window_probs(q, keys, qtag_ref, ktag_ref):
    rows = qtag_ref.shape[0]
    span = keys.shape[0]
    reach = span - rows
    t_idx = lax.broadcasted_iota(jnp.int32, (rows, span), 0)
    l_idx = lax.broadcasted_iota(jnp.int32, (rows, span), 1)
    allowed = (qtag_ref[...] == ktag_ref[...]) & (l_idx > t_idx) & (l_idx <= t_idx + reach)
    allowed = jnp.concatenate([allowed] * GROUP, axis=0)
    scores = lax.dot_general(q, keys, (((1,), (1,)), ((), ())), preferred_element_type=jnp.float32) * score_scale
    scores = jnp.where(allowed, scores, -jnp.inf)
    highest = jnp.max(scores, axis=-1, keepdims=True)
    raw = jnp.exp(scores - highest)
    return raw / jnp.sum(raw, axis=-1, keepdims=True)


def stacked_heads(ref):
    return jnp.concatenate([ref[:, r * HD:(r + 1) * HD] for r in range(GROUP)], axis=0)


def value_grad_kernel(q_ref, k_ref, do_ref, qtag_ref, ktag_ref, dv_ref):
    probs_low = window_probs(stacked_heads(q_ref), k_ref[...], qtag_ref, ktag_ref).astype(jnp.bfloat16)
    grad = stacked_heads(do_ref)
    dv = lax.dot_general(probs_low, grad, (((0,), (0,)), ((), ())), preferred_element_type=jnp.float32)
    dv_ref[...] = dv.astype(jnp.bfloat16)


def attention_kernel(q_ref, k_ref, v_ref, do_ref, qtag_ref, ktag_ref, out_ref, dq_ref, dk_ref):
    rows = q_ref.shape[0]
    q = stacked_heads(q_ref)
    grad = stacked_heads(do_ref)
    keys = k_ref[...]
    vals = v_ref[...]
    probs = window_probs(q, keys, qtag_ref, ktag_ref)
    probs_low = probs.astype(jnp.bfloat16)
    out = jnp.dot(probs_low, vals, preferred_element_type=jnp.float32).astype(jnp.bfloat16)
    grad_probs = lax.dot_general(grad, vals, (((1,), (1,)), ((), ())), preferred_element_type=jnp.float32)
    delta = jnp.sum(grad.astype(jnp.float32) * out.astype(jnp.float32), axis=-1, keepdims=True)
    grad_scores = (probs * (grad_probs - delta)).astype(jnp.bfloat16)
    dq = (score_scale * jnp.dot(grad_scores, keys, preferred_element_type=jnp.float32)).astype(jnp.bfloat16)
    dk = score_scale * lax.dot_general(grad_scores, q, (((0,), (0,)), ((), ())), preferred_element_type=jnp.float32)
    for r in range(GROUP):
        out_ref[:, r * HD:(r + 1) * HD] = out[r * rows:(r + 1) * rows]
        dq_ref[:, r * HD:(r + 1) * HD] = dq[r * rows:(r + 1) * rows]
    dk_ref[...] = dk.astype(jnp.bfloat16)


def head_specs(rows, span):
    q_spec = pl.BlockSpec((rows, GROUP * HD), lambda g: (0, g))
    kv_spec = pl.BlockSpec((span, HD), lambda g: (0, g))
    tag_specs = [pl.BlockSpec((rows, 1), lambda g: (0, 0)), pl.BlockSpec((1, span), lambda g: (0, 0))]
    return q_spec, kv_spec, tag_specs


def value_grads(queries, keys, grads, query_tags, key_tags):
    rows, q_width = queries.shape
    span, kv_width = keys.shape
    heads = kv_width // HD
    q_spec, kv_spec, tag_specs = head_specs(rows, span)
    return pl.pallas_call(
        value_grad_kernel,
        grid=(heads,),
        in_specs=[q_spec, kv_spec, q_spec] + tag_specs,
        out_specs=kv_spec,
        out_shape=jax.ShapeDtypeStruct((span, kv_width), jnp.bfloat16),
        cost_estimate=pl.CostEstimate(
            flops=4 * rows * GROUP * span * HD * heads,
            transcendentals=rows * GROUP * span * heads,
            bytes_accessed=2 * (2 * rows * q_width + 2 * span * kv_width),
        ),
    )(queries, keys, grads, query_tags, key_tags)


def fused_attention(queries, keys, values, grads, query_tags, key_tags):
    rows, q_width = queries.shape
    span, kv_width = keys.shape
    heads = kv_width // HD
    q_spec, kv_spec, tag_specs = head_specs(rows, span)
    return pl.pallas_call(
        attention_kernel,
        grid=(heads,),
        in_specs=[q_spec, kv_spec, kv_spec, q_spec] + tag_specs,
        out_specs=[q_spec, q_spec, kv_spec],
        out_shape=[
            jax.ShapeDtypeStruct((rows, q_width), jnp.bfloat16),
            jax.ShapeDtypeStruct((rows, q_width), jnp.bfloat16),
            jax.ShapeDtypeStruct((span, kv_width), jnp.bfloat16),
        ],
        cost_estimate=pl.CostEstimate(
            flops=10 * rows * GROUP * span * HD * heads,
            transcendentals=rows * GROUP * span * heads,
            bytes_accessed=2 * (4 * rows * q_width + 3 * span * kv_width),
        ),
    )(queries, keys, values, grads, query_tags, key_tags)


def peer_gather_kernel(axis, n, x_ref, o_ref, send_sem, recv_sem, local_sem):
    me = lax.axis_index(axis)
    barrier = pltpu.get_barrier_semaphore()
    for k in range(1, n):
        pl.semaphore_signal(
            barrier, inc=1, device_id={axis: lax.rem(me + k, n)}, device_id_type=pl.DeviceIdType.MESH
        )
    pl.semaphore_wait(barrier, n - 1)
    local = pltpu.make_async_copy(x_ref, o_ref.at[me], local_sem)
    local.start()
    copies = []
    for k in range(1, n):
        copy = pltpu.make_async_remote_copy(
            src_ref=x_ref,
            dst_ref=o_ref.at[me],
            send_sem=send_sem.at[k],
            recv_sem=recv_sem.at[k],
            device_id={axis: lax.rem(me + k, n)},
            device_id_type=pl.DeviceIdType.MESH,
        )
        copy.start()
        copies.append(copy)
    for copy in copies:
        copy.wait()
    local.wait()


def peer_gather(x, axis, collective_id):
    n = lax.axis_size(axis)
    return pl.pallas_call(
        functools.partial(peer_gather_kernel, axis, n),
        out_shape=jax.ShapeDtypeStruct((n,) + x.shape, x.dtype),
        in_specs=[pl.BlockSpec(memory_space=pl.ANY)],
        out_specs=pl.BlockSpec(memory_space=pl.ANY),
        scratch_shapes=[
            pltpu.SemaphoreType.DMA((n,)),
            pltpu.SemaphoreType.DMA((n,)),
            pltpu.SemaphoreType.DMA,
        ],
        compiler_params=pltpu.CompilerParams(collective_id=collective_id, has_side_effects=True),
    )(x)


def peer_sum_kernel(axis, n, x_ref, o_ref, landed, send_sem, recv_sem, local_sem):
    me = lax.axis_index(axis)
    barrier = pltpu.get_barrier_semaphore()
    for k in range(1, n):
        pl.semaphore_signal(
            barrier, inc=1, device_id={axis: lax.rem(me + k, n)}, device_id_type=pl.DeviceIdType.MESH
        )
    pl.semaphore_wait(barrier, n - 1)
    local = pltpu.make_async_copy(x_ref.at[me], landed.at[0], local_sem)
    local.start()
    copies = []
    for k in range(1, n):
        peer = lax.rem(me + k, n)
        copy = pltpu.make_async_remote_copy(
            src_ref=x_ref.at[peer],
            dst_ref=landed.at[k],
            send_sem=send_sem.at[k],
            recv_sem=recv_sem.at[k],
            device_id={axis: peer},
            device_id_type=pl.DeviceIdType.MESH,
        )
        copy.start()
        copies.append(copy)
    local.wait()
    total = landed[0].astype(jnp.float32)
    for k in range(1, n):
        copies[k - 1].wait()
        total = total + landed[k].astype(jnp.float32)
    o_ref[...] = total


def peer_sum_scatter(x, axis, collective_id):
    n = lax.axis_size(axis)
    return pl.pallas_call(
        functools.partial(peer_sum_kernel, axis, n),
        out_shape=jax.ShapeDtypeStruct(x.shape[1:], jnp.float32),
        in_specs=[pl.BlockSpec(memory_space=pl.ANY)],
        out_specs=pl.BlockSpec(memory_space=pltpu.VMEM),
        scratch_shapes=[
            pltpu.VMEM(x.shape, x.dtype),
            pltpu.SemaphoreType.DMA((n,)),
            pltpu.SemaphoreType.DMA((n,)),
            pltpu.SemaphoreType.DMA,
        ],
        compiler_params=pltpu.CompilerParams(collective_id=collective_id, has_side_effects=True),
    )(x)


def shifted(x, axis, by):
    length = lax.axis_size(axis)
    pairs = [(i, i + by) for i in range(length) if 0 <= i + by < length]
    return lax.ppermute(x, axis, pairs)


def shards(hidden, queries, key_heads, w_value, d_out, segments):
    shard_rows = hidden.shape[1]
    kv_width = w_value.shape[1]
    n_hops = WINDOW // shard_rows
    span_rows = (n_hops + 1) * shard_rows
    tokens_in = hidden[0]
    own_keys = key_heads[0]
    own_segments = segments[0]
    n_fsdp = lax.axis_size("fsdp")
    n_ctx = lax.axis_size("ctx")
    model_width = tokens_in.shape[1]
    half_rows = w_value.shape[0] // 2
    core = lax.axis_index("ctx") % 2
    w_mine = lax.all_gather(
        lax.dynamic_slice_in_dim(w_value, core * half_rows, half_rows, 0), "fsdp", axis=0, tiled=False
    )
    partner = [(i, i ^ 1) for i in range(n_ctx)]
    token_halves = tokens_in.reshape(shard_rows, n_fsdp, 2, half_rows)
    tokens_mine = lax.dynamic_index_in_dim(token_halves, core, axis=2, keepdims=False)
    partner_tokens = lax.ppermute(
        lax.dynamic_index_in_dim(token_halves, 1 - core, axis=2, keepdims=False), "ctx", partner
    )
    out_rows = model_width // (n_ctx * n_fsdp)
    token_cols = (
        tokens_in.reshape(shard_rows, n_ctx, n_fsdp, out_rows).transpose(2, 0, 1, 3)
    )
    tag_columns = jnp.broadcast_to(own_segments.astype(jnp.bfloat16)[:, None], (shard_rows, HD))
    parcel = jnp.concatenate([own_keys, tag_columns], 1)
    arrived = [shifted(parcel, "ctx", hop) for hop in range(1, n_hops + 1)]
    window_parcel = jnp.concatenate(arrived[::-1] + [parcel], 0)
    window_parcel, partner_tokens, token_cols = lax.optimization_barrier(
        (window_parcel, partner_tokens, token_cols)
    )
    window_keys = window_parcel[:, :kv_width]
    window_tags = window_parcel[:, kv_width].astype(jnp.int32)
    first_query = lax.axis_index("ctx") * shard_rows
    key_pos = first_query - WINDOW + jnp.arange(span_rows, dtype=jnp.int32)
    key_tags = jnp.where(key_pos >= 0, window_tags, -1)
    query_tags = own_segments.astype(jnp.int32)[:, None]
    own_start = n_hops * shard_rows

    def returned_sum(terms):
        total = terms[own_start:].astype(jnp.float32)
        for hop in range(1, n_hops + 1):
            low_edge = (n_hops - hop) * shard_rows
            total = total + shifted(terms[low_edge : low_edge + shard_rows], "ctx", -hop).astype(jnp.float32)
        return total.astype(jnp.bfloat16)

    value_terms = value_grads(queries[0], window_keys, d_out[0], query_tags, key_tags[None, :])
    d_values_low = returned_sum(value_terms)
    w_mine, _ = lax.optimization_barrier((w_mine, d_values_low))
    grads_all = lax.all_gather(d_values_low, "fsdp", axis=0, tiled=False)

    partner_part = jnp.einsum("tfr,frn->tn", partner_tokens, w_mine, preferred_element_type=jnp.float32)
    values = (
        jnp.einsum("tfr,frn->tn", tokens_mine, w_mine, preferred_element_type=jnp.float32)
        + lax.ppermute(partner_part.astype(jnp.bfloat16), "ctx", partner).astype(jnp.float32)
    ).astype(jnp.bfloat16)
    arrived_values = [shifted(values, "ctx", hop) for hop in range(1, n_hops + 1)]
    token_cols, _ = lax.optimization_barrier((token_cols, values))
    token_cols = lax.all_to_all(token_cols, "fsdp", 0, 0, tiled=True)
    window_values = jnp.concatenate(arrived_values[::-1] + [values], 0)
    d_mine = jnp.einsum("tn,frn->tfr", d_values_low, w_mine, preferred_element_type=jnp.float32).astype(jnp.bfloat16)
    partner_grads = lax.ppermute(d_values_low, "ctx", partner)
    d_for_partner = jnp.einsum(
        "tn,frn->tfr", partner_grads, w_mine, preferred_element_type=jnp.float32
    ).astype(jnp.bfloat16)
    window_values, d_mine, d_for_partner = lax.optimization_barrier((window_values, d_mine, d_for_partner))
    d_other = lax.ppermute(d_for_partner, "ctx", partner)
    out_rows_attn, d_query_heads, key_terms = fused_attention(
        queries[0], window_keys, window_values, d_out[0], query_tags, key_tags[None, :]
    )
    d_key_rows = returned_sum(key_terms)
    grads_all, _ = lax.optimization_barrier((grads_all, key_terms))
    weight_part = jnp.einsum(
        "ftcr,ftn->crn", token_cols, grads_all, preferred_element_type=jnp.float32
    )
    d_weight = peer_sum_scatter(weight_part.astype(jnp.bfloat16), "ctx", 3)
    d_tokens = jnp.where(
        core == 0, jnp.stack([d_mine, d_other], 2), jnp.stack([d_other, d_mine], 2)
    ).reshape(shard_rows, model_width)
    return (
        out_rows_attn[None],
        d_query_heads[None],
        d_key_rows[None],
        d_tokens[None],
        d_weight,
    )


def solution(mesh):
    in_specs = (
        P("fsdp", "ctx", None),
        P("fsdp", "ctx", None),
        P("fsdp", "ctx", None),
        P("fsdp", None),
        P("fsdp", "ctx", None),
        P("fsdp", "ctx"),
    )
    out_specs = (
        P("fsdp", "ctx", None),
        P("fsdp", "ctx", None),
        P("fsdp", "ctx", None),
        P("fsdp", "ctx", None),
        P(("ctx", "fsdp"), None),
    )
    return jax.shard_map(shards, mesh=mesh, in_specs=in_specs, out_specs=out_specs, check_vma=False)
```

```python
import functools
import math

import jax
import jax.numpy as jnp
from jax import lax
from jax.experimental import pallas as pl
from jax.experimental.pallas import tpu as pltpu
from jax.sharding import PartitionSpec as P

HQ = 16
HK = 8
HD = 128
WINDOW = 1024
GROUP = 2


score_scale = 1.0 / math.sqrt(168.0)


def window_probs(q, keys, qtag_ref, ktag_ref):
    rows = qtag_ref.shape[0]
    span = keys.shape[0]
    reach = span - rows
    t_idx = lax.broadcasted_iota(jnp.int32, (rows, span), 0)
    l_idx = lax.broadcasted_iota(jnp.int32, (rows, span), 1)
    allowed = (qtag_ref[...] == ktag_ref[...]) & (l_idx > t_idx) & (l_idx <= t_idx + reach)
    allowed = jnp.concatenate([allowed] * GROUP, axis=0)
    scores = lax.dot_general(q, keys, (((1,), (1,)), ((), ())), preferred_element_type=jnp.float32) * score_scale
    scores = jnp.where(allowed, scores, -jnp.inf)
    highest = jnp.max(scores, axis=-1, keepdims=True)
    raw = jnp.exp(scores - highest)
    return raw / jnp.sum(raw, axis=-1, keepdims=True)


def stacked_heads(ref):
    return jnp.concatenate([ref[:, r * HD:(r + 1) * HD] for r in range(GROUP)], axis=0)


def value_grad_kernel(q_ref, k_ref, do_ref, qtag_ref, ktag_ref, dv_ref):
    probs_low = window_probs(stacked_heads(q_ref), k_ref[...], qtag_ref, ktag_ref).astype(jnp.bfloat16)
    grad = stacked_heads(do_ref)
    dv = lax.dot_general(probs_low, grad, (((0,), (0,)), ((), ())), preferred_element_type=jnp.float32)
    dv_ref[...] = dv.astype(jnp.bfloat16)


def attention_kernel(q_ref, k_ref, v_ref, do_ref, qtag_ref, ktag_ref, out_ref, dq_ref, dk_ref):
    rows = q_ref.shape[0]
    q = stacked_heads(q_ref)
    grad = stacked_heads(do_ref)
    keys = k_ref[...]
    vals = v_ref[...]
    probs = window_probs(q, keys, qtag_ref, ktag_ref)
    probs_low = probs.astype(jnp.bfloat16)
    out = jnp.dot(probs_low, vals, preferred_element_type=jnp.float32).astype(jnp.bfloat16)
    grad_probs = lax.dot_general(grad, vals, (((1,), (1,)), ((), ())), preferred_element_type=jnp.float32)
    delta = jnp.sum(grad.astype(jnp.float32) * out.astype(jnp.float32), axis=-1, keepdims=True)
    grad_scores = (probs * (grad_probs - delta)).astype(jnp.bfloat16)
    dq = (score_scale * jnp.dot(grad_scores, keys, preferred_element_type=jnp.float32)).astype(jnp.bfloat16)
    dk = score_scale * lax.dot_general(grad_scores, q, (((0,), (0,)), ((), ())), preferred_element_type=jnp.float32)
    for r in range(GROUP):
        out_ref[:, r * HD:(r + 1) * HD] = out[r * rows:(r + 1) * rows]
        dq_ref[:, r * HD:(r + 1) * HD] = dq[r * rows:(r + 1) * rows]
    dk_ref[...] = dk.astype(jnp.bfloat16)


def head_specs(rows, span):
    q_spec = pl.BlockSpec((rows, GROUP * HD), lambda g: (0, g))
    kv_spec = pl.BlockSpec((span, HD), lambda g: (0, g))
    tag_specs = [pl.BlockSpec((rows, 1), lambda g: (0, 0)), pl.BlockSpec((1, span), lambda g: (0, 0))]
    return q_spec, kv_spec, tag_specs


def value_grads(queries, keys, grads, query_tags, key_tags):
    rows, q_width = queries.shape
    span, kv_width = keys.shape
    heads = kv_width // HD
    q_spec, kv_spec, tag_specs = head_specs(rows, span)
    return pl.pallas_call(
        value_grad_kernel,
        grid=(heads,),
        in_specs=[q_spec, kv_spec, q_spec] + tag_specs,
        out_specs=kv_spec,
        out_shape=jax.ShapeDtypeStruct((span, kv_width), jnp.bfloat16),
        cost_estimate=pl.CostEstimate(
            flops=4 * rows * GROUP * span * HD * heads,
            transcendentals=rows * GROUP * span * heads,
            bytes_accessed=2 * (2 * rows * q_width + 2 * span * kv_width),
        ),
    )(queries, keys, grads, query_tags, key_tags)


def fused_attention(queries, keys, values, grads, query_tags, key_tags):
    rows, q_width = queries.shape
    span, kv_width = keys.shape
    heads = kv_width // HD
    q_spec, kv_spec, tag_specs = head_specs(rows, span)
    return pl.pallas_call(
        attention_kernel,
        grid=(heads,),
        in_specs=[q_spec, kv_spec, kv_spec, q_spec] + tag_specs,
        out_specs=[q_spec, q_spec, kv_spec],
        out_shape=[
            jax.ShapeDtypeStruct((rows, q_width), jnp.bfloat16),
            jax.ShapeDtypeStruct((rows, q_width), jnp.bfloat16),
            jax.ShapeDtypeStruct((span, kv_width), jnp.bfloat16),
        ],
        cost_estimate=pl.CostEstimate(
            flops=10 * rows * GROUP * span * HD * heads,
            transcendentals=rows * GROUP * span * heads,
            bytes_accessed=2 * (4 * rows * q_width + 3 * span * kv_width),
        ),
    )(queries, keys, values, grads, query_tags, key_tags)


def peer_gather_kernel(axis, n, x_ref, o_ref, send_sem, recv_sem, local_sem):
    me = lax.axis_index(axis)
    barrier = pltpu.get_barrier_semaphore()
    for k in range(1, n):
        pl.semaphore_signal(
            barrier, inc=1, device_id={axis: lax.rem(me + k, n)}, device_id_type=pl.DeviceIdType.MESH
        )
    pl.semaphore_wait(barrier, n - 1)
    local = pltpu.make_async_copy(x_ref, o_ref.at[me], local_sem)
    local.start()
    copies = []
    for k in range(1, n):
        copy = pltpu.make_async_remote_copy(
            src_ref=x_ref,
            dst_ref=o_ref.at[me],
            send_sem=send_sem.at[k],
            recv_sem=recv_sem.at[k],
            device_id={axis: lax.rem(me + k, n)},
            device_id_type=pl.DeviceIdType.MESH,
        )
        copy.start()
        copies.append(copy)
    for copy in copies:
        copy.wait()
    local.wait()


def peer_gather(x, axis, collective_id):
    n = lax.axis_size(axis)
    return pl.pallas_call(
        functools.partial(peer_gather_kernel, axis, n),
        out_shape=jax.ShapeDtypeStruct((n,) + x.shape, x.dtype),
        in_specs=[pl.BlockSpec(memory_space=pl.ANY)],
        out_specs=pl.BlockSpec(memory_space=pl.ANY),
        scratch_shapes=[
            pltpu.SemaphoreType.DMA((n,)),
            pltpu.SemaphoreType.DMA((n,)),
            pltpu.SemaphoreType.DMA,
        ],
        compiler_params=pltpu.CompilerParams(collective_id=collective_id, has_side_effects=True),
    )(x)


def peer_sum_kernel(axis, n, x_ref, o_ref, landed, send_sem, recv_sem, local_sem):
    me = lax.axis_index(axis)
    barrier = pltpu.get_barrier_semaphore()
    for k in range(1, n):
        pl.semaphore_signal(
            barrier, inc=1, device_id={axis: lax.rem(me + k, n)}, device_id_type=pl.DeviceIdType.MESH
        )
    pl.semaphore_wait(barrier, n - 1)
    local = pltpu.make_async_copy(x_ref.at[me], landed.at[0], local_sem)
    local.start()
    copies = []
    for k in range(1, n):
        peer = lax.rem(me + k, n)
        copy = pltpu.make_async_remote_copy(
            src_ref=x_ref.at[peer],
            dst_ref=landed.at[k],
            send_sem=send_sem.at[k],
            recv_sem=recv_sem.at[k],
            device_id={axis: peer},
            device_id_type=pl.DeviceIdType.MESH,
        )
        copy.start()
        copies.append(copy)
    local.wait()
    total = landed[0].astype(jnp.float32)
    for k in range(1, n):
        copies[k - 1].wait()
        total = total + landed[k].astype(jnp.float32)
    o_ref[...] = total


def peer_sum_scatter(x, axis, collective_id):
    n = lax.axis_size(axis)
    return pl.pallas_call(
        functools.partial(peer_sum_kernel, axis, n),
        out_shape=jax.ShapeDtypeStruct(x.shape[1:], jnp.float32),
        in_specs=[pl.BlockSpec(memory_space=pl.ANY)],
        out_specs=pl.BlockSpec(memory_space=pltpu.VMEM),
        scratch_shapes=[
            pltpu.VMEM(x.shape, x.dtype),
            pltpu.SemaphoreType.DMA((n,)),
            pltpu.SemaphoreType.DMA((n,)),
            pltpu.SemaphoreType.DMA,
        ],
        compiler_params=pltpu.CompilerParams(collective_id=collective_id, has_side_effects=True),
    )(x)


def shifted(x, axis, by):
    length = lax.axis_size(axis)
    pairs = [(i, i + by) for i in range(length) if 0 <= i + by < length]
    return lax.ppermute(x, axis, pairs)


def shards(hidden, queries, key_heads, w_value, d_out, segments):
    shard_rows = hidden.shape[1]
    kv_width = w_value.shape[1]
    n_hops = WINDOW // shard_rows
    span_rows = (n_hops + 1) * shard_rows
    tokens_in = hidden[0]
    own_keys = key_heads[0]
    own_segments = segments[0]
    n_fsdp = lax.axis_size("fsdp")
    n_ctx = lax.axis_size("ctx")
    model_width = tokens_in.shape[1]
    half_rows = w_value.shape[0] // 2
    core = lax.axis_index("ctx") % 2
    w_mine = lax.all_gather(
        lax.dynamic_slice_in_dim(w_value, core * half_rows, half_rows, 0), "fsdp", axis=0, tiled=False
    )
    partner = [(i, i ^ 1) for i in range(n_ctx)]
    token_halves = tokens_in.reshape(shard_rows, n_fsdp, 2, half_rows)
    tokens_mine = lax.dynamic_index_in_dim(token_halves, core, axis=2, keepdims=False)
    partner_tokens = lax.ppermute(
        lax.dynamic_index_in_dim(token_halves, 1 - core, axis=2, keepdims=False), "ctx", partner
    )
    out_rows = model_width // (n_ctx * n_fsdp)
    token_cols = (
        tokens_in.reshape(shard_rows, n_ctx, n_fsdp, out_rows).transpose(2, 0, 1, 3)
    )
    tag_columns = jnp.broadcast_to(own_segments.astype(jnp.bfloat16)[:, None], (shard_rows, HD))
    parcel = jnp.concatenate([own_keys, tag_columns], 1)
    arrived = [shifted(parcel, "ctx", hop) for hop in range(1, n_hops + 1)]
    window_parcel = jnp.concatenate(arrived[::-1] + [parcel], 0)
    window_parcel, partner_tokens, token_cols = lax.optimization_barrier(
        (window_parcel, partner_tokens, token_cols)
    )
    window_keys = window_parcel[:, :kv_width]
    window_tags = window_parcel[:, kv_width].astype(jnp.int32)
    first_query = lax.axis_index("ctx") * shard_rows
    key_pos = first_query - WINDOW + jnp.arange(span_rows, dtype=jnp.int32)
    key_tags = jnp.where(key_pos >= 0, window_tags, -1)
    query_tags = own_segments.astype(jnp.int32)[:, None]
    own_start = n_hops * shard_rows

    def returned_sum(terms):
        total = terms[own_start:].astype(jnp.float32)
        for hop in range(1, n_hops + 1):
            low_edge = (n_hops - hop) * shard_rows
            total = total + shifted(terms[low_edge : low_edge + shard_rows], "ctx", -hop).astype(jnp.float32)
        return total.astype(jnp.bfloat16)

    value_terms = value_grads(queries[0], window_keys, d_out[0], query_tags, key_tags[None, :])
    d_values_low = returned_sum(value_terms)
    w_mine, _ = lax.optimization_barrier((w_mine, d_values_low))
    grads_all = lax.all_gather(d_values_low, "fsdp", axis=0, tiled=False)

    partner_part = jnp.einsum("tfr,frn->tn", partner_tokens, w_mine, preferred_element_type=jnp.float32)
    values = (
        jnp.einsum("tfr,frn->tn", tokens_mine, w_mine, preferred_element_type=jnp.float32)
        + lax.ppermute(partner_part.astype(jnp.bfloat16), "ctx", partner).astype(jnp.float32)
    ).astype(jnp.bfloat16)
    arrived_values = [shifted(values, "ctx", hop) for hop in range(1, n_hops + 1)]
    token_cols, _ = lax.optimization_barrier((token_cols, values))
    token_cols = lax.all_to_all(token_cols, "fsdp", 0, 0, tiled=True)
    window_values = jnp.concatenate(arrived_values[::-1] + [values], 0)
    out_rows_attn, d_query_heads, key_terms = fused_attention(
        queries[0], window_keys, window_values, d_out[0], query_tags, key_tags[None, :]
    )
    d_key_rows = returned_sum(key_terms)
    d_mine = jnp.einsum("tn,frn->tfr", d_values_low, w_mine, preferred_element_type=jnp.float32).astype(jnp.bfloat16)
    partner_grads = lax.ppermute(d_values_low, "ctx", partner)
    d_other = lax.ppermute(
        jnp.einsum("tn,frn->tfr", partner_grads, w_mine, preferred_element_type=jnp.float32).astype(jnp.bfloat16),
        "ctx",
        partner,
    )
    d_tokens = jnp.where(
        core == 0, jnp.stack([d_mine, d_other], 2), jnp.stack([d_other, d_mine], 2)
    ).reshape(shard_rows, model_width)
    grads_all, _, d_tokens = lax.optimization_barrier((grads_all, key_terms, d_tokens))
    weight_part = jnp.einsum(
        "ftcr,ftn->crn", token_cols, grads_all, preferred_element_type=jnp.float32
    )
    d_weight = peer_sum_scatter(weight_part.astype(jnp.bfloat16), "ctx", 3)
    return (
        out_rows_attn[None],
        d_query_heads[None],
        d_key_rows[None],
        d_tokens[None],
        d_weight,
    )


def solution(mesh):
    in_specs = (
        P("fsdp", "ctx", None),
        P("fsdp", "ctx", None),
        P("fsdp", "ctx", None),
        P("fsdp", None),
        P("fsdp", "ctx", None),
        P("fsdp", "ctx"),
    )
    out_specs = (
        P("fsdp", "ctx", None),
        P("fsdp", "ctx", None),
        P("fsdp", "ctx", None),
        P("fsdp", "ctx", None),
        P(("ctx", "fsdp"), None),
    )
    return jax.shard_map(shards, mesh=mesh, in_specs=in_specs, out_specs=out_specs, check_vma=False)
```
